32 devices in a mesh: dp: 8 (over z, x), tensor: 4 (over y, core).
Axes of the slice: x: 2, y: 2, z: 4, core: 2. Of those that a mesh axis runs over, the one named last changes fastest.
Arguments:
- block_input: float32 [8192, 768], P(('dp', 'tensor')), may hold values from -40 to 40
- norm_gain: float32 [768], replicated, may hold values from 0.5 to 1.5
- zx_weight: bfloat16 [2, 768, 1536], P(None, 'dp', 'tensor'), may hold values from -0.21875 to 0.21875
- bc_weight: bfloat16 [768, 256], P('dp'), may hold values from -0.21875 to 0.21875
- dt_weight: bfloat16 [768, 24], P('dp', 'tensor'), may hold values from -0.21875 to 0.21875
- conv_x_weight: float32 [4, 1536], replicated, may hold values from -3 to 3
- conv_x_bias: float32 [1536], replicated, may hold values from -0.5 to 0.5
- conv_bc_weight: float32 [4, 256], replicated, may hold values from -3 to 3
- conv_bc_bias: float32 [256], replicated, may hold values from -0.5 to 0.5
- dt_bias: float32 [24], replicated, may hold values from -7 to -2
- decay_log: float32 [24], replicated, may hold values from 0 to 1.5
- skip_gain: float32 [24], replicated, may hold values from 0.2 to 1
- gate_gain: float32 [1536], replicated, may hold values from 0.5 to 1.5
- out_weight: bfloat16 [1536, 768], P('tensor', 'dp'), may hold values from -0.15625 to 0.15625
- segments: int32 [8192], P('dp'), may hold values from 0 to 3, never falling along the last dimension, each value on 1 to 4096 neighbouring positions
- cotangent: float32 [8192, 768], P(('dp', 'tensor')), may hold values from -6 to 6
Outputs:
- output: float32 [8192, 768], P(('dp', 'tensor'))
- grad_input: float32 [8192, 768], P(('dp', 'tensor'))
- grad_norm_gain: float32 [768], replicated
- grad_zx_weight: float32 [2, 768, 1536], P(None, 'dp', 'tensor')
- grad_bc_weight: float32 [768, 256], P('dp')
- grad_dt_weight: float32 [768, 24], P('dp', 'tensor')
- grad_conv_x_weight: float32 [4, 1536], replicated
- grad_conv_x_bias: float32 [1536], replicated
- grad_conv_bc_weight: float32 [4, 256], replicated
- grad_conv_bc_bias: float32 [256], replicated
- grad_dt_bias: float32 [24], replicated
- grad_decay_log: float32 [24], replicated
- grad_skip_gain: float32 [24], replicated
- grad_gate_gain: float32 [1536], replicated
- grad_out_weight: float32 [1536, 768], P('tensor', 'dp')
The draws below stay inside these ranges and needn't reach their ends.
Inputs may be any that keep to these rules, and one draw needn't show every extreme that they name: `segments`: segment numbers never fall along the tokens and every number from 0 up occurs; a number covers at most 4096 consecutive tokens, and one covers exactly that many.
All inputs are finite; a program needn't handle non-finite values.
Results may differ from the reference program's by a relative error of at most 0.012.
The reference program's roundings to bfloat16 on the way (of `normed`, `pre`, `activ`, `normed_out`, `cot_b`, `d_gate_in`, `d_pre` and `d_raw_b`) count: a program that leaves them out, or rounds other values in their place, can miss the bound.
Values may be sent and summed in bfloat16 or wider, within the bound.
A program may use at most 256 MiB of HBM per device.

```python
import math
import jax
import jax.numpy as jnp
import numpy as np
from jax import lax

D = 768
H = 24
P_SIZE = 64
N = 128
KCONV = 4
GROUP = 256
LENGTH = 4096
TOK_DEV = 1024
DI = 1536
TOKENS = 8192


def draw_block_input(key, part):
    key_base, key_rows, key_cols = jax.random.split(key, 3)
    base = jnp.clip(jax.random.normal(key_base, (TOKENS, D), jnp.float32), -4.0, 4.0)
    row_scale = jnp.exp(jax.random.uniform(key_rows, (TOKENS, 1), jnp.float32, -1.15, 1.15))
    col_scale = jnp.exp(jax.random.uniform(key_cols, (1, D), jnp.float32, -1.15, 1.15))
    return base * row_scale * col_scale


def block_levels(key, extent, cuts, smallest, high):
    def one(axis_at, shards_of):
        draws = jax.random.uniform(jax.random.fold_in(jax.random.fold_in(key, 6), axis_at), (shards_of,), jnp.float32, smallest / len(cuts), high / len(cuts))
        return jnp.repeat(jnp.exp(draws), extent[axis_at] // shards_of).reshape((-1,) + (1,) * (len(extent) - axis_at - 1))

    gain = one(*cuts[0])
    for cut in cuts[1:]:
        gain = gain * one(*cut)
    return gain


def profile(amount, total, reach, skew):
    weights = [(1 << 20) // math.isqrt(grade ** skew) + 1 for grade in range(2, amount + 1)]
    surplus, counts = total - reach - (amount - 1), [1] * (amount - 1)
    while surplus > 0:
        free = [i for i in range(amount - 1) if counts[i] < reach]
        pool, budget = sum([weights[i] for i in free]), surplus
        for i in free:
            more = min(reach - counts[i], max(1, budget * weights[i] // pool), surplus)
            counts[i] = counts[i] + more
            surplus = surplus - more
    return np.array([reach] + counts)


def ragged(rng, count, total, bound, skew):
    if count == 2:
        one = jax.random.randint(rng, (), max(1, total - bound), min(bound, total - 1) + 1)
        return jnp.stack([one, total - one])
    lengths = jnp.asarray(profile(count, total, bound, skew), jnp.int32)
    pairs = (count - 1) // 2
    source_of, taker = lengths[1:1 + 2 * pairs:2], lengths[2:2 + 2 * pairs:2]
    margin = jnp.minimum(source_of - 1, bound - taker)
    shifted = jax.random.randint(jax.random.fold_in(rng, 1), (pairs,), 0, 1 << 20) % (margin + 1)
    lengths = lengths.at[1:1 + 2 * pairs:2].set(source_of - shifted).at[2:2 + 2 * pairs:2].set(taker + shifted)
    return lengths[jax.random.permutation(jax.random.fold_in(rng, 2), count)]


def normal_values(stream_key, extent, deviation, reach, cuts=(), kind=jnp.bfloat16):
    drawn = deviation * jax.random.normal(stream_key, extent, jnp.float32)
    if cuts:
        drawn = drawn * block_levels(stream_key, extent, cuts, -0.22, 0.18)
    return jnp.clip(drawn, -reach, reach).astype(kind)


def setup_inputs(seed: int = 0) -> dict:
    key_list = jax.random.split(jax.random.key(seed), 17)
    return {
        "block_input": draw_block_input(jax.random.fold_in(key_list[16], 71), 0),
        "norm_gain": jnp.clip(1.0 + 0.1 * jax.random.normal(key_list[1], (D,), jnp.float32), 0.5, 1.5),
        "zx_weight": normal_values(key_list[2], (2, D, DI), D ** -0.5, 0.21875, ((1, 8), (2, 4))),
        "bc_weight": normal_values(key_list[3], (D, 2 * N), D ** -0.5, 0.21875, ((0, 8),)),
        "dt_weight": normal_values(key_list[4], (D, H), D ** -0.5, 0.21875, ((0, 8), (1, 4))),
        "conv_x_weight": normal_values(key_list[5], (KCONV, DI), KCONV ** -0.5, 3.0, (), jnp.float32),
        "conv_x_bias": jnp.clip(jax.random.uniform(key_list[6], (DI,), jnp.float32, -0.5, 0.5), -0.5, 0.5),
        "conv_bc_weight": normal_values(key_list[7], (KCONV, 2 * N), KCONV ** -0.5, 3.0, (), jnp.float32),
        "conv_bc_bias": jnp.clip(jax.random.uniform(key_list[8], (2 * N,), jnp.float32, -0.5, 0.5), -0.5, 0.5),
        "dt_bias": jnp.clip(jax.random.uniform(key_list[9], (H,), jnp.float32, -7.0, -2.0), -7.0, -2.0),
        "decay_log": jnp.clip(jax.random.uniform(key_list[10], (H,), jnp.float32, 0.0, 1.5), 0.0, 1.5),
        "skip_gain": jnp.clip(jax.random.uniform(key_list[11], (H,), jnp.float32, 0.2, 1.0), 0.2, 1.0),
        "gate_gain": jnp.clip(1.0 + 0.1 * jax.random.normal(key_list[12], (DI,), jnp.float32), 0.5, 1.5),
        "out_weight": normal_values(key_list[13], (DI, D), DI ** -0.5, 0.15625, ((0, 4), (1, 8))),
        "segments": jnp.searchsorted(jnp.cumsum(ragged(key_list[14], TOKENS // (2 * TOK_DEV), TOKENS, 4 * TOK_DEV, 1)), jnp.arange(TOKENS), side="right").astype(jnp.int32),
        "cotangent": normal_values(key_list[15], (TOKENS, D), 1.0, 6.0, ((0, 32),), jnp.float32),
    }


EPSILON = 1e-05
exact_prec = lax.Precision.HIGHEST

def dot_wide(left, right):
    return jnp.dot(left, right, preferred_element_type=jnp.float32)

def ssd_groups(inner_x, state_b, state_c, step_dt, decay_log, resets, start_state):
    tokens_here = inner_x.shape[0]
    blocks = tokens_here // GROUP

    def to_blocks(array):
        return array.reshape((blocks, GROUP) + array.shape[1:])
    rate = -jnp.exp(decay_log)
    index = jnp.arange(GROUP, dtype=jnp.int32)
    lower = index[:, None] >= index[None, :]

    def advance(state, pieces):
        block_x, block_b, block_c, block_dt, block_reset = pieces
        log_decay = block_dt * rate[None, :]
        cumul = jnp.cumsum(log_decay, axis=0)
        run_id = jnp.cumsum(block_reset)
        same_run = (run_id[:, None] == run_id[None, :]) & lower
        spread = cumul[:, None, :] - cumul[None, :, :]
        mask_three = same_run[:, :, None]
        decay = jnp.where(mask_three, jnp.exp(jnp.where(mask_three, spread, 0.0)), 0.0)
        scores = jnp.dot(block_c, block_b.T, precision=exact_prec)
        weighted_x = block_x * block_dt[:, :, None]
        mixing = decay * scores[:, :, None]
        within = jnp.einsum('tsh,shp->thp', mixing, weighted_x, precision=exact_prec)
        keep_first = (run_id == 0).astype(jnp.float32)
        inflow_w = jnp.exp(cumul) * keep_first[:, None]
        carried = jnp.einsum('tn,hpn->thp', block_c, state, precision=exact_prec) * inflow_w[:, :, None]
        tail_w = decay[GROUP - 1]
        new_state = state * inflow_w[GROUP - 1][:, None, None] + jnp.einsum('sh,shp,sn->hpn', tail_w, weighted_x, block_b, precision=exact_prec)
        return (new_state, within + carried)
    final, outputs = lax.scan(advance, start_state, (to_blocks(inner_x), to_blocks(state_b), to_blocks(state_c), to_blocks(step_dt), to_blocks(resets)))
    return (outputs.reshape(inner_x.shape), final)

def conv_apply(pre_ext, kernel, offsets, validity):
    length = validity.shape[0]
    total = jnp.broadcast_to(offsets[None, :], (length, offsets.shape[0]))
    for offset in range(kernel.shape[0]):
        total = total + kernel[offset][None, :] * pre_ext[offset:offset + length] * validity[:, offset:offset + 1]
    return jax.nn.silu(total)

def valid_and_resets(seg_ext, pos_ext, width_back):
    length = seg_ext.shape[0] - width_back
    own_seg = seg_ext[width_back:]
    own_pos = pos_ext[width_back:]
    columns = []
    for offset in range(width_back + 1):
        same = (seg_ext[offset:offset + length] == own_seg) & (pos_ext[offset:offset + length] // LENGTH == own_pos // LENGTH)
        columns.append(same.astype(jnp.float32))
    validity = jnp.stack(columns, axis=1)
    resets = ((seg_ext[width_back - 1:width_back - 1 + length] != own_seg) | (own_pos % LENGTH == 0)).astype(jnp.float32)
    return (validity, resets)

def reference(block_input, norm_gain, zx_weight, bc_weight, dt_weight, conv_x_weight, conv_x_bias, conv_bc_weight, conv_bc_bias, dt_bias, decay_log, skip_gain, gate_gain, out_weight, segments, cotangent):
    width_back = conv_x_weight.shape[0] - 1
    seq_count = TOKENS // LENGTH
    conv_weight = jnp.concatenate([conv_x_weight, conv_bc_weight], axis=1)
    conv_bias = jnp.concatenate([conv_x_bias, conv_bc_bias])
    pos_ext = jnp.arange(LENGTH + width_back, dtype=jnp.int32) - width_back
    zero_state = jnp.zeros((H, P_SIZE, N), jnp.float32)

    def one_sequence(totals, pieces):
        resid, seg, cot = pieces
        rstd = lax.rsqrt(lax.optimization_barrier(jnp.mean(resid * resid, axis=-1, keepdims=True)) + EPSILON)
        normed = (resid * rstd * norm_gain).astype(jnp.bfloat16)
        gate_in = dot_wide(normed, zx_weight[0])
        pre = jnp.concatenate([dot_wide(normed, zx_weight[1]), dot_wide(normed, bc_weight)], axis=1).astype(jnp.bfloat16)
        raw_dt = dot_wide(normed, dt_weight) + dt_bias
        step_dt = jax.nn.softplus(raw_dt)
        seg_ext = jnp.concatenate([jnp.full((width_back,), -1, jnp.int32), seg.astype(jnp.int32)])
        validity, resets = valid_and_resets(seg_ext, pos_ext, width_back)
        pre_ext = jnp.concatenate([jnp.zeros((width_back, pre.shape[1]), jnp.float32), pre.astype(jnp.float32)], axis=0)
        activ = conv_apply(pre_ext, conv_weight, conv_bias, validity).astype(jnp.bfloat16)
        inner_x = activ[:, :DI].astype(jnp.float32).reshape(LENGTH, H, P_SIZE)
        state_b = activ[:, DI:DI + N].astype(jnp.float32)
        state_c = activ[:, DI + N:].astype(jnp.float32)

        def mixer(arg_x, arg_b, arg_c, arg_dt, arg_log):
            return ssd_groups(arg_x, arg_b, arg_c, arg_dt, arg_log, resets, zero_state)[0]
        scan_y, mixer_back = jax.vjp(mixer, inner_x, state_b, state_c, step_dt, decay_log)
        mixed_three = scan_y + skip_gain[None, :, None] * inner_x
        mixed = mixed_three.reshape(LENGTH, DI)
        gate_act = jax.nn.silu(gate_in)
        gated = mixed * gate_act
        rstd_gate = lax.rsqrt(lax.optimization_barrier(jnp.mean(gated * gated, axis=-1, keepdims=True)) + EPSILON)
        normed_out = (gated * rstd_gate * gate_gain).astype(jnp.bfloat16)
        result = resid + dot_wide(normed_out, out_weight)
        cot_b = cot.astype(jnp.bfloat16)
        d_normed_out = dot_wide(cot_b, out_weight.T)
        g_out = dot_wide(normed_out.T, cot_b)
        g_gate = lax.optimization_barrier(jnp.sum(d_normed_out * gated * rstd_gate, axis=0))
        scaled = gate_gain * d_normed_out
        d_gated = rstd_gate * scaled - gated * rstd_gate ** 3 * lax.optimization_barrier(jnp.mean(scaled * gated, axis=-1, keepdims=True))
        sigm = jax.nn.sigmoid(gate_in)
        d_mixed = d_gated * gate_act
        d_gate_in = (d_gated * mixed * sigm * (1.0 + gate_in * (1.0 - sigm))).astype(jnp.bfloat16)
        d_mixed_three = d_mixed.reshape(LENGTH, H, P_SIZE)
        g_skip = lax.optimization_barrier(jnp.sum(d_mixed_three * inner_x, axis=(0, 2)))
        d_x, d_b, d_c, d_step, d_log = mixer_back(d_mixed_three)
        d_x = d_x + skip_gain[None, :, None] * d_mixed_three
        d_activ = jnp.concatenate([d_x.reshape(LENGTH, DI), d_b, d_c], axis=1)

        def conv_part(values, kernel, offsets):
            return conv_apply(values, kernel, offsets, validity)
        conv_out, conv_back = jax.vjp(conv_part, pre_ext, conv_weight, conv_bias)
        d_pre_ext, g_conv_w, g_conv_b = conv_back(d_activ)
        d_pre = d_pre_ext[width_back:].astype(jnp.bfloat16)
        d_raw = d_step * jax.nn.sigmoid(raw_dt)
        g_dt_bias = lax.optimization_barrier(jnp.sum(d_raw, axis=0))
        d_raw_b = d_raw.astype(jnp.bfloat16)
        d_normed = dot_wide(d_gate_in, zx_weight[0].T) + dot_wide(d_pre[:, :DI], zx_weight[1].T) + dot_wide(d_pre[:, DI:], bc_weight.T) + dot_wide(d_raw_b, dt_weight.T)
        g_zx = jnp.stack([dot_wide(normed.T, d_gate_in), dot_wide(normed.T, d_pre[:, :DI])])
        g_bc = dot_wide(normed.T, d_pre[:, DI:])
        g_dt = dot_wide(normed.T, d_raw_b)
        scaled_in = norm_gain * d_normed
        g_norm = lax.optimization_barrier(jnp.sum(d_normed * resid * rstd, axis=0))
        d_resid = cot + rstd * scaled_in - resid * rstd ** 3 * lax.optimization_barrier(jnp.mean(scaled_in * resid, axis=-1, keepdims=True))
        parts = (g_norm, g_zx, g_bc, g_dt, g_conv_w, g_conv_b, g_dt_bias, d_log, g_skip, g_gate, g_out)
        new_totals = tuple((before + extra for before, extra in zip(totals, parts)))
        return (new_totals, (result, d_resid))
    start_totals = (jnp.zeros((D,), jnp.float32), jnp.zeros((2, D, DI), jnp.float32), jnp.zeros((D, 2 * N), jnp.float32), jnp.zeros((D, H), jnp.float32), jnp.zeros((KCONV, DI + 2 * N), jnp.float32), jnp.zeros((DI + 2 * N,), jnp.float32), jnp.zeros((H,), jnp.float32), jnp.zeros((H,), jnp.float32), jnp.zeros((H,), jnp.float32), jnp.zeros((DI,), jnp.float32), jnp.zeros((DI, D), jnp.float32))
    totals, outputs = lax.scan(one_sequence, start_totals, (block_input.reshape(seq_count, LENGTH, D), segments.reshape(seq_count, LENGTH), cotangent.reshape(seq_count, LENGTH, D)))
    result = outputs[0].reshape(TOKENS, D)
    grad_input = outputs[1].reshape(TOKENS, D)
    g_norm, g_zx, g_bc, g_dt, g_conv_w, g_conv_b, g_dt_bias, g_log, g_skip, g_gate, g_out = totals
    return (result, grad_input, g_norm, g_zx, g_bc, g_dt, g_conv_w[:, :DI], g_conv_b[:DI], g_conv_w[:, DI:], g_conv_b[DI:], g_dt_bias, g_log, g_skip, g_gate, g_out)
```

```python
import functools
import jax
import jax.numpy as jnp
from jax import lax
from jax.experimental import pallas as pl
from jax.experimental.pallas import tpu as pltpu
from jax.sharding import PartitionSpec as P

GROUP = 256
LENGTH = 4096
EPSILON = 1e-05
exact_prec = lax.Precision.HIGHEST
PAD = 8
LANES = 128
MESH = pl.DeviceIdType.MESH
low = jnp.bfloat16


def dot_wide(left, right):
    return jnp.dot(left, right, preferred_element_type=jnp.float32)


def dot_exact(left, right):
    return jnp.dot(left, right, precision=exact_prec, preferred_element_type=jnp.float32)


def dot_nt(left, right):
    return lax.dot_general(left, right, (((1,), (1,)), ((), ())), preferred_element_type=jnp.float32)


def dot_tn(left, right):
    return lax.dot_general(left, right, (((0,), (0,)), ((), ())), preferred_element_type=jnp.float32)


def head_maps(inner, head_size):
    wide = (
        lax.broadcasted_iota(jnp.int32, (PAD, inner), 1) // head_size
        == lax.broadcasted_iota(jnp.int32, (PAD, inner), 0)
    ).astype(jnp.float32)
    tall = (
        lax.broadcasted_iota(jnp.int32, (inner, PAD), 0) // head_size
        == lax.broadcasted_iota(jnp.int32, (inner, PAD), 1)
    ).astype(jnp.float32)
    return wide, tall


def block_terms(rows, la_ref, lat_ref, key_ref, keyt_ref, before):
    size = rows.size
    row_i = lax.broadcasted_iota(jnp.int32, (size, size), 0)
    col_i = lax.broadcasted_iota(jnp.int32, (size, size), 1)
    lower = row_i >= col_i
    lower_f = lower.astype(jnp.float32)
    upper_f = (row_i <= col_i).astype(jnp.float32)
    la = la_ref[rows, :]
    cum = dot_exact(lower_f, la)
    cumt = dot_exact(lat_ref[:, rows], upper_f)
    key = key_ref[rows, :]
    keyt = keyt_ref[:, rows]
    same = lower & (key == keyt)
    last_key = key[size - 1 :, :]
    last = cum[size - 1 :, :]
    inflow = jnp.where(key == before, jnp.exp(cum), 0.0)
    tail = jnp.where(key == last_key, jnp.exp(last - cum), 0.0)
    passing = jnp.where(last_key == before, jnp.exp(last), 0.0)
    passing_t = jnp.where(last_key == before, jnp.exp(cumt[:, size - 1 :]), 0.0)
    return cum, cumt, same, inflow, tail, passing, passing_t, last_key


def head_decay(same, cum, cumt, head):
    spread = jnp.where(same, cum[:, head : head + 1] - cumt[head : head + 1, :], -1e30)
    return jnp.exp(spread)


def scan_forward_kernel(
    heads, head_size, size, x_ref, b_ref, c_ref, dt_ref, dtt_ref, la_ref, lat_ref, key_ref,
    keyt_ref, before_ref, y_ref, end_ref, inflow_ref,
):
    tokens, inner = x_ref.shape
    wide, tall = head_maps(inner, head_size)
    end_ref[...] = jnp.zeros_like(end_ref)
    first_before = before_ref[...]

    def step(index, carry):
        before, total = carry
        rows = pl.ds(pl.multiple_of(index * size, size), size)
        cum, cumt, same, inflow, tail, passing, passing_t, last_key = block_terms(
            rows, la_ref, lat_ref, key_ref, keyt_ref, before
        )
        x, b, c = x_ref[rows, :], b_ref[rows, :], c_ref[rows, :]
        scores = dot_nt(c, b)
        state = end_ref[...]
        carried = dot_nt(c, state.astype(jnp.bfloat16)) * dot_exact(inflow, wide)
        for head in range(heads):
            cols = slice(head * head_size, (head + 1) * head_size)
            mixing = (
                scores * head_decay(same, cum, cumt, head) * dtt_ref[head : head + 1, rows]
            ).astype(jnp.bfloat16)
            y_ref[rows, cols] = dot_wide(mixing, x[:, cols]) + carried[:, cols]
        pushed = (x.astype(jnp.float32) * dot_exact(tail * dt_ref[rows, :], wide)).astype(
            jnp.bfloat16
        )
        end_ref[...] = state * dot_exact(tall, passing_t) + dot_tn(pushed, b)
        reach = jnp.where(key_ref[rows, :] == first_before, jnp.exp(cum + total), 0.0)
        inflow_ref[rows, :] = dot_exact(reach, wide)
        return last_key, total + cum[size - 1 :, :]

    lax.fori_loop(0, tokens // size, step, (first_before, jnp.zeros((1, PAD), jnp.float32)))


def scan_backward_kernel(
    dp, tensor, heads, head_size, size, branch_ref, gb_ref, x_ref, b_ref, c_ref, dy_ref, dt_ref, dtt_ref, la_ref, lat_ref,
    key_ref, keyt_ref, before_ref, skip_ref, entry_ref, exit_ref,
    branch_own, gb_own, dx_ref, db_ref, dc_ref, dcum_ref, colt_ref, const_ref, sx_ref, states, cot,
    r1, r2, r3, rs, rr, g1, g2, g3, gs, gr,
):
    data, model = Grid2("dp", dp), Grid2("tensor", tensor)
    greet(("dp", dp), ("tensor", tensor))
    scatter_rows = Scatter(model, branch_ref, r1, r2, r3, branch_ref.shape[0] // tensor, rs, rr)
    scatter_g = Scatter(data, gb_ref, g1, g2, g3, gb_ref.shape[0] // dp, gs, gr)
    scatter_rows.start()
    scatter_g.start()
    tokens, inner = x_ref.shape
    blocks = tokens // size
    wide, tall = head_maps(inner, head_size)
    states[0] = entry_ref[...]
    first_before = before_ref[...]

    def block_before(index):
        if isinstance(index, int) and index == 0:
            return first_before
        return key_ref[pl.ds(index * size - 1, 1), :]

    def block_rows(index):
        return pl.ds(index * size, size)

    for index in range(blocks - 1):
        rows = block_rows(index)
        terms = block_terms(rows, la_ref, lat_ref, key_ref, keyt_ref, block_before(index))
        tail, passing_t = terms[4], terms[6]
        pushed = (
            x_ref[rows, :].astype(jnp.float32) * dot_exact(tail * dt_ref[rows, :], wide)
        ).astype(jnp.bfloat16)
        states[index + 1] = states[index] * dot_exact(tall, passing_t) + dot_tn(
            pushed, b_ref[rows, :]
        )
    cot[...] = exit_ref[...]

    def step(turn, carry):
        index = blocks - 1 - turn
        rows = pl.ds(pl.multiple_of(index * size, size), size)
        prior = key_ref[pl.ds(jnp.maximum(index * size - 1, 0), 1), :]
        before = jnp.where(index == 0, first_before, prior)
        cum, cumt, same, inflow, tail, passing, passing_t, last_key = block_terms(
            rows, la_ref, lat_ref, key_ref, keyt_ref, before
        )
        strict = lax.broadcasted_iota(jnp.int32, (size, size), 0) > lax.broadcasted_iota(
            jnp.int32, (size, size), 1
        )
        x, b, c = x_ref[rows, :], b_ref[rows, :], c_ref[rows, :]
        x_wide = x.astype(jnp.float32)
        dy = dy_ref[rows, :]
        dy_low = dy.astype(jnp.bfloat16)
        dt = dt_ref[rows, :]
        state, grad = states[index], cot[...]
        state_low, grad_low = state.astype(jnp.bfloat16), grad.astype(jnp.bfloat16)
        scores = dot_nt(c, b)
        from_state = dot_nt(c, state_low)
        from_grad = dot_nt(b, grad_low)
        tail_wide = dot_exact(tail, wide)
        dt_wide = dot_exact(dt, wide)
        d_in = (dy * dot_exact(inflow, wide)).astype(jnp.bfloat16)
        pushed = (x_wide * tail_wide * dt_wide).astype(jnp.bfloat16)
        d_scores = jnp.zeros((size, size), jnp.float32)
        dxd = []
        row_sums = []
        for head in range(heads):
            cols = slice(head * head_size, (head + 1) * head_size)
            decay = head_decay(same, cum, cumt, head)
            mixing = scores * decay
            both = dot_nt(dy_low[:, cols], x[:, cols]) * dtt_ref[head : head + 1, rows]
            d_scores = d_scores + both * decay
            joint = jnp.where(strict, both * mixing, 0.0)
            row_sums.append(jnp.sum(joint, axis=1, keepdims=True))
            colt_ref[head : head + 1, rows] = jnp.sum(joint, axis=0, keepdims=True)
            dxd.append(dot_tn(mixing.astype(jnp.bfloat16), dy_low[:, cols]))
        for head in range(heads, PAD):
            row_sums.append(jnp.zeros((size, 1), jnp.float32))
            colt_ref[head : head + 1, rows] = jnp.zeros((1, size), jnp.float32)
        dxd = jnp.concatenate(dxd, axis=1) + from_grad * tail_wide
        sx_ref[rows, :] = dot_exact(dxd * x_wide, tall)
        dx_ref[rows, :] = dxd * dt_wide + dy * skip_ref[...]
        d_low = d_scores.astype(jnp.bfloat16)
        dc_ref[rows, :] = dot_wide(d_low, b) + dot_wide(d_in, state_low)
        db_ref[rows, :] = dot_tn(d_low, c) + dot_wide(pushed, grad_low)
        through = dot_exact(dy * from_state, tall) * inflow
        kept = dot_exact(x_wide * from_grad, tall) * tail * dt
        dcum_ref[rows, :] = jnp.concatenate(row_sums, axis=1) + through - kept
        whole = dot_exact(jnp.sum(state * grad, axis=1, keepdims=True).T, tall)
        const_ref[rows, :] = jnp.broadcast_to(
            jnp.sum(kept, axis=0, keepdims=True) + passing * whole, (size, PAD)
        )
        cot[...] = grad * dot_exact(tall, passing_t) + dot_tn(d_in, c)
        return carry

    half = blocks // 2
    lax.fori_loop(0, half, step, 0)
    scatter_rows.middle()
    scatter_g.middle()
    lax.fori_loop(half, blocks, step, 0)
    branch_own[...] = scatter_rows.finish()
    gb_own[...] = scatter_g.finish()
    scatter_rows.drain()
    scatter_g.drain()


def vmem(count):
    return [pl.BlockSpec(memory_space=pltpu.VMEM)] * count


def scan_forward(x, b, c, dt, dtt, la, lat, key, keyt, before, heads):
    tokens, inner = x.shape
    size = min(GROUP, tokens)
    return pl.pallas_call(
        functools.partial(scan_forward_kernel, heads, inner // heads, size),
        out_shape=(
            jax.ShapeDtypeStruct((tokens, inner), jnp.float32),
            jax.ShapeDtypeStruct((inner, b.shape[1]), jnp.float32),
            jax.ShapeDtypeStruct((tokens, inner), jnp.float32),
        ),
        in_specs=vmem(10),
        out_specs=tuple(vmem(3)),
        compiler_params=pltpu.CompilerParams(vmem_limit_bytes=40 * 2**20),
        name="scan_forward",
    )(x, b, c, dt, dtt, la, lat, key, keyt, before)


def scan_backward(dp, tensor, heads, branch, gb, *arrays):
    x, b = arrays[:2]
    tokens, inner = x.shape
    size = min(GROUP, tokens)
    wide = b.shape[1]
    shape = jax.ShapeDtypeStruct
    f32 = jnp.float32
    return pl.pallas_call(
        functools.partial(scan_backward_kernel, dp, tensor, heads, inner // heads, size),
        out_shape=(
            shape((branch.shape[0] // tensor, branch.shape[1]), f32),
            shape((gb.shape[0] // dp, gb.shape[1]), f32),
            shape((tokens, inner), f32),
            shape((tokens, wide), f32),
            shape((tokens, wide), f32),
            shape((tokens, PAD), f32),
            shape((PAD, tokens), f32),
            shape((tokens, PAD), f32),
            shape((tokens, PAD), f32),
        ),
        in_specs=vmem(16),
        out_specs=tuple(vmem(9)),
        scratch_shapes=[
            pltpu.VMEM((tokens // size, inner, wide), f32),
            pltpu.VMEM((inner, wide), f32),
            *Scatter.scratch(tensor, branch.shape[0] // tensor, branch.shape[1]),
            *Scatter.scratch(dp, gb.shape[0] // dp, gb.shape[1]),
        ],
        compiler_params=pltpu.CompilerParams(
            collective_id=4, has_side_effects=True, vmem_limit_bytes=60 * 2**20
        ),
        name="scan_backward",
    )(branch, gb, *arrays)


def step_gradients(dcum, colt, const, sx, dt, la, rate):
    tokens = dcum.shape[0]
    size = min(GROUP, tokens)
    change = (dcum - colt.T).reshape(tokens // size, size, PAD)
    index = jnp.arange(size, dtype=jnp.int32)
    upper = (index[:, None] <= index[None, :]).astype(jnp.float32)
    d_la = jnp.einsum("ts,bsh->bth", upper, change, precision=exact_prec).reshape(tokens, PAD)
    d_la = d_la + const
    return d_la * rate + sx, jnp.sum(d_la * la, axis=0)


class Grid2:
    def __init__(self, axis, count):
        self.axis, self.count = axis, count
        self.inner = 2 if count % 2 == 0 else 1
        self.outer = count // self.inner
        self.me = lax.axis_index(axis)
        self.mi = lax.rem(self.me, self.inner)
        self.mo = self.me // self.inner

    def at(self, hop, inner):
        return lax.rem(self.mo + hop + self.outer, self.outer) * self.inner + inner

    @property
    def partner(self):
        return self.mo * self.inner + (self.inner - 1 - self.mi)


def remote(src, dst, send, recv, axis, index):
    return pltpu.make_async_remote_copy(
        src_ref=src, dst_ref=dst, send_sem=send, recv_sem=recv,
        device_id={axis: index}, device_id_type=MESH,
    )


def greet(*axes):
    barrier = pltpu.get_barrier_semaphore()
    total = 0
    for axis, count in axes:
        me = lax.axis_index(axis)
        for hop in range(1, count):
            pl.semaphore_signal(
                barrier, inc=1, device_id={axis: lax.rem(me + hop, count)}, device_id_type=MESH
            )
            total += 1
    if total:
        pl.semaphore_wait(barrier, total)


class Gather:
    def __init__(self, grid, ref, rows, send, recv):
        self.grid, self.ref, self.rows, self.send, self.recv = grid, ref, rows, send, recv

    @staticmethod
    def semaphores(count):
        return 2 * count

    def block(self, index):
        return self.ref.at[pl.ds(pl.multiple_of(index * self.rows, self.rows), self.rows), :]

    def copy(self, index, slot, target):
        piece = self.block(index)
        return remote(piece, piece, self.send.at[slot], self.recv.at[slot], self.grid.axis, target)

    def start(self):
        g = self.grid
        if g.inner > 1:
            self.copy(g.me, 0, g.partner).start()
        for hop in range(1, g.outer):
            self.copy(g.me, hop, g.at(hop, g.mi)).start()

    def forward(self):
        g = self.grid
        for hop in range(1, g.outer):
            source = g.at(-hop, g.mi)
            self.copy(source, hop, g.me).wait_recv()
            if g.inner > 1:
                self.copy(source, g.outer + hop, g.partner).start()

    def finish(self):
        g = self.grid
        if g.inner > 1:
            self.copy(g.partner, 0, g.partner).wait_recv()
            for hop in range(1, g.outer):
                source = g.at(-hop, g.inner - 1 - g.mi)
                self.copy(source, g.outer + hop, g.partner).wait_recv()

    def drain(self):
        g = self.grid
        if g.inner > 1:
            self.copy(g.me, 0, g.partner).wait_send()
            for hop in range(1, g.outer):
                self.copy(g.me, g.outer + hop, g.partner).wait_send()
        for hop in range(1, g.outer):
            self.copy(g.me, hop, g.partner).wait_send()


class Scatter:
    def __init__(self, grid, src, first, second, landed, rows, send, recv):
        self.grid, self.src, self.rows, self.send, self.recv = grid, src, rows, send, recv
        self.first, self.second, self.landed = first, second, landed

    @staticmethod
    def scratch(count, rows, width):
        outer = count // (2 if count % 2 == 0 else 1)
        return [
            pltpu.VMEM((outer, rows, width), low),
            pltpu.VMEM((outer, rows, width), low),
            pltpu.VMEM((outer, rows, width), low),
            pltpu.SemaphoreType.DMA((2 * outer,)),
            pltpu.SemaphoreType.DMA((2 * outer,)),
        ]

    def block(self, index):
        return self.src.at[pl.ds(pl.multiple_of(index * self.rows, self.rows), self.rows), :]

    def over(self, hop):
        g = self.grid
        return remote(
            self.block(g.at(hop, g.inner - 1 - g.mi)), self.first.at[hop],
            self.send.at[hop], self.recv.at[hop], g.axis, g.partner,
        )

    def along(self, hop):
        g = self.grid
        slot = g.outer + hop
        return remote(
            self.second.at[hop], self.landed.at[hop],
            self.send.at[slot], self.recv.at[slot], g.axis, g.at(hop, g.mi),
        )

    def start(self):
        if self.grid.inner > 1:
            for hop in list(range(1, self.grid.outer)) + [0]:
                self.over(hop).start()

    def pair(self, hop):
        g = self.grid
        total = self.block(g.at(hop, g.mi))[...].astype(jnp.float32)
        if g.inner > 1:
            self.over(hop).wait_recv()
            total = total + self.first[hop].astype(jnp.float32)
        return total

    def middle(self):
        for hop in range(1, self.grid.outer):
            self.second[hop] = self.pair(hop).astype(low)
            self.along(hop).start()

    def finish(self):
        g = self.grid
        total = self.pair(0)
        for hop in range(1, g.outer):
            self.along(hop).wait_recv()
            total = total + self.landed[hop].astype(jnp.float32)
        return total

    def drain(self):
        g = self.grid
        for hop in range(g.outer):
            if g.inner > 1:
                self.over(hop).wait_send()
            if hop:
                self.along(hop).wait_send()


def inproj_kernel(
    dp, tensor, mean_of, x_ref, gain_ref, cot_ref, zx_ref, bc_ref, dt_ref, out_ref, seg_ref,
    normed_ref, cotl_ref, wa_ref, wb_ref, pre_ref, raw_ref, gate_ref, dno_ref, halo_ref, segp_ref,
    tail, sa, ra, sb, rb, sn, rn, sc, rc, sh, rh,
):
    rows, width = x_ref.shape
    tokens = normed_ref.shape[0]
    part, inner = zx_ref.shape[1], zx_ref.shape[2]
    bc = bc_ref.shape[1]
    data, model = Grid2("dp", dp), Grid2("tensor", tensor)
    mine = pl.ds(pl.multiple_of(data.me * part, part), part)
    own = pl.ds(pl.multiple_of(model.me * rows, rows), rows)
    wa_ref[mine, :inner] = zx_ref[1]
    wa_ref[mine, inner : inner + bc] = bc_ref[...]
    wa_ref[mine, inner + bc :] = dt_ref[...]
    wb_ref[mine, :inner] = zx_ref[0]
    wb_ref[mine, inner:] = out_ref[...]
    x = x_ref[...]
    rstd = lax.rsqrt(jnp.sum(x * x, axis=-1, keepdims=True) / mean_of + EPSILON)
    normed_ref[own, :] = (x * rstd * gain_ref[...]).astype(low)
    cotl_ref[own, :] = cot_ref[...].astype(low)
    greet(("dp", dp), ("tensor", tensor))
    wa = Gather(data, wa_ref, part, sa, ra)
    wb = Gather(data, wb_ref, part, sb, rb)
    nm = Gather(model, normed_ref, rows, sn, rn)
    ct = Gather(model, cotl_ref, rows, sc, rc)
    following = lax.rem(data.me + 1, dp)
    seg_copy = remote(seg_ref, segp_ref, sh.at[0], rh.at[0], "dp", following)
    pre_copy = remote(tail, halo_ref, sh.at[1], rh.at[1], "dp", following)
    wa.start()
    nm.start()
    if dp > 1:
        seg_copy.start()
    wb.start()
    ct.start()
    nm.forward()
    wa.forward()
    nm.finish()
    wa.finish()
    block = min(GROUP, tokens)
    order = [tokens // block - 1] + list(range(tokens // block - 1))
    for index in order:
        at = pl.ds(index * block, block)
        first = dot_wide(normed_ref[at, :], wa_ref[...])
        pre_ref[at, :] = first[:, : inner + bc].astype(low)
        raw_ref[at, :] = first[:, inner + bc :]
        if index == tokens // block - 1:
            tail[...] = pre_ref[tokens - tail.shape[0] :, :]
            if dp > 1:
                pre_copy.start()
    ct.forward()
    wb.forward()
    ct.finish()
    wb.finish()
    for index in range(tokens // block):
        at = pl.ds(index * block, block)
        gate_ref[at, :] = dot_wide(normed_ref[at, :], wb_ref[:, :inner])
        dno_ref[at, :] = dot_wide(cotl_ref[at, :], wb_ref[:, inner:])
    if dp > 1:
        seg_copy.wait()
        pre_copy.wait()
    else:
        segp_ref[...] = seg_ref[...]
        halo_ref[...] = tail[...]
    for one in (wa, wb, nm, ct):
        one.drain()


def inproj(dp, tensor, mean_of, x, gain, cot, zx, bc, dt, out, seg):
    rows, width = x.shape
    tokens, part, inner = rows * tensor, zx.shape[1], zx.shape[2]
    wide = inner + bc.shape[1]
    shape = jax.ShapeDtypeStruct
    f32 = jnp.float32
    return pl.pallas_call(
        functools.partial(inproj_kernel, dp, tensor, mean_of),
        out_shape=(
            shape((tokens, width), low),
            shape((tokens, width), low),
            shape((dp * part, wide + dt.shape[1]), low),
            shape((dp * part, 2 * inner), low),
            shape((tokens, wide), low),
            shape((tokens, dt.shape[1]), f32),
            shape((tokens, inner), f32),
            shape((tokens, inner), f32),
            shape((16, wide), low),
            shape(seg.shape, jnp.int32),
        ),
        in_specs=vmem(8),
        out_specs=tuple(vmem(10)),
        scratch_shapes=[pltpu.VMEM((16, wide), low)]
        + [pltpu.SemaphoreType.DMA((2 * n,)) for n in (dp, dp, dp, dp, tensor, tensor, tensor, tensor)]
        + [pltpu.SemaphoreType.DMA((2,)), pltpu.SemaphoreType.DMA((2,))],
        compiler_params=pltpu.CompilerParams(
            collective_id=0, has_side_effects=True, vmem_limit_bytes=56 * 2**20
        ),
        name="inproj",
    )(x, gain, cot, zx, bc, dt, out, seg)


def line_kernel(group, array_ref, out_ref, send, recv):
    me = lax.axis_index("dp")
    start = (me // group) * group
    mine = lax.rem(me, group)

    def peer(hop):
        return start + lax.rem(mine + hop, group)

    barrier = pltpu.get_barrier_semaphore()
    for hop in range(1, group):
        pl.semaphore_signal(barrier, inc=1, device_id={"dp": peer(hop)}, device_id_type=MESH)
    pl.semaphore_wait(barrier, group - 1)

    def copy(hop):
        return remote(array_ref, out_ref.at[mine], send.at[hop], recv.at[hop], "dp", peer(hop))

    for hop in range(1, group):
        copy(hop).start()
    out_ref[mine] = array_ref[...]
    for hop in range(1, group):
        copy(hop).wait()


def gather_line(array, group, identity):
    if group == 1:
        return array[None]
    return pl.pallas_call(
        functools.partial(line_kernel, group),
        out_shape=jax.ShapeDtypeStruct((group,) + array.shape, array.dtype),
        in_specs=vmem(1),
        out_specs=vmem(1)[0],
        scratch_shapes=[pltpu.SemaphoreType.DMA((group,)), pltpu.SemaphoreType.DMA((group,))],
        compiler_params=pltpu.CompilerParams(
            collective_id=identity, has_side_effects=True, vmem_limit_bytes=32 * 2**20
        ),
        name=f"line{identity}",
    )(array)


def tail_kernel(
    dp, tensor, mean_of, kernel, dx_ref, dbc_ref, pre_ref, valid_ref, cw_ref, cb_ref, normed_ref,
    wa_ref, wb_ref, dgate_ref, draw_ref, side_ref, x_ref, gain_ref, cot_ref, extra_ref,
    gin_ref, ga_ref, gbc_ref, sums_ref,
    dz, dpre, dbc_all, rows_part, ga_part, halo_out, halo_in, halo_bc_out, halo_bc_in,
    small, small_all, sums_own, bc_own,
    b1, b2, b3, bs, br, r1, r2, r3, rs, rr, g1, g2, g3, gs, gr,
    as_, ar_, hs, hr, ss, sr, ts, tr, us, ur,
):
    tokens, inner = dx_ref.shape
    bc = dbc_ref.shape[1]
    wide = inner + bc
    rows, width = x_ref.shape
    part = wa_ref.shape[0] // dp
    data, model = Grid2("dp", dp), Grid2("tensor", tensor)
    block = min(GROUP, tokens)
    steps = tokens // block
    before = lax.rem(data.me + dp - 1, dp)
    f32 = jnp.float32
    greet(("dp", dp), ("tensor", tensor))
    scatter_bc = Scatter(model, dbc_ref, b1, b2, b3, rows, bs, br)
    scatter_rows = Scatter(model, rows_part, r1, r2, r3, rows, rs, rr)
    scatter_g = Scatter(data, ga_part, g1, g2, g3, part, gs, gr)
    scatter_bc.start()

    small[...] = extra_ref[...]

    def conv_back(cols, get):
        size = cols.stop - cols.start
        dz[0:8, cols] = jnp.zeros((8, size), f32)
        dz[8 + tokens :, cols] = jnp.zeros((8, size), f32)
        tap_sums = [jnp.zeros((1, size), f32) for _ in range(kernel + 1)]
        for index in range(steps):
            start = index * block
            total = jnp.broadcast_to(cb_ref[:, cols], (block, size))
            taps = []
            for offset in range(kernel):
                at = slice(8 - kernel + 1 + offset + start, 8 - kernel + 1 + offset + start + block)
                tap = pre_ref[at, cols] * valid_ref[8 + start : 8 + start + block, offset : offset + 1]
                taps.append(tap)
                total = total + cw_ref[offset : offset + 1, cols] * tap
            sigm = jax.nn.sigmoid(total)
            change = get(index) * (sigm * (1.0 + total * (1.0 - sigm)))
            dz[8 + start : 8 + start + block, cols] = change
            for offset in range(kernel):
                tap_sums[offset] += jnp.sum(taps[offset] * change, axis=0, keepdims=True)
            tap_sums[kernel] += jnp.sum(change, axis=0, keepdims=True)
        for offset in range(kernel + 1):
            small[offset : offset + 1, cols] = tap_sums[offset]

    def back_rows(start, size, cols):
        total = jnp.zeros((size, cols.stop - cols.start), f32)
        for offset in range(kernel):
            at = slice(start + kernel - 1 - offset, start + kernel - 1 - offset + size)
            total = total + cw_ref[offset : offset + 1, cols] * (
                dz[at, cols] * valid_ref[at, offset : offset + 1]
            )
        return total

    def halo(cols, out, arrived, slot):
        out[...] = back_rows(0, 8, cols)
        copy = remote(out, arrived, hs.at[slot], hr.at[slot], "dp", before)
        if dp > 1:
            copy.start()
        return copy

    def finish_pre(cols, copy, arrived):
        for index in range(steps):
            start = index * block
            value = back_rows(8 + start, block, cols)
            if index == steps - 1:
                edge = value[block - 8 :, :]
                if dp > 1:
                    copy.wait()
                    edge = edge + arrived[...]
                value = jnp.concatenate([value[: block - 8], edge], axis=0)
            dpre[start : start + block, cols] = value.astype(low)

    cols = slice(0, inner)
    conv_back(cols, lambda index: dx_ref[index * block : (index + 1) * block, :])
    copy = halo(cols, halo_out, halo_in, 0)
    scatter_bc.middle()
    finish_pre(cols, copy, halo_in)

    for index in range(steps):
        at = slice(index * block, (index + 1) * block)
        part_sum = dot_nt(dgate_ref[at, :], wb_ref[:, :inner])
        part_sum = part_sum + dot_nt(dpre[at, :inner], wa_ref[:, :inner])
        part_sum = part_sum + dot_nt(draw_ref[at, :], wa_ref[:, wide:])
        rows_part[at, :] = part_sum.astype(low)
    scatter_rows.start()
    own = pl.ds(pl.multiple_of(model.me * rows, rows), rows)
    dbc_all[own, :] = scatter_bc.finish().astype(low)
    gather_bc = Gather(model, dbc_all, rows, as_, ar_)
    gather_bc.start()
    g_mix = lax.dot_general(
        normed_ref[...], dpre[:, :inner], (((0,), (0,)), ((), ())), preferred_element_type=f32
    )
    ga_part[:, :inner] = g_mix.astype(low)
    scatter_rows.middle()
    gather_bc.forward()
    gather_bc.finish()
    cols = slice(inner, wide)
    conv_back(cols, lambda index: dbc_all[index * block : (index + 1) * block, :].astype(f32))
    copy = halo(cols, halo_bc_out, halo_bc_in, 1)
    finish_pre(cols, copy, halo_bc_in)
    quarter = bc // tensor
    pick = (
        lax.broadcasted_iota(jnp.int32, (bc, LANES), 0)
        == lax.broadcasted_iota(jnp.int32, (bc, LANES), 1) + model.me * quarter
    ) & (lax.broadcasted_iota(jnp.int32, (bc, LANES), 1) < quarter)
    pick = pick.astype(f32).astype(low)
    side = (dot_wide(dpre[:, inner:], pick) + side_ref[...].astype(f32)).astype(low)
    g_side = lax.dot_general(
        normed_ref[...], side, (((0,), (0,)), ((), ())), preferred_element_type=f32
    )
    ga_part[:, inner:] = g_side.astype(low)
    scatter_g.start()
    d_rows = scatter_rows.finish() + dot_nt(dpre[own, inner:], wa_ref[:, inner:wide])
    scatter_g.middle()
    x = x_ref[...]
    rstd = lax.rsqrt(jnp.sum(x * x, axis=-1, keepdims=True) / mean_of + EPSILON)
    scaled = gain_ref[...] * d_rows
    small[kernel + 1 : kernel + 2, :width] = jnp.sum(d_rows * x * rstd, axis=0, keepdims=True)
    hops = [hop for hop in range(1, dp)]

    def small_copy(hop):
        return remote(
            small, small_all.at[hop], ss.at[hop], sr.at[hop], "dp", lax.rem(data.me + hop, dp)
        )

    for hop in hops:
        small_copy(hop).start()
    gin_ref[...] = (
        cot_ref[...]
        + rstd * scaled
        - x * rstd**3 * (jnp.sum(scaled * x, axis=-1, keepdims=True) / mean_of)
    )
    total = small[...]
    for hop in hops:
        small_copy(hop).wait_recv()
        total = total + small_all[hop]
    sums_own[...] = total

    def sums_copy(hop):
        return remote(
            sums_own, sums_ref.at[model.me], ts.at[hop], tr.at[hop], "tensor",
            lax.rem(model.me + hop, tensor),
        )

    for hop in range(1, tensor):
        sums_copy(hop).start()
    sums_ref[model.me] = total
    ga = scatter_g.finish()
    ga_ref[...] = ga
    bc_own[...] = ga[:, inner:]

    def bc_copy(hop):
        return remote(
            bc_own, gbc_ref.at[model.me], us.at[hop], ur.at[hop], "tensor",
            lax.rem(model.me + hop, tensor),
        )

    for hop in range(1, tensor):
        bc_copy(hop).start()
    gbc_ref[model.me] = ga[:, inner:]
    for hop in range(1, tensor):
        sums_copy(hop).wait()
        bc_copy(hop).wait()
    for hop in hops:
        small_copy(hop).wait_send()
    for one in (scatter_bc, scatter_rows, scatter_g, gather_bc):
        one.drain()


def tail_call(dp, tensor, mean_of, kernel, *arrays):
    dx, dbc, pre, valid, cw, cb, normed, wa, wb, dgate, draw, side, x, gain, cot, extra = arrays
    tokens, inner = dx.shape
    bc = dbc.shape[1]
    wide = inner + bc
    rows, width = x.shape
    part = wa.shape[0] // dp
    shape = jax.ShapeDtypeStruct
    f32 = jnp.float32
    dma = pltpu.SemaphoreType.DMA
    return pl.pallas_call(
        functools.partial(tail_kernel, dp, tensor, mean_of, kernel),
        out_shape=(
            shape((rows, width), f32),
            shape((part, inner + LANES), f32),
            shape((tensor, part, LANES), f32),
            shape((tensor,) + extra.shape, f32),
        ),
        in_specs=vmem(16),
        out_specs=tuple(vmem(4)),
        scratch_shapes=[
            pltpu.VMEM((tokens + 16, wide), f32),
            pltpu.VMEM((tokens, wide), low),
            pltpu.VMEM((tokens, bc), low),
            pltpu.VMEM((tokens, width), low),
            pltpu.VMEM((dp * part, inner + LANES), low),
            pltpu.VMEM((8, inner), f32),
            pltpu.VMEM((8, inner), f32),
            pltpu.VMEM((8, bc), f32),
            pltpu.VMEM((8, bc), f32),
            pltpu.VMEM(extra.shape, f32),
            pltpu.VMEM((dp,) + extra.shape, f32),
            pltpu.VMEM(extra.shape, f32),
            pltpu.VMEM((part, LANES), f32),
            *Scatter.scratch(tensor, rows, bc),
            *Scatter.scratch(tensor, rows, width),
            *Scatter.scratch(dp, part, inner + LANES),
            dma((2 * tensor,)), dma((2 * tensor,)),
            dma((2,)), dma((2,)),
            dma((dp,)), dma((dp,)),
            dma((tensor,)), dma((tensor,)),
            dma((tensor,)), dma((tensor,)),
        ],
        compiler_params=pltpu.CompilerParams(
            collective_id=3, has_side_effects=True, vmem_limit_bytes=60 * 2**20
        ),
        name="tail",
    )(*arrays)


def conv_apply(pre_ext, kernel, offsets, validity):
    length = validity.shape[0]
    total = jnp.broadcast_to(offsets[None, :], (length, offsets.shape[0]))
    for offset in range(kernel.shape[0]):
        total = (
            total
            + kernel[offset][None, :]
            * pre_ext[offset : offset + length]
            * validity[:, offset : offset + 1]
        )
    return jax.nn.silu(total)


def pad_to(array, size, axis):
    widths = [(0, 0)] * array.ndim
    widths[axis] = (0, size - array.shape[axis])
    return jnp.pad(array, widths)


def chain(values, decays, mine, backward):
    count = values.shape[0]
    running = jnp.zeros(values.shape[1:], jnp.float32)
    order = range(count - 1, 0, -1) if backward else range(count - 1)
    for index in order:
        longer = running * decays[index] + values[index].astype(jnp.float32)
        reached = index > mine if backward else index < mine
        running = jnp.where(reached, longer, running)
    return running


def per_device(
    block_input,
    norm_gain,
    zx_weight,
    bc_weight,
    dt_weight,
    conv_x_weight,
    conv_x_bias,
    conv_bc_weight,
    conv_bc_bias,
    dt_bias,
    decay_log,
    skip_gain,
    gate_gain,
    out_weight,
    segments,
    cotangent,
):
    low = jnp.bfloat16
    tensor_count = lax.axis_size("tensor")
    tensor_index = lax.axis_index("tensor")
    data_count = lax.axis_size("dp")
    data_index = lax.axis_index("dp")
    token_count = segments.shape[0]
    row_count, width = block_input.shape
    part = zx_weight.shape[1]
    heads_here = dt_weight.shape[1]
    inner_here = out_weight.shape[0]
    head_size = inner_here // heads_here
    inner_total = inner_here * tensor_count
    heads_total = heads_here * tensor_count
    width_back = conv_x_weight.shape[0] - 1
    bc_size = bc_weight.shape[1]
    state_size = bc_size // 2
    head_start = tensor_index * heads_here
    inner_start = tensor_index * inner_here

    def own_heads(array):
        return pad_to(lax.dynamic_slice_in_dim(array, head_start, heads_here), PAD, 0)

    local_bias, local_log, local_skip = map(own_heads, (dt_bias, decay_log, skip_gain))
    local_gate_gain = lax.dynamic_slice_in_dim(gate_gain, inner_start, inner_here)
    skip_wide = jnp.repeat(local_skip[:heads_here], head_size)[None, :]
    conv_weight = jnp.concatenate(
        [lax.dynamic_slice_in_dim(conv_x_weight, inner_start, inner_here, 1), conv_bc_weight],
        axis=1,
    )
    conv_bias = jnp.concatenate(
        [lax.dynamic_slice_in_dim(conv_x_bias, inner_start, inner_here), conv_bc_bias]
    )
    padded = -(-part // 16) * 16
    columns = data_count * padded

    def widen(array):
        if padded == part:
            return array
        lead = array.shape[:-1]
        return pad_to(array.reshape(lead + (data_count, part)), padded, -1).reshape(lead + (columns,))

    def narrow(array):
        if padded == part:
            return array
        lead = array.shape[:-1]
        return array.reshape(lead + (data_count, padded))[..., :part].reshape(lead + (width,))

    x_rows, cot_rows = widen(block_input), widen(cotangent)
    norm_row = widen(norm_gain)[None, :]
    seg_tail = jnp.broadcast_to(segments[token_count - 8 :, None], (8, LANES))
    normed, cot_full, wa, wb, pre, raw, gate_in, d_normed_out, halo, seg_prev = inproj(
        data_count,
        tensor_count,
        width,
        x_rows,
        norm_row,
        cot_rows,
        pad_to(zx_weight, padded, 1),
        pad_to(bc_weight, padded, 0),
        pad_to(pad_to(dt_weight, padded, 0), LANES, 1),
        pad_to(out_weight.T, padded, 0),
        seg_tail,
    )
    w_out = wb[:, inner_here:]
    raw_dt = raw[:, :PAD] + local_bias
    step_dt = jax.nn.softplus(raw_dt)
    rate = -jnp.exp(local_log) * (jnp.arange(PAD) < heads_here)
    log_decay = step_dt * rate

    seg_ext = jnp.concatenate([seg_prev[8 - width_back :, 0], segments])
    pos_ext = (
        data_index * token_count
        - width_back
        + jnp.arange(token_count + width_back, dtype=jnp.int32)
    )
    sequences = data_count * token_count // LENGTH + 1
    key_ext = seg_ext * sequences + pos_ext // LENGTH
    key = key_ext[width_back:]
    before = key_ext[width_back - 1 : width_back].reshape(1, 1)
    validity = jnp.stack(
        [key_ext[k : k + token_count] == key for k in range(width_back + 1)], axis=1
    ).astype(jnp.float32)
    pre_pad = jnp.concatenate([halo[8:], pre], axis=0).astype(jnp.float32)
    pre_ext = pre_pad[8 - width_back :]
    activ = conv_apply(pre_ext, conv_weight, conv_bias, validity).astype(low)
    inner_x = activ[:, :inner_here]
    state_b = activ[:, inner_here : inner_here + state_size]
    state_c = activ[:, inner_here + state_size :]
    scan_args = (
        step_dt, step_dt.T, log_decay, log_decay.T, key[:, None], key[None, :], before,
    )
    local_y, local_end, inflow = scan_forward(
        inner_x, state_b, state_c, *scan_args, heads=heads_here
    )

    group = max(1, LENGTH // token_count)
    if data_count % group:
        group = data_count
    lines = [list(range(i, i + group)) for i in range(0, data_count, group)]
    mine = data_index % group

    device_decay = jnp.repeat(inflow[-1].reshape(heads_here, head_size)[:, :1], state_size, axis=1)
    sent = jnp.concatenate([local_end.astype(low), pad_to(device_decay, 16, 0).astype(low)])
    arrived = gather_line(sent, group, 1)
    decays = jnp.repeat(
        arrived[:, inner_here : inner_here + heads_here].astype(jnp.float32), head_size, axis=1
    )
    entry_state = chain(arrived[:, :inner_here], decays, mine, False)
    x_wide = inner_x.astype(jnp.float32)
    mixed = (
        local_y + dot_wide(state_c, entry_state.T.astype(low)) * inflow + skip_wide * x_wide
    )
    sigm = jax.nn.sigmoid(gate_in)
    gate_act = gate_in * sigm
    gated = mixed * gate_act
    scaled = local_gate_gain * d_normed_out
    sums = jnp.stack([jnp.sum(gated * gated, axis=1), jnp.sum(scaled * gated, axis=1)])
    sums = lax.psum(sums, "tensor") / inner_total
    rstd_gate = lax.rsqrt(sums[0] + EPSILON)[:, None]
    gate_dots = sums[1][:, None]
    gated_normed = gated * rstd_gate
    normed_out = (gated_normed * local_gate_gain).astype(low)
    d_gated = rstd_gate * scaled - gated * rstd_gate**3 * gate_dots
    d_mixed = d_gated * gate_act
    state_cot = dot_wide((d_mixed * inflow).T.astype(low), state_c)
    cots = gather_line(state_cot.astype(low), group, 2)
    leave_cot = chain(cots, decays, mine, True)
    branch_part = dot_nt(normed_out, w_out).astype(low)
    g_gate_local = jnp.sum(d_normed_out * gated_normed, axis=0)
    d_gate_in = (d_gated * mixed * sigm * (1.0 + gate_in * (1.0 - sigm))).astype(low)
    gb_part = jnp.concatenate(
        [dot_tn(normed, d_gate_in).astype(low), dot_tn(cot_full, normed_out).astype(low)], axis=1
    )
    g_skip_wide = jnp.sum(d_mixed * x_wide, axis=0)
    g_skip_local = jnp.sum(g_skip_wide.reshape(heads_here, head_size), axis=1)

    branch, gb, d_x, d_b, d_c, dcum, colt, const, sx = scan_backward(
        data_count, tensor_count, heads_here, branch_part, gb_part,
        inner_x, state_b, state_c, d_mixed, *scan_args, skip_wide, entry_state, leave_cot,
    )
    result = block_input + narrow(branch)
    d_step, d_log = step_gradients(dcum, colt, const, sx, step_dt, log_decay, rate)
    d_raw = d_step * jax.nn.sigmoid(raw_dt)
    d_raw_b = d_raw.astype(low)
    quarter = bc_size // tensor_count
    row_width = max(columns, inner_here + bc_size)
    line = jnp.concatenate(
        [g_gate_local, jnp.sum(d_raw, axis=0), d_log, pad_to(g_skip_local, PAD, 0)]
    )
    small_rows = width_back + 4
    extra = pad_to(pad_to(line, row_width, 0)[None, :], small_rows, 0)
    extra = pad_to(jnp.roll(extra, width_back + 3, axis=0), -(-small_rows // 8) * 8, 0)
    grad_rows, ga, gbc, sums = tail_call(
        data_count,
        tensor_count,
        width,
        width_back + 1,
        d_x,
        jnp.concatenate([d_b, d_c], axis=1).astype(low),
        pre_pad,
        jnp.pad(validity, ((8, 8), (0, 0))),
        conv_weight,
        conv_bias[None, :],
        normed,
        wa,
        wb,
        d_gate_in,
        pad_to(d_raw_b, LANES, 1),
        jnp.pad(d_raw_b, ((0, 0), (quarter, LANES - quarter - PAD))),
        x_rows,
        norm_row,
        cot_rows,
        extra,
    )
    grad_input = narrow(grad_rows)
    grad_zx = jnp.stack([gb[:part, :inner_here], ga[:part, :inner_here]])
    grad_out = gb[:part, inner_here:].T
    grad_dt = ga[:part, inner_here + quarter : inner_here + quarter + heads_here]
    grad_bc = jnp.concatenate([gbc[i, :part, :quarter] for i in range(tensor_count)], axis=1)
    grad_norm = narrow(jnp.sum(sums[:, width_back + 2, :columns], axis=0))

    def across(rows, start, size):
        return jnp.concatenate([sums[i, rows, start : start + size] for i in range(tensor_count)], axis=-1)

    taps, bias_at, line_at = slice(0, width_back + 1), width_back + 1, width_back + 3
    grad_cxw = across(taps, 0, inner_here)
    grad_cxb = across(bias_at, 0, inner_here)
    grad_cbw = sums[0, taps, inner_here : inner_here + bc_size]
    grad_cbb = sums[0, bias_at, inner_here : inner_here + bc_size]
    grad_gate = across(line_at, 0, inner_here)
    grad_dtb = across(line_at, inner_here, heads_here)
    grad_log = across(line_at, inner_here + PAD, heads_here)
    grad_skip = across(line_at, inner_here + 2 * PAD, heads_here)
    return (
        result,
        grad_input,
        grad_norm,
        grad_zx,
        grad_bc,
        grad_dt,
        grad_cxw,
        grad_cxb,
        grad_cbw,
        grad_cbb,
        grad_dtb,
        grad_log,
        grad_skip,
        grad_gate,
        grad_out,
    )


def solution(mesh):
    in_specs = (
        P(("dp", "tensor"), None),
        P(),
        P(None, "dp", "tensor"),
        P("dp", None),
        P("dp", "tensor"),
        P(),
        P(),
        P(),
        P(),
        P(),
        P(),
        P(),
        P(),
        P("tensor", "dp"),
        P("dp"),
        P(("dp", "tensor"), None),
    )
    out_specs = (
        P(("dp", "tensor"), None),
        P(("dp", "tensor"), None),
        P(),
        P(None, "dp", "tensor"),
        P("dp", None),
        P("dp", "tensor"),
        P(),
        P(),
        P(),
        P(),
        P(),
        P(),
        P(),
        P(),
        P("tensor", "dp"),
    )
    return jax.shard_map(
        per_device, mesh=mesh, in_specs=in_specs, out_specs=out_specs, check_vma=False
    )
```

```python
import functools
import jax
import jax.numpy as jnp
from jax import lax
from jax.experimental import pallas as pl
from jax.experimental.pallas import tpu as pltpu
from jax.sharding import PartitionSpec as P

GROUP = 256
LENGTH = 4096
EPSILON = 1e-05
PAD = 8
LANES = 128
MESH = pl.DeviceIdType.MESH
low = jnp.bfloat16


def dot_wide(left, right):
    return jnp.dot(left, right, preferred_element_type=jnp.float32)


def dot_nt(left, right):
    return lax.dot_general(left, right, (((1,), (1,)), ((), ())), preferred_element_type=jnp.float32)


def dot_tn(left, right):
    return lax.dot_general(left, right, (((0,), (0,)), ((), ())), preferred_element_type=jnp.float32)


def head_decay(same, cum, cumt, head):
    spread = jnp.where(same, cum[:, head : head + 1] - cumt[head : head + 1, :], -1e30)
    return jnp.exp(spread)


def vmem(count):
    return [pl.BlockSpec(memory_space=pltpu.VMEM)] * count


class Grid2:
    def __init__(self, axis, count):
        self.axis, self.count = axis, count
        self.inner = 2 if count % 2 == 0 else 1
        self.outer = count // self.inner
        self.me = lax.axis_index(axis)
        self.mi = lax.rem(self.me, self.inner)
        self.mo = self.me // self.inner

    def at(self, hop, inner):
        return lax.rem(self.mo + hop + self.outer, self.outer) * self.inner + inner

    @property
    def partner(self):
        return self.mo * self.inner + (self.inner - 1 - self.mi)


def remote(src, dst, send, recv, axis, index):
    return pltpu.make_async_remote_copy(
        src_ref=src, dst_ref=dst, send_sem=send, recv_sem=recv,
        device_id={axis: index}, device_id_type=MESH,
    )


def greet(*axes):
    barrier = pltpu.get_barrier_semaphore()
    total = 0
    for axis, count in axes:
        me = lax.axis_index(axis)
        for hop in range(1, count):
            pl.semaphore_signal(
                barrier, inc=1, device_id={axis: lax.rem(me + hop, count)}, device_id_type=MESH
            )
            total += 1
    if total:
        pl.semaphore_wait(barrier, total)


class Gather:
    def __init__(self, grid, ref, rows, send, recv):
        self.grid, self.ref, self.rows, self.send, self.recv = grid, ref, rows, send, recv

    @staticmethod
    def semaphores(count):
        return 2 * count

    def block(self, index):
        return self.ref.at[pl.ds(pl.multiple_of(index * self.rows, self.rows), self.rows), :]

    def copy(self, index, slot, target):
        piece = self.block(index)
        return remote(piece, piece, self.send.at[slot], self.recv.at[slot], self.grid.axis, target)

    def start(self):
        g = self.grid
        if g.inner > 1:
            self.copy(g.me, 0, g.partner).start()
        for hop in range(1, g.outer):
            self.copy(g.me, hop, g.at(hop, g.mi)).start()

    def forward(self):
        g = self.grid
        for hop in range(1, g.outer):
            source = g.at(-hop, g.mi)
            self.copy(source, hop, g.me).wait_recv()
            if g.inner > 1:
                self.copy(source, g.outer + hop, g.partner).start()

    def finish(self):
        g = self.grid
        if g.inner > 1:
            self.copy(g.partner, 0, g.partner).wait_recv()
            for hop in range(1, g.outer):
                source = g.at(-hop, g.inner - 1 - g.mi)
                self.copy(source, g.outer + hop, g.partner).wait_recv()

    def drain(self):
        g = self.grid
        if g.inner > 1:
            self.copy(g.me, 0, g.partner).wait_send()
            for hop in range(1, g.outer):
                self.copy(g.me, g.outer + hop, g.partner).wait_send()
        for hop in range(1, g.outer):
            self.copy(g.me, hop, g.partner).wait_send()


class Scatter:
    def __init__(self, grid, src, first, second, landed, rows, send, recv):
        self.grid, self.src, self.rows, self.send, self.recv = grid, src, rows, send, recv
        self.first, self.second, self.landed = first, second, landed

    @staticmethod
    def scratch(count, rows, width):
        outer = count // (2 if count % 2 == 0 else 1)
        return [
            pltpu.VMEM((outer, rows, width), low),
            pltpu.VMEM((outer, rows, width), low),
            pltpu.VMEM((outer, rows, width), low),
            pltpu.SemaphoreType.DMA((2 * outer,)),
            pltpu.SemaphoreType.DMA((2 * outer,)),
        ]

    def block(self, index):
        return self.src.at[pl.ds(pl.multiple_of(index * self.rows, self.rows), self.rows), :]

    def over(self, hop):
        g = self.grid
        return remote(
            self.block(g.at(hop, g.inner - 1 - g.mi)), self.first.at[hop],
            self.send.at[hop], self.recv.at[hop], g.axis, g.partner,
        )

    def along(self, hop):
        g = self.grid
        slot = g.outer + hop
        return remote(
            self.second.at[hop], self.landed.at[hop],
            self.send.at[slot], self.recv.at[slot], g.axis, g.at(hop, g.mi),
        )

    def start(self):
        if self.grid.inner > 1:
            for hop in list(range(1, self.grid.outer)) + [0]:
                self.over(hop).start()

    def pair(self, hop):
        g = self.grid
        total = self.block(g.at(hop, g.mi))[...].astype(jnp.float32)
        if g.inner > 1:
            self.over(hop).wait_recv()
            total = total + self.first[hop].astype(jnp.float32)
        return total

    def middle(self):
        for hop in range(1, self.grid.outer):
            self.second[hop] = self.pair(hop).astype(low)
            self.along(hop).start()

    def finish(self):
        g = self.grid
        total = self.pair(0)
        for hop in range(1, g.outer):
            self.along(hop).wait_recv()
            total = total + self.landed[hop].astype(jnp.float32)
        return total

    def drain(self):
        g = self.grid
        for hop in range(g.outer):
            if g.inner > 1:
                self.over(hop).wait_send()
            if hop:
                self.along(hop).wait_send()


def split(value, pieces):
    out = []
    for _ in range(pieces):
        piece = value.astype(low)
        out.append(piece)
        value = value - piece.astype(jnp.float32)
    return out


def spread_heads(value, head_size, inner, pieces=2):
    one = (
        lax.broadcasted_iota(jnp.int32, (LANES, inner), 1) // head_size
        == lax.broadcasted_iota(jnp.int32, (LANES, inner), 0)
    ).astype(jnp.float32).astype(low)
    return dot_wide(
        jnp.concatenate(split(value, pieces), axis=1), jnp.concatenate([one] * pieces, axis=0)
    )


def sum_heads(value, head_size, pieces=2):
    inner = value.shape[1]
    one = (
        lax.broadcasted_iota(jnp.int32, (inner, LANES), 0) // head_size
        == lax.broadcasted_iota(jnp.int32, (inner, LANES), 1)
    ).astype(jnp.float32).astype(low)
    return dot_wide(
        jnp.concatenate(split(value, pieces), axis=1), jnp.concatenate([one] * pieces, axis=0)
    )


def running_sum(value, reverse=False):
    size = value.shape[0]
    row = lax.broadcasted_iota(jnp.int32, (size, size), 0)
    col = lax.broadcasted_iota(jnp.int32, (size, size), 1)
    keep = (row <= col) if reverse else (row >= col)
    keep = keep.astype(jnp.float32).astype(low)
    pieces = split(value, 3)
    total = dot_wide(keep, jnp.concatenate(pieces, axis=1))
    width = value.shape[1]
    return total[:, :width] + total[:, width : 2 * width] + total[:, 2 * width :]


def rows_of_heads(row, heads, head_size):
    turned = jnp.broadcast_to(row, (LANES, LANES)).T
    return jnp.concatenate(
        [jnp.broadcast_to(turned[h : h + 1, :], (head_size, LANES)) for h in range(heads)], axis=0
    )


def softplus(value):
    return jnp.maximum(value, 0.0) + jnp.log1p(jnp.exp(-jnp.abs(value)))


def block_parts(cum, key, before):
    size = cum.shape[0]
    last_key, last = key[size - 1 :, :], cum[size - 1 :, :]
    inflow = jnp.where(key == before, jnp.exp(cum), 0.0)
    tail = jnp.where(key == last_key, jnp.exp(last - cum), 0.0)
    passing = jnp.where(last_key == before, jnp.exp(last), 0.0)
    return inflow, tail, passing


def forward_kernel(
    dp, tensor, group, heads, mean_of, sequences,
    x_ref, gain_ref, cot_ref, zx_ref, bcw_ref, dtt_ref, out_ref, seg_ref, cxw_ref, cxb_ref, cbw_ref,
    cbb_ref, head_ref, ggain_ref,
    normed_ref, cotl_ref, wa_ref, wb_ref, wdt_ref, pre_ref, key_ref, act_ref, raw_ref, cum_ref,
    states_ref, dmix_ref, dgate_ref, nout_ref, scot_ref, gsum_ref,
    tail, dtall, cw, y, gate, dno, sent, got, ends, decays, sums, sums_all,
    sa, ra, sb, rb, sd, rd, sn, rn, sc, rc, sh, rh, sl, rl, ss, rs,
):
    rows, width = x_ref.shape
    tokens = normed_ref.shape[0]
    part, inner = zx_ref.shape[1], zx_ref.shape[2]
    bc = bcw_ref.shape[1]
    wide, state = inner + bc, bc // 2
    head_size = inner // heads
    kernel = cxw_ref.shape[0]
    block = min(GROUP, tokens)
    steps = tokens // block
    f32 = jnp.float32
    data, model = Grid2("dp", dp), Grid2("tensor", tensor)
    mine = pl.ds(pl.multiple_of(data.me * part, part), part)
    own = pl.ds(pl.multiple_of(model.me * rows, rows), rows)
    units = pl.ds(pl.multiple_of(model.me * inner, LANES), inner)

    wa_ref[mine, :inner] = zx_ref[1]
    wa_ref[mine, inner:] = bcw_ref[...]
    wb_ref[mine, :inner] = zx_ref[0]
    eye = (
        lax.broadcasted_iota(jnp.int32, (part, out_ref.shape[1]), 0)
        == lax.broadcasted_iota(jnp.int32, (part, out_ref.shape[1]), 1)
    ).astype(f32).astype(low)
    wb_ref[mine, inner:] = dot_nt(eye, out_ref[...]).astype(low)
    dtall[pl.ds(pl.multiple_of(data.me * 16, 16), 16), :] = dtt_ref[...]
    x = x_ref[...]
    rstd = lax.rsqrt(jnp.sum(x * x, axis=-1, keepdims=True) / mean_of + EPSILON)
    normed_ref[own, :] = (x * rstd * gain_ref[...]).astype(low)
    cotl_ref[own, :] = cot_ref[...].astype(low)
    for index in range(steps):
        at = slice(index * block, (index + 1) * block)
        line = seg_ref[:, at].astype(f32)
        key_ref[8 + index * block : 8 + (index + 1) * block, :] = jnp.broadcast_to(
            line, (LANES, block)
        ).T
    key_ref[8 + tokens :, :] = jnp.zeros((8, LANES), f32)
    greet(("dp", dp), ("tensor", tensor))
    wa = Gather(data, wa_ref, part, sa, ra)
    wb = Gather(data, wb_ref, part, sb, rb)
    wd = Gather(data, dtall, 16, sd, rd)
    nm = Gather(model, normed_ref, rows, sn, rn)
    ct = Gather(model, cotl_ref, rows, sc, rc)
    following = lax.rem(data.me + 1, dp)
    seg_copy = remote(
        key_ref.at[pl.ds(tokens, 8), :], key_ref.at[pl.ds(0, 8), :], sh.at[0], rh.at[0], "dp",
        following,
    )
    pre_copy = remote(
        tail, pre_ref.at[pl.ds(0, 8), :], sh.at[1], rh.at[1], "dp", following
    )
    wd.start()
    wa.start()
    nm.start()
    seg_copy.start()
    nm.forward()
    ct.start()
    wd.forward()
    wa.forward()
    wb.start()
    cw[0:kernel, :inner] = cxw_ref[:, units]
    cw[0:kernel, inner:] = cbw_ref[...]
    cw[kernel : kernel + 1, :inner] = cxb_ref[:, units]
    cw[kernel : kernel + 1, inner:] = cbb_ref[...]
    wd.finish()
    turn = (
        lax.broadcasted_iota(jnp.int32, (part, LANES), 0)
        == lax.broadcasted_iota(jnp.int32, (part, LANES), 1)
    ).astype(f32).astype(low)
    for index in range(dp):
        shard = jnp.concatenate(
            [dtall[index * 16 : (index + 1) * 16, :], jnp.zeros((LANES - 16, LANES), low)], axis=0
        )
        wdt_ref[index * part : (index + 1) * part, :] = dot_nt(turn, shard).astype(low)
    nm.finish()
    wa.finish()
    last = steps - 1
    bias, rate = head_ref[0:1, :], head_ref[1:2, :]
    for index in [last] + list(range(last)):
        at = slice(index * block, (index + 1) * block)
        first = dot_wide(normed_ref[at, :], wa_ref[...])
        pre_ref[8 + index * block : 8 + (index + 1) * block, :] = first.astype(low).astype(f32)
        if index == last:
            tail[...] = pre_ref[tokens : tokens + 8, :]
            pre_copy.start()
        raw_ref[at, :] = dot_wide(normed_ref[at, :], wdt_ref[...]) + bias
    seg_copy.wait()
    pos = lax.broadcasted_iota(jnp.int32, (tokens + 16, LANES), 0) + (data.me * tokens - 8 + LENGTH)
    key_ref[...] = key_ref[...] * sequences + (pos // LENGTH).astype(f32)
    ends[...] = jnp.zeros_like(ends)
    total_cum = jnp.zeros((1, LANES), f32)
    first_before = key_ref[7:8, :]
    before = first_before
    pre_copy.wait()
    for index in range(steps):
        start = index * block
        at = slice(start, start + block)
        key = key_ref[8 + start : 8 + start + block, :]
        total = jnp.broadcast_to(cw[kernel : kernel + 1, :], (block, wide))
        for offset in range(kernel):
            shift = slice(8 - kernel + 1 + offset + start, 8 - kernel + 1 + offset + start + block)
            tap = cw[offset : offset + 1, :] * pre_ref[shift, :]
            if offset < kernel - 1:
                same = jnp.where(key_ref[shift, :] == key, 1.0, 0.0)
                tap = tap * jnp.concatenate([same] * (wide // LANES), axis=1)
            total = total + tap
        act_ref[at, :] = (total * jax.nn.sigmoid(total)).astype(low)
        dt = softplus(raw_ref[at, :])
        cum = running_sum(dt * rate)
        cum_ref[at, :] = cum
        inflow, tail_w, passing = block_parts(cum, key, before)
        pushed = (
            act_ref[at, :inner].astype(f32) * spread_heads(tail_w * dt, head_size, inner)
        ).astype(low)
        states_ref[index] = ends[...]
        reach = jnp.where(before == first_before, jnp.exp(total_cum), 0.0)
        decays[index * 8 : index * 8 + 1, :] = reach
        ends[...] = ends[...] * rows_of_heads(passing, heads, head_size) + dot_tn(
            pushed, act_ref[at, inner : inner + state]
        )
        total_cum = total_cum + cum[block - 1 :, :]
        before = key[block - 1 :, :]
        if index == 0:
            ct.forward()
    reach = jnp.where(before == first_before, jnp.exp(total_cum), 0.0)
    turned = jnp.broadcast_to(reach, (LANES, LANES)).T[:8, :]
    hi, lo = split(turned, 2)
    sent[0:inner, :] = ends[...].astype(low)
    sent[inner : inner + 16, :] = jnp.concatenate([hi, lo], axis=0)
    line_start = (data.me // group) * group
    place = lax.rem(data.me, group)

    def line_copy(hop):
        return remote(
            sent, got.at[place], sl.at[hop], rl.at[hop], "dp",
            line_start + lax.rem(place + hop, group),
        )

    for hop in range(1, group):
        line_copy(hop).start()
    got[place] = sent[...]
    row_i = lax.broadcasted_iota(jnp.int32, (block, block), 0)
    col_i = lax.broadcasted_iota(jnp.int32, (block, block), 1)
    for index in range(steps):
        start = index * block
        at = slice(start, start + block)
        key = key_ref[8 + start : 8 + start + block, :]
        keyt = key.T
        same = (row_i >= col_i) & (
            jnp.concatenate([key] * (block // LANES), axis=1) == keyt[0:1, :]
        )
        cum = cum_ref[at, :]
        cumt = cum.T
        dtt = softplus(raw_ref[at, :]).T
        x = act_ref[at, :inner]
        scores = dot_nt(act_ref[at, inner + state :], act_ref[at, inner : inner + state])
        for head in range(heads):
            cols = slice(head * head_size, (head + 1) * head_size)
            mixing = (
                scores * head_decay(same, cum, cumt, head) * dtt[head : head + 1, :]
            ).astype(low)
            y[at, cols] = dot_wide(mixing, x[:, cols])
        if index == 0:
            wb.forward()
    ct.finish()
    wb.finish()
    for index in range(steps):
        at = slice(index * block, (index + 1) * block)
        gate[at, :] = dot_wide(normed_ref[at, :], wb_ref[:, :inner])
        dno[at, :] = dot_wide(cotl_ref[at, :], wb_ref[:, inner:])
    for hop in range(1, group):
        line_copy(hop).wait()
    entry = jnp.zeros((inner, state), f32)
    for index in range(group - 1):
        factor = got[index, inner : inner + 8, :].astype(f32) + got[index, inner + 8 :, :].astype(f32)
        factor = jnp.concatenate(
            [jnp.broadcast_to(factor[h : h + 1, :], (head_size, LANES)) for h in range(heads)], axis=0
        )
        longer = entry * factor + got[index, :inner, :].astype(f32)
        entry = jnp.where(index < place, longer, entry)
    skip = spread_heads(head_ref[0:8, :], head_size, inner, 3)[2:3, :]
    ggain = ggain_ref[:, units]
    before = first_before
    for index in range(steps):
        start = index * block
        at = slice(start, start + block)
        full = states_ref[index] + entry * rows_of_heads(
            decays[index * 8 : index * 8 + 1, :], heads, head_size
        )
        states_ref[index] = full
        key = key_ref[8 + start : 8 + start + block, :]
        inflow = jnp.where(key == before, jnp.exp(cum_ref[at, :]), 0.0)
        before = key[block - 1 :, :]
        mixed = (
            y[at, :]
            + dot_nt(act_ref[at, inner + state :], full.astype(low))
            * spread_heads(inflow, head_size, inner)
            + skip * act_ref[at, :inner].astype(f32)
        )
        y[at, :] = mixed
        gate_in = gate[at, :]
        gated = mixed * (gate_in * jax.nn.sigmoid(gate_in))
        squares = jnp.sum(gated * gated, axis=1, keepdims=True)
        dots = jnp.sum(gated * (ggain * dno[at, :]), axis=1, keepdims=True)
        lane = lax.broadcasted_iota(jnp.int32, (block, LANES), 1)
        both = jnp.where(lane == 0, squares, jnp.where(lane == 1, dots, 0.0))
        sums[:, at] = both.T[:8, :]

    def sums_copy(hop):
        return remote(
            sums, sums_all.at[hop], ss.at[hop], rs.at[hop], "tensor",
            lax.rem(model.me + hop, tensor),
        )

    for hop in range(1, tensor):
        sums_copy(hop).start()
    for hop in range(1, tensor):
        sums_copy(hop).wait_recv()
    before = first_before
    to_exit = jnp.zeros((1, LANES), f32)
    scot = jnp.zeros((inner, state), f32)
    g_gate = jnp.zeros((1, inner), f32)
    g_skip = jnp.zeros((1, inner), f32)
    total_cum = jnp.zeros((1, LANES), f32)
    for index in range(steps):
        start = index * block
        at = slice(start, start + block)
        total = sums[:, at]
        for hop in range(1, tensor):
            total = total + sums_all[hop, :, at]
        total = total / (inner * tensor)
        turned = jnp.concatenate([total, jnp.zeros((LANES - 8, block), f32)], axis=0).T
        rstd_gate = lax.rsqrt(turned[:, 0:1] + EPSILON)
        gate_dots = turned[:, 1:2]
        gate_in, mixed, d_out = gate[at, :], y[at, :], dno[at, :]
        sigm = jax.nn.sigmoid(gate_in)
        gate_act = gate_in * sigm
        gated = mixed * gate_act
        gated_normed = gated * rstd_gate
        nout_ref[at, :] = (gated_normed * ggain).astype(low)
        g_gate += jnp.sum(d_out * gated_normed, axis=0, keepdims=True)
        d_gated = rstd_gate * (ggain * d_out) - gated * (rstd_gate * rstd_gate * rstd_gate * gate_dots)
        d_mixed = d_gated * gate_act
        dmix_ref[at, :] = d_mixed
        dgate_ref[at, :] = (
            d_gated * mixed * sigm * (1.0 + gate_in * (1.0 - sigm))
        ).astype(low)
        g_skip += jnp.sum(d_mixed * act_ref[at, :inner].astype(f32), axis=0, keepdims=True)
        key = key_ref[8 + start : 8 + start + block, :]
        cum = cum_ref[at, :]
        reach = jnp.where(key == first_before, jnp.exp(cum + total_cum), 0.0)
        total_cum = total_cum + cum[block - 1 :, :]
        scot += dot_tn(
            (d_mixed * spread_heads(reach, head_size, inner)).astype(low),
            act_ref[at, inner + state :],
        )
    scot_ref[0:inner, :] = scot.astype(low)
    scot_ref[inner:, :] = sent[inner:, :]
    gsum_ref[...] = jnp.concatenate([g_gate, g_skip, jnp.zeros((6, inner), f32)], axis=0)
    for hop in range(1, tensor):
        sums_copy(hop).wait_send()
    for one in (wa, wb, wd, nm, ct):
        one.drain()


def backward_kernel(
    dp, tensor, group, heads, mean_of,
    normed_ref, cotl_ref, wa_ref, wb_ref, wdt_ref, pre_ref, key_ref, act_ref, raw_ref, cum_ref,
    states_ref, dmix_ref, dgate_ref, nout_ref, scot_ref, gsum_ref,
    x_ref, gain_ref, cot_ref, cxw_ref, cxb_ref, cbw_ref, cbb_ref, head_ref,
    res_ref, gin_ref, gb_ref, ga_ref, gs_ref, gbc_ref, sums_ref,
    dx, dbc, draw, dz, dpre, dbc_all, branch_part, gb_part, rows_part, ga_part, gs_part,
    halo_out, halo_in, halo_bc_out, halo_bc_in, cw, cot, got, small, small_all, sums_own, bc_own,
    b1, b2, b3, bs, br, r1, r2, r3, rs, rr, q1, q2, q3, qs, qr, g1, g2, g3, gs, gr,
    h1, h2, h3, hs_, hr_, k1, k2, k3, ks, kr,
    as_, ar_, hs, hr, ss, sr, ts, tr, us, ur, sl, rl,
):
    tokens = normed_ref.shape[0]
    wide = act_ref.shape[1]
    inner = dmix_ref.shape[1]
    bc = wide - inner
    state = bc // 2
    head_size = inner // heads
    kernel = cxw_ref.shape[0]
    rows, width = x_ref.shape
    part = wa_ref.shape[0] // dp
    data, model = Grid2("dp", dp), Grid2("tensor", tensor)
    block = min(GROUP, tokens)
    steps = tokens // block
    following = lax.rem(data.me + dp - 1, dp)
    f32 = jnp.float32
    units = pl.ds(pl.multiple_of(model.me * inner, LANES), inner)
    own = pl.ds(pl.multiple_of(model.me * rows, rows), rows)
    quarter = bc // tensor
    bc_lane = lax.rem(model.me * quarter, LANES)
    dt_lane = lax.rem(bc_lane + quarter, LANES)

    greet(("dp", dp), ("tensor", tensor))
    line_start = (data.me // group) * group
    place = lax.rem(data.me, group)

    def line_copy(hop):
        return remote(
            scot_ref, got.at[place], sl.at[hop], rl.at[hop], "dp",
            line_start + lax.rem(place + hop, group),
        )

    for hop in range(1, group):
        line_copy(hop).start()
    scatter_br = Scatter(model, branch_part, q1, q2, q3, rows, qs, qr)
    scatter_gb = Scatter(data, gb_part, h1, h2, h3, part, hs_, hr_)
    scatter_bc = Scatter(model, dbc, b1, b2, b3, rows, bs, br)
    scatter_rows = Scatter(model, rows_part, r1, r2, r3, rows, rs, rr)
    scatter_ga = Scatter(data, ga_part, g1, g2, g3, part, gs, gr)
    scatter_gs = Scatter(data, gs_part, k1, k2, k3, part, ks, kr)
    gb_part[:, :inner] = dot_tn(normed_ref[...], dgate_ref[...]).astype(low)
    gb_part[:, inner:] = dot_tn(cotl_ref[...], nout_ref[...]).astype(low)
    scatter_gb.start()
    for index in range(steps):
        at = slice(index * block, (index + 1) * block)
        branch_part[at, :] = dot_nt(nout_ref[at, :], wb_ref[:, inner:]).astype(low)
    scatter_br.start()
    got[place] = scot_ref[...]
    cw[0:kernel, :inner] = cxw_ref[:, units]
    cw[0:kernel, inner:] = cbw_ref[...]
    cw[kernel : kernel + 1, :inner] = cxb_ref[:, units]
    cw[kernel : kernel + 1, inner:] = cbb_ref[...]
    small[...] = jnp.zeros_like(small)
    for hop in range(1, group):
        line_copy(hop).wait()
    leave = jnp.zeros((inner, state), f32)
    for index in range(group - 1, 0, -1):
        factor = got[index, inner : inner + 8, :].astype(f32) + got[index, inner + 8 :, :].astype(f32)
        factor = jnp.concatenate(
            [jnp.broadcast_to(factor[h : h + 1, :], (head_size, LANES)) for h in range(heads)], axis=0
        )
        longer = leave * factor + got[index, :inner, :].astype(f32)
        leave = jnp.where(index > place, longer, leave)
    cot[...] = leave
    rate = head_ref[1:2, :]
    skip = spread_heads(head_ref[0:8, :], head_size, inner, 3)[2:3, :]
    row_i = lax.broadcasted_iota(jnp.int32, (block, block), 0)
    col_i = lax.broadcasted_iota(jnp.int32, (block, block), 1)
    lane = lax.broadcasted_iota(jnp.int32, (block, LANES), 1)
    d_bias = jnp.zeros((1, LANES), f32)
    d_log = jnp.zeros((1, LANES), f32)
    for index in range(steps - 1, -1, -1):
        start = index * block
        at = slice(start, start + block)
        key = key_ref[8 + start : 8 + start + block, :]
        keyt = key.T
        equal = jnp.concatenate([key] * (block // LANES), axis=1) == keyt[0:1, :]
        same, strict = equal & (row_i >= col_i), row_i > col_i
        cum = cum_ref[at, :]
        cumt = cum.T
        raw = raw_ref[at, :]
        dt = softplus(raw)
        dtt = dt.T
        inflow, tail, passing = block_parts(cum, key, key_ref[7 + start : 8 + start, :])
        x, b, c = act_ref[at, :inner], act_ref[at, inner : inner + state], act_ref[at, inner + state :]
        x_wide = x.astype(f32)
        dy = dmix_ref[at, :]
        dy_low = dy.astype(low)
        full, grad = states_ref[index], cot[...]
        full_low, grad_low = full.astype(low), grad.astype(low)
        scores = dot_nt(c, b)
        from_state = dot_nt(c, full_low)
        from_grad = dot_nt(b, grad_low)
        tail_wide = spread_heads(tail, head_size, inner)
        dt_wide = spread_heads(dt, head_size, inner)
        d_in = (dy * spread_heads(inflow, head_size, inner)).astype(low)
        pushed = (x_wide * tail_wide * dt_wide).astype(low)
        d_scores = jnp.zeros((block, block), f32)
        dxd, col_sums = [], []
        change = jnp.zeros((block, LANES), f32)
        for head in range(heads):
            cols = slice(head * head_size, (head + 1) * head_size)
            decay = head_decay(same, cum, cumt, head)
            mixing = scores * decay
            both = dot_nt(dy_low[:, cols], x[:, cols]) * dtt[head : head + 1, :]
            d_scores = d_scores + both * decay
            joint = jnp.where(strict, both * mixing, 0.0)
            change = jnp.where(lane == head, jnp.sum(joint, axis=1, keepdims=True), change)
            col_sums.append(jnp.sum(joint, axis=0, keepdims=True))
            dxd.append(dot_tn(mixing.astype(low), dy_low[:, cols]))
        dxd = jnp.concatenate(dxd, axis=1) + from_grad * tail_wide
        dx[at, :] = dxd * dt_wide + dy * skip
        d_low = d_scores.astype(low)
        dbc[at, state:] = (dot_wide(d_low, b) + dot_wide(d_in, full_low)).astype(low)
        dbc[at, :state] = (dot_tn(d_low, c) + dot_wide(pushed, grad_low)).astype(low)
        through = sum_heads(dy * from_state, head_size) * inflow
        kept = sum_heads(x_wide * from_grad, head_size) * (tail * dt)
        columns = jnp.concatenate(
            col_sums + [jnp.zeros((LANES - heads, block), f32)], axis=0
        ).T
        product = full * grad
        whole = jnp.concatenate(
            [
                jnp.sum(product[h * head_size : (h + 1) * head_size, :], axis=0, keepdims=True)
                for h in range(heads)
            ]
            + [jnp.zeros((LANES - heads, state), f32)],
            axis=0,
        )
        whole = jnp.sum(whole.T, axis=0, keepdims=True)
        d_la = running_sum(change - columns + through - kept, True) + (
            jnp.sum(kept, axis=0, keepdims=True) + passing * whole
        )
        d_log = d_log + jnp.sum(d_la * (dt * rate), axis=0, keepdims=True)
        d_raw = (d_la * rate + sum_heads(dxd * x_wide, head_size)) * jax.nn.sigmoid(raw)
        d_raw = jnp.where(lane < heads, d_raw, 0.0)
        d_bias = d_bias + jnp.sum(d_raw, axis=0, keepdims=True)
        draw[at, :] = d_raw.astype(low)
        cot[...] = grad * rows_of_heads(passing, heads, head_size) + dot_tn(d_in, c)
        if index == steps - 2:
            scatter_br.middle()
            scatter_gb.middle()
    scatter_bc.start()

    def conv_back(cols, get):
        size = cols.stop - cols.start
        dz[0:8, cols] = jnp.zeros((8, size), f32)
        dz[8 + tokens :, cols] = jnp.zeros((8, size), f32)
        tap_sums = [jnp.zeros((1, size), f32) for _ in range(kernel + 1)]
        for index in range(steps):
            start = index * block
            key = key_ref[8 + start : 8 + start + block, :]
            total = jnp.broadcast_to(cw[kernel : kernel + 1, cols], (block, size))
            taps = []
            for offset in range(kernel):
                at = slice(8 - kernel + 1 + offset + start, 8 - kernel + 1 + offset + start + block)
                tap = pre_ref[at, cols]
                if offset < kernel - 1:
                    same = jnp.where(key_ref[at, :] == key, 1.0, 0.0)
                    tap = tap * jnp.concatenate([same] * (size // LANES), axis=1)
                taps.append(tap)
                total = total + cw[offset : offset + 1, cols] * tap
            sigm = jax.nn.sigmoid(total)
            change = get(index) * (sigm * (1.0 + total * (1.0 - sigm)))
            dz[8 + start : 8 + start + block, cols] = change
            for offset in range(kernel):
                tap_sums[offset] += jnp.sum(taps[offset] * change, axis=0, keepdims=True)
            tap_sums[kernel] += jnp.sum(change, axis=0, keepdims=True)
        for offset in range(kernel + 1):
            small[offset : offset + 1, cols] = tap_sums[offset]

    def back_rows(start, size, cols):
        span = cols.stop - cols.start
        key = key_ref[start : start + size, :]
        total = cw[kernel - 1 : kernel, cols] * dz[start : start + size, cols]
        for offset in range(kernel - 1):
            at = slice(start + kernel - 1 - offset, start + kernel - 1 - offset + size)
            same = jnp.where(key_ref[at, :] == key, 1.0, 0.0)
            total = total + cw[offset : offset + 1, cols] * (
                dz[at, cols] * jnp.concatenate([same] * (span // LANES), axis=1)
            )
        return total

    def halo(cols, out, arrived, slot):
        out[...] = back_rows(0, 8, cols)
        copy = remote(out, arrived, hs.at[slot], hr.at[slot], "dp", following)
        copy.start()
        return copy

    def finish_pre(cols, copy, arrived):
        for index in range(steps):
            start = index * block
            value = back_rows(8 + start, block, cols)
            if index == steps - 1:
                copy.wait()
                edge = value[block - 8 :, :] + arrived[...]
                value = jnp.concatenate([value[: block - 8], edge], axis=0)
            dpre[start : start + block, cols] = value.astype(low)

    cols = slice(0, inner)
    conv_back(cols, lambda index: dx[index * block : (index + 1) * block, :])
    copy = halo(cols, halo_out, halo_in, 0)
    scatter_bc.middle()
    finish_pre(cols, copy, halo_in)
    ga_part[...] = dot_tn(normed_ref[...], dpre[:, :inner]).astype(low)
    scatter_ga.start()
    dbc_all[own, :] = scatter_bc.finish().astype(low)
    gather_bc = Gather(model, dbc_all, rows, as_, ar_)
    gather_bc.start()
    for index in range(steps):
        at = slice(index * block, (index + 1) * block)
        part_sum = dot_nt(dgate_ref[at, :], wb_ref[:, :inner])
        part_sum = part_sum + dot_nt(dpre[at, :inner], wa_ref[:, :inner])
        part_sum = part_sum + dot_nt(draw[at, :], wdt_ref[...])
        rows_part[at, :] = part_sum.astype(low)
    scatter_rows.start()
    gather_bc.forward()
    gather_bc.finish()
    cols = slice(inner, wide)
    conv_back(cols, lambda index: dbc_all[index * block : (index + 1) * block, :].astype(f32))
    copy = halo(cols, halo_bc_out, halo_bc_in, 1)
    scatter_rows.middle()
    scatter_ga.middle()
    finish_pre(cols, copy, halo_bc_in)

    def pick_exact(value, one):
        return dot_wide(
            jnp.concatenate(split(value, 3), axis=1), jnp.concatenate([one] * 3, axis=0)
        )

    def picker(count, first, lane_at, many):
        down = lax.broadcasted_iota(jnp.int32, (count, LANES), 0)
        over = lax.broadcasted_iota(jnp.int32, (count, LANES), 1) - lane_at
        return ((down == over + first) & (over >= 0) & (over < many)).astype(f32).astype(low)

    side = (
        dot_wide(dpre[:, inner:], picker(bc, model.me * quarter, bc_lane, quarter))
        + dot_wide(draw[...], picker(LANES, 0, dt_lane, heads))
    ).astype(low)
    gs_part[...] = dot_tn(normed_ref[...], side).astype(low)
    scatter_gs.start()
    d_rows = scatter_rows.finish() + dot_nt(dpre[own, inner:], wa_ref[:, inner:wide])
    scatter_gs.middle()
    x = x_ref[...]
    rstd = lax.rsqrt(jnp.sum(x * x, axis=-1, keepdims=True) / mean_of + EPSILON)
    scaled = gain_ref[...] * d_rows
    small[kernel + 1 : kernel + 2, :width] = jnp.sum(d_rows * x * rstd, axis=0, keepdims=True)
    small[kernel + 2 : kernel + 3, :inner] = gsum_ref[0:1, :]
    d_heads = jnp.concatenate(
        [d_bias, d_log, sum_heads(gsum_ref[...], head_size, 3)[1:2, :], jnp.zeros((5, LANES), f32)],
        axis=0,
    )
    d_heads = pick_exact(d_heads, picker(LANES, 0, model.me * heads, heads))
    for index in range(3):
        small[kernel + 3 : kernel + 4, index * LANES : (index + 1) * LANES] = d_heads[
            index : index + 1, :
        ]

    def small_copy(hop):
        return remote(
            small, small_all.at[hop], ss.at[hop], sr.at[hop], "dp", lax.rem(data.me + hop, dp)
        )

    for hop in range(1, dp):
        small_copy(hop).start()
    gin_ref[...] = (
        cot_ref[...]
        + rstd * scaled
        - x * (rstd * rstd * rstd * (jnp.sum(scaled * x, axis=-1, keepdims=True) / mean_of))
    )
    res_ref[...] = x + scatter_br.finish()
    gb_ref[...] = scatter_gb.finish()
    ga_ref[...] = scatter_ga.finish()
    total = small[...]
    for hop in range(1, dp):
        small_copy(hop).wait_recv()
        total = total + small_all[hop]
    sums_own[...] = total

    def sums_copy(hop):
        return remote(
            sums_own, sums_ref.at[model.me], ts.at[hop], tr.at[hop], "tensor",
            lax.rem(model.me + hop, tensor),
        )

    for hop in range(1, tensor):
        sums_copy(hop).start()
    sums_ref[model.me] = total
    side_sum = scatter_gs.finish()
    gs_ref[...] = pick_exact(side_sum, picker(LANES, dt_lane, 0, heads))
    bc_own[...] = side_sum

    def bc_copy(hop):
        return remote(
            bc_own, gbc_ref.at[model.me], us.at[hop], ur.at[hop], "tensor",
            lax.rem(model.me + hop, tensor),
        )

    for hop in range(1, tensor):
        bc_copy(hop).start()
    gbc_ref[model.me] = side_sum
    for hop in range(1, tensor):
        sums_copy(hop).wait()
        bc_copy(hop).wait()
    for hop in range(1, dp):
        small_copy(hop).wait_send()
    for one in (scatter_bc, scatter_rows, scatter_ga, scatter_gs, scatter_br, scatter_gb, gather_bc):
        one.drain()


def finish_kernel(
    tensor, heads, kernel,
    res_ref, gin_ref, gb_ref, ga_ref, gs_ref, gbc_ref, sums_ref,
    o_res, o_gin, o_norm, o_zx, o_bc, o_dt, o_cxw, o_cxb, o_cbw, o_cbb, o_dtb, o_log, o_skip,
    o_gate, o_out,
):
    part, inner = ga_ref.shape
    width = o_gin.shape[1]
    bc = o_bc.shape[1]
    quarter = bc // tensor
    o_res[...] = res_ref[...]
    o_gin[...] = gin_ref[...]
    o_zx[0] = gb_ref[:, :inner]
    o_zx[1] = ga_ref[...]
    o_dt[...] = gs_ref[:, : o_dt.shape[1]]
    tall = jnp.concatenate(
        [gb_ref[:, inner:], jnp.zeros((-part % LANES, inner), jnp.float32)], axis=0
    )
    o_out[...] = tall.T[:, :part]
    lane = lax.broadcasted_iota(jnp.int32, (part, LANES), 1)
    for start in range(0, bc, LANES):
        tile = jnp.zeros((part, LANES), jnp.float32)
        for one in range(tensor):
            if start <= one * quarter < start + LANES:
                at = one * quarter - start
                tile = jnp.where((lane >= at) & (lane < at + quarter), gbc_ref[one], tile)
        o_bc[:, start : start + LANES] = tile
    total = sums_ref[0]
    for one in range(1, tensor):
        total = total + sums_ref[one]
    o_norm[...] = total[kernel + 1 : kernel + 2, :width]
    o_cbw[...] = sums_ref[0, 0:kernel, inner : inner + bc]
    o_cbb[...] = sums_ref[0, kernel : kernel + 1, inner : inner + bc]
    for one in range(tensor):
        cols = slice(one * inner, (one + 1) * inner)
        o_cxw[:, cols] = sums_ref[one, 0:kernel, :inner]
        o_cxb[:, cols] = sums_ref[one, kernel : kernel + 1, :inner]
        o_gate[:, cols] = sums_ref[one, kernel + 2 : kernel + 3, :inner]
    for index, out in enumerate((o_dtb, o_log, o_skip)):
        out[...] = total[kernel + 3 : kernel + 4, index * LANES : index * LANES + out.shape[1]]


def forward_call(dp, tensor, group, heads, mean_of, sequences, *arrays):
    x, zx, bcw, cxw = arrays[0], arrays[3], arrays[4], arrays[8]
    rows, width = x.shape
    tokens, part, inner = rows * tensor, zx.shape[1], zx.shape[2]
    bc = bcw.shape[1]
    wide, state = inner + bc, bc // 2
    steps = tokens // min(GROUP, tokens)
    shape = jax.ShapeDtypeStruct
    f32 = jnp.float32
    dma = pltpu.SemaphoreType.DMA
    return pl.pallas_call(
        functools.partial(forward_kernel, dp, tensor, group, heads, mean_of, sequences),
        out_shape=(
            shape((tokens, width), low),
            shape((tokens, width), low),
            shape((dp * part, wide), low),
            shape((dp * part, 2 * inner), low),
            shape((dp * part, LANES), low),
            shape((tokens + 8, wide), f32),
            shape((tokens + 16, LANES), f32),
            shape((tokens, wide), low),
            shape((tokens, LANES), f32),
            shape((tokens, LANES), f32),
            shape((steps, inner, state), f32),
            shape((tokens, inner), f32),
            shape((tokens, inner), low),
            shape((tokens, inner), low),
            shape((inner + 16, state), low),
            shape((8, inner), f32),
        ),
        in_specs=vmem(len(arrays)),
        out_specs=tuple(vmem(16)),
        scratch_shapes=[
            pltpu.VMEM((8, wide), f32),
            pltpu.VMEM((dp * 16, LANES), low),
            pltpu.VMEM((8, wide), f32),
            pltpu.VMEM((tokens, inner), f32),
            pltpu.VMEM((tokens, inner), f32),
            pltpu.VMEM((tokens, inner), f32),
            pltpu.VMEM((inner + 16, state), low),
            pltpu.VMEM((group, inner + 16, state), low),
            pltpu.VMEM((inner, state), f32),
            pltpu.VMEM((8 * steps, LANES), f32),
            pltpu.VMEM((8, tokens), f32),
            pltpu.VMEM((tensor, 8, tokens), f32),
            *[dma((2 * n,)) for n in (dp, dp, dp, dp, dp, dp, tensor, tensor, tensor, tensor)],
            dma((2,)), dma((2,)),
            dma((group,)), dma((group,)),
            dma((tensor,)), dma((tensor,)),
        ],
        compiler_params=pltpu.CompilerParams(
            collective_id=0, has_side_effects=True, vmem_limit_bytes=60 * 2**20
        ),
        name="forward",
    )(*arrays)


def backward_call(dp, tensor, group, heads, mean_of, *arrays):
    normed, wa, wb, act, dmix = arrays[0], arrays[2], arrays[3], arrays[7], arrays[11]
    scot, x = arrays[14], arrays[16]
    tokens, wide = act.shape
    inner = dmix.shape[1]
    bc = wide - inner
    state = bc // 2
    rows, width = x.shape
    part = wa.shape[0] // dp
    small = (8, -(-max(width, wide, 3 * LANES) // LANES) * LANES)
    shape = jax.ShapeDtypeStruct
    f32 = jnp.float32
    dma = pltpu.SemaphoreType.DMA
    outs = (
        (rows, width), (rows, width), (part, 2 * inner), (part, inner), (part, LANES),
        (tensor, part, LANES), (tensor,) + small,
    )
    return pl.pallas_call(
        functools.partial(backward_kernel, dp, tensor, group, heads, mean_of),
        out_shape=tuple(shape(one, f32) for one in outs),
        in_specs=vmem(len(arrays)),
        out_specs=tuple(vmem(len(outs))),
        scratch_shapes=[
            pltpu.VMEM((tokens, inner), f32),
            pltpu.VMEM((tokens, bc), low),
            pltpu.VMEM((tokens, LANES), low),
            pltpu.VMEM((tokens + 16, wide), f32),
            pltpu.VMEM((tokens, wide), low),
            pltpu.VMEM((tokens, bc), low),
            pltpu.VMEM((tokens, width), low),
            pltpu.VMEM((dp * part, 2 * inner), low),
            pltpu.VMEM((tokens, width), low),
            pltpu.VMEM((dp * part, inner), low),
            pltpu.VMEM((dp * part, LANES), low),
            pltpu.VMEM((8, inner), f32),
            pltpu.VMEM((8, inner), f32),
            pltpu.VMEM((8, bc), f32),
            pltpu.VMEM((8, bc), f32),
            pltpu.VMEM((8, wide), f32),
            pltpu.VMEM((inner, state), f32),
            pltpu.VMEM((group,) + scot.shape, low),
            pltpu.VMEM(small, f32),
            pltpu.VMEM((dp,) + small, f32),
            pltpu.VMEM(small, f32),
            pltpu.VMEM((part, LANES), f32),
            *Scatter.scratch(tensor, rows, bc),
            *Scatter.scratch(tensor, rows, width),
            *Scatter.scratch(tensor, rows, width),
            *Scatter.scratch(dp, part, inner),
            *Scatter.scratch(dp, part, 2 * inner),
            *Scatter.scratch(dp, part, LANES),
            dma((2 * tensor,)), dma((2 * tensor,)),
            dma((2,)), dma((2,)),
            dma((dp,)), dma((dp,)),
            dma((tensor,)), dma((tensor,)),
            dma((tensor,)), dma((tensor,)),
            dma((group,)), dma((group,)),
        ],
        compiler_params=pltpu.CompilerParams(
            collective_id=1, has_side_effects=True, vmem_limit_bytes=63 * 2**20
        ),
        name="backward",
    )(*arrays)


def finish_call(tensor, heads, kernel, inner_total, heads_total, bc, arrays):
    res, gin, gb, ga = arrays[:4]
    part, inner = ga.shape
    width = res.shape[1]
    outs = (
        res.shape, gin.shape, (1, width), (2, part, inner), (part, bc), (part, heads),
        (kernel, inner_total), (1, inner_total), (kernel, bc), (1, bc), (1, heads_total),
        (1, heads_total), (1, heads_total), (1, inner_total), (inner, part),
    )
    return pl.pallas_call(
        functools.partial(finish_kernel, tensor, heads, kernel),
        out_shape=tuple(jax.ShapeDtypeStruct(one, jnp.float32) for one in outs),
        in_specs=vmem(len(arrays)),
        out_specs=tuple(vmem(len(outs))),
        compiler_params=pltpu.CompilerParams(vmem_limit_bytes=32 * 2**20),
        name="finish",
    )(*arrays)


def pad_to(array, size, axis):
    widths = [(0, 0)] * array.ndim
    widths[axis] = (0, size - array.shape[axis])
    return jnp.pad(array, widths)


def per_device(
    block_input,
    norm_gain,
    zx_weight,
    bc_weight,
    dt_weight,
    conv_x_weight,
    conv_x_bias,
    conv_bc_weight,
    conv_bc_bias,
    dt_bias,
    decay_log,
    skip_gain,
    gate_gain,
    out_weight,
    segments,
    cotangent,
):
    tensor_count = lax.axis_size("tensor")
    tensor_index = lax.axis_index("tensor")
    data_count = lax.axis_size("dp")
    token_count = segments.shape[0]
    row_count, width = block_input.shape
    part = zx_weight.shape[1]
    heads_here = dt_weight.shape[1]
    heads_total = dt_bias.shape[0]
    taps, inner_total = conv_x_weight.shape
    bc_size = bc_weight.shape[1]
    padded = -(-part // 16) * 16
    columns = data_count * padded

    def widen(array):
        if padded == part:
            return array
        lead = array.shape[:-1]
        return pad_to(array.reshape(lead + (data_count, part)), padded, -1).reshape(lead + (columns,))

    def narrow(array):
        if padded == part:
            return array
        lead = array.shape[:-1]
        return array.reshape(lead + (data_count, padded))[..., :part].reshape(lead + (width,))

    group = max(1, LENGTH // token_count)
    if data_count % group:
        group = data_count
    sequences = data_count * token_count // LENGTH + 1
    per_head = jnp.stack([dt_bias, -jnp.exp(decay_log), skip_gain])
    per_head = lax.dynamic_slice_in_dim(per_head, tensor_index * heads_here, heads_here, 1)
    per_head = jnp.pad(per_head, ((0, 5), (0, LANES - heads_here)))
    x_rows, cot_rows, norm_row = widen(block_input), widen(cotangent), widen(norm_gain)[None, :]
    conv = (conv_x_weight, conv_x_bias[None, :], conv_bc_weight, conv_bc_bias[None, :], per_head)
    kept = forward_call(
        data_count, tensor_count, group, heads_here, width, sequences,
        x_rows, norm_row, cot_rows, pad_to(zx_weight, padded, 1), pad_to(bc_weight, padded, 0),
        pad_to(pad_to(dt_weight.T, 16, 0), LANES, 1), out_weight, segments[None, :], *conv,
        gate_gain[None, :],
    )
    sums = backward_call(
        data_count, tensor_count, group, heads_here, width, *kept, x_rows, norm_row, cot_rows, *conv
    )
    outs = list(
        finish_call(tensor_count, heads_here, taps, inner_total, heads_total, bc_size, sums)
    )
    for index in (0, 1, 2):
        outs[index] = narrow(outs[index])
    if padded != part:
        outs[3] = outs[3][:, :part]
        outs[4], outs[5], outs[14] = outs[4][:part], outs[5][:part], outs[14][:, :part]
    for index in (2, 7, 9, 10, 11, 12, 13):
        outs[index] = outs[index][0]
    return tuple(outs)


def solution(mesh):
    in_specs = (
        P(("dp", "tensor"), None),
        P(),
        P(None, "dp", "tensor"),
        P("dp", None),
        P("dp", "tensor"),
        P(),
        P(),
        P(),
        P(),
        P(),
        P(),
        P(),
        P(),
        P("tensor", "dp"),
        P("dp"),
        P(("dp", "tensor"), None),
    )
    out_specs = (
        P(("dp", "tensor"), None),
        P(("dp", "tensor"), None),
        P(),
        P(None, "dp", "tensor"),
        P("dp", None),
        P("dp", "tensor"),
        P(),
        P(),
        P(),
        P(),
        P(),
        P(),
        P(),
        P(),
        P("tensor", "dp"),
    )
    return jax.shard_map(
        per_device, mesh=mesh, in_specs=in_specs, out_specs=out_specs, check_vma=False
    )
```

```python
import functools
import jax
import jax.numpy as jnp
from jax import lax
from jax.experimental import pallas as pl
from jax.experimental.pallas import tpu as pltpu
from jax.sharding import PartitionSpec as P

GROUP = 256
LENGTH = 4096
EPSILON = 1e-05
PAD = 8
LANES = 128
MESH = pl.DeviceIdType.MESH
low = jnp.bfloat16


def dot_wide(left, right):
    return jnp.dot(left, right, preferred_element_type=jnp.float32)


def dot_nt(left, right):
    return lax.dot_general(left, right, (((1,), (1,)), ((), ())), preferred_element_type=jnp.float32)


def dot_tn(left, right):
    return lax.dot_general(left, right, (((0,), (0,)), ((), ())), preferred_element_type=jnp.float32)


def head_decay(same, cum, cumt, head):
    spread = jnp.where(same, cum[:, head : head + 1] - cumt[head : head + 1, :], -1e30)
    return jnp.exp(spread)


def vmem(count):
    return [pl.BlockSpec(memory_space=pltpu.VMEM)] * count


class Grid2:
    def __init__(self, axis, count):
        self.axis, self.count = axis, count
        self.inner = 2 if count % 2 == 0 else 1
        self.outer = count // self.inner
        self.me = lax.axis_index(axis)
        self.mi = lax.rem(self.me, self.inner)
        self.mo = self.me // self.inner

    def at(self, hop, inner):
        return lax.rem(self.mo + hop + self.outer, self.outer) * self.inner + inner

    @property
    def partner(self):
        return self.mo * self.inner + (self.inner - 1 - self.mi)


def remote(src, dst, send, recv, axis, index):
    return pltpu.make_async_remote_copy(
        src_ref=src, dst_ref=dst, send_sem=send, recv_sem=recv,
        device_id={axis: index}, device_id_type=MESH,
    )


def greet(*axes):
    barrier = pltpu.get_barrier_semaphore()
    total = 0
    for axis, count in axes:
        me = lax.axis_index(axis)
        for hop in range(1, count):
            pl.semaphore_signal(
                barrier, inc=1, device_id={axis: lax.rem(me + hop, count)}, device_id_type=MESH
            )
            total += 1
    if total:
        pl.semaphore_wait(barrier, total)


class Gather:
    def __init__(self, grid, ref, rows, send, recv):
        self.grid, self.ref, self.rows, self.send, self.recv = grid, ref, rows, send, recv

    @staticmethod
    def semaphores(count):
        return 2 * count

    def block(self, index):
        return self.ref.at[pl.ds(pl.multiple_of(index * self.rows, self.rows), self.rows), :]

    def copy(self, index, slot, target):
        piece = self.block(index)
        return remote(piece, piece, self.send.at[slot], self.recv.at[slot], self.grid.axis, target)

    def start(self):
        g = self.grid
        if g.inner > 1:
            self.copy(g.me, 0, g.partner).start()
        for hop in range(1, g.outer):
            self.copy(g.me, hop, g.at(hop, g.mi)).start()

    def forward(self):
        g = self.grid
        for hop in range(1, g.outer):
            source = g.at(-hop, g.mi)
            self.copy(source, hop, g.me).wait_recv()
            if g.inner > 1:
                self.copy(source, g.outer + hop, g.partner).start()

    def finish(self):
        g = self.grid
        if g.inner > 1:
            self.copy(g.partner, 0, g.partner).wait_recv()
            for hop in range(1, g.outer):
                source = g.at(-hop, g.inner - 1 - g.mi)
                self.copy(source, g.outer + hop, g.partner).wait_recv()

    def drain(self):
        g = self.grid
        if g.inner > 1:
            self.copy(g.me, 0, g.partner).wait_send()
            for hop in range(1, g.outer):
                self.copy(g.me, g.outer + hop, g.partner).wait_send()
        for hop in range(1, g.outer):
            self.copy(g.me, hop, g.partner).wait_send()


class Scatter:
    def __init__(self, grid, src, first, second, landed, rows, send, recv):
        self.grid, self.src, self.rows, self.send, self.recv = grid, src, rows, send, recv
        self.first, self.second, self.landed = first, second, landed

    @staticmethod
    def scratch(count, rows, width):
        outer = count // (2 if count % 2 == 0 else 1)
        return [
            pltpu.VMEM((outer, rows, width), low),
            pltpu.VMEM((outer, rows, width), low),
            pltpu.VMEM((outer, rows, width), low),
            pltpu.SemaphoreType.DMA((2 * outer,)),
            pltpu.SemaphoreType.DMA((2 * outer,)),
        ]

    def block(self, index):
        return self.src.at[pl.ds(pl.multiple_of(index * self.rows, self.rows), self.rows), :]

    def over(self, hop):
        g = self.grid
        return remote(
            self.block(g.at(hop, g.inner - 1 - g.mi)), self.first.at[hop],
            self.send.at[hop], self.recv.at[hop], g.axis, g.partner,
        )

    def along(self, hop):
        g = self.grid
        slot = g.outer + hop
        return remote(
            self.second.at[hop], self.landed.at[hop],
            self.send.at[slot], self.recv.at[slot], g.axis, g.at(hop, g.mi),
        )

    def start(self):
        if self.grid.inner > 1:
            for hop in list(range(1, self.grid.outer)) + [0]:
                self.over(hop).start()

    def pair(self, hop):
        g = self.grid
        total = self.block(g.at(hop, g.mi))[...].astype(jnp.float32)
        if g.inner > 1:
            self.over(hop).wait_recv()
            total = total + self.first[hop].astype(jnp.float32)
        return total

    def middle(self):
        for hop in range(1, self.grid.outer):
            self.second[hop] = self.pair(hop).astype(low)
            self.along(hop).start()

    def finish(self):
        g = self.grid
        total = self.pair(0)
        for hop in range(1, g.outer):
            self.along(hop).wait_recv()
            total = total + self.landed[hop].astype(jnp.float32)
        return total

    def drain(self):
        g = self.grid
        for hop in range(g.outer):
            if g.inner > 1:
                self.over(hop).wait_send()
            if hop:
                self.along(hop).wait_send()


def split(value, pieces):
    out = []
    for _ in range(pieces):
        piece = value.astype(low)
        out.append(piece)
        value = value - piece.astype(jnp.float32)
    return out


def spread_heads(value, head_size, inner, pieces=2):
    one = (
        lax.broadcasted_iota(jnp.int32, (LANES, inner), 1) // head_size
        == lax.broadcasted_iota(jnp.int32, (LANES, inner), 0)
    ).astype(jnp.float32).astype(low)
    return dot_wide(
        jnp.concatenate(split(value, pieces), axis=1), jnp.concatenate([one] * pieces, axis=0)
    )


def sum_heads(value, head_size, pieces=2):
    inner = value.shape[1]
    one = (
        lax.broadcasted_iota(jnp.int32, (inner, LANES), 0) // head_size
        == lax.broadcasted_iota(jnp.int32, (inner, LANES), 1)
    ).astype(jnp.float32).astype(low)
    return dot_wide(
        jnp.concatenate(split(value, pieces), axis=1), jnp.concatenate([one] * pieces, axis=0)
    )


def running_sum(value, reverse=False):
    size = value.shape[0]
    row = lax.broadcasted_iota(jnp.int32, (size, size), 0)
    col = lax.broadcasted_iota(jnp.int32, (size, size), 1)
    keep = (row <= col) if reverse else (row >= col)
    keep = keep.astype(jnp.float32).astype(low)
    pieces = split(value, 3)
    total = dot_wide(keep, jnp.concatenate(pieces, axis=1))
    width = value.shape[1]
    return total[:, :width] + total[:, width : 2 * width] + total[:, 2 * width :]


def rows_of_heads(row, heads, head_size):
    turned = jnp.broadcast_to(row, (LANES, LANES)).T
    return jnp.concatenate(
        [jnp.broadcast_to(turned[h : h + 1, :], (head_size, LANES)) for h in range(heads)], axis=0
    )


def softplus(value):
    return jnp.maximum(value, 0.0) + jnp.log1p(jnp.exp(-jnp.abs(value)))


def block_parts(cum, key, before):
    size = cum.shape[0]
    last_key, last = key[size - 1 :, :], cum[size - 1 :, :]
    inflow = jnp.where(key == before, jnp.exp(cum), 0.0)
    tail = jnp.where(key == last_key, jnp.exp(last - cum), 0.0)
    passing = jnp.where(last_key == before, jnp.exp(last), 0.0)
    return inflow, tail, passing


def forward_part(
    dp, tensor, group, heads, mean_of, sequences,
    x_ref, gain_ref, cot_ref, zx_ref, bcw_ref, dtt_ref, out_ref, seg_ref, cxw_ref, cxb_ref, cbw_ref,
    cbb_ref, head_ref, ggain_ref,
    normed_ref, cotl_ref, wa_ref, wb_ref, wdt_ref, pre_ref, key_ref, act_ref, raw_ref, cum_ref,
    states_ref, dmix_ref, dgate_ref, nout_ref, scot_ref, gsum_ref,
    tail, dtall, cw, y, gate, dno, sent, got, ends, decays, sums, sums_all,
    sa, ra, sb, rb, sd, rd, sn, rn, sc, rc, sh, rh, sl, rl, ss, rs,
):
    rows, width = x_ref.shape
    tokens = normed_ref.shape[0]
    part, inner = zx_ref.shape[1], zx_ref.shape[2]
    bc = bcw_ref.shape[1]
    wide, state = inner + bc, bc // 2
    head_size = inner // heads
    kernel = cxw_ref.shape[0]
    block = min(GROUP, tokens)
    steps = tokens // block
    f32 = jnp.float32
    data, model = Grid2("dp", dp), Grid2("tensor", tensor)
    mine = pl.ds(pl.multiple_of(data.me * part, part), part)
    own = pl.ds(pl.multiple_of(model.me * rows, rows), rows)
    units = pl.ds(pl.multiple_of(model.me * inner, LANES), inner)

    wa_ref[mine, :inner] = zx_ref[1]
    wa_ref[mine, inner:] = bcw_ref[...]
    wb_ref[mine, :inner] = zx_ref[0]
    wb_ref[mine, inner:] = out_ref[...]
    flat = dtt_ref[...].astype(f32)
    flat = jnp.concatenate([flat, jnp.zeros((heads, LANES - flat.shape[1]), f32)], axis=1)
    flat = jnp.concatenate([flat, jnp.zeros((16 - heads, LANES), f32)], axis=0)
    dtall[pl.ds(pl.multiple_of(data.me * 16, 16), 16), :] = flat.astype(low)
    x = x_ref[...]
    rstd = lax.rsqrt(jnp.sum(x * x, axis=-1, keepdims=True) / mean_of + EPSILON)
    normed_ref[own, :] = (x * rstd * gain_ref[...][None, :]).astype(low)
    cotl_ref[own, :] = cot_ref[...].astype(low)
    for index in range(steps):
        at = slice(index * block, (index + 1) * block)
        line = seg_ref[at][None, :].astype(f32)
        key_ref[8 + index * block : 8 + (index + 1) * block, :] = jnp.broadcast_to(
            line, (LANES, block)
        ).T
    key_ref[8 + tokens :, :] = jnp.zeros((8, LANES), f32)
    greet(("dp", dp), ("tensor", tensor))
    wa = Gather(data, wa_ref, part, sa, ra)
    wb = Gather(data, wb_ref, part, sb, rb)
    wd = Gather(data, dtall, 16, sd, rd)
    nm = Gather(model, normed_ref, rows, sn, rn)
    ct = Gather(model, cotl_ref, rows, sc, rc)
    following = lax.rem(data.me + 1, dp)
    seg_copy = remote(
        key_ref.at[pl.ds(tokens, 8), :], key_ref.at[pl.ds(0, 8), :], sh.at[0], rh.at[0], "dp",
        following,
    )
    pre_copy = remote(
        tail, pre_ref.at[pl.ds(0, 8), :], sh.at[1], rh.at[1], "dp", following
    )
    wd.start()
    wa.start()
    nm.start()
    seg_copy.start()
    nm.forward()
    ct.start()
    wd.forward()
    wa.forward()
    wb.start()
    cw[0:kernel, :inner] = cxw_ref[:, units]
    cw[0:kernel, inner:] = cbw_ref[...]
    cw[kernel : kernel + 1, :inner] = cxb_ref[units][None, :]
    cw[kernel : kernel + 1, inner:] = cbb_ref[...][None, :]
    wd.finish()
    turn = (
        lax.broadcasted_iota(jnp.int32, (part, LANES), 0)
        == lax.broadcasted_iota(jnp.int32, (part, LANES), 1)
    ).astype(f32).astype(low)
    for index in range(dp):
        shard = jnp.concatenate(
            [dtall[index * 16 : (index + 1) * 16, :], jnp.zeros((LANES - 16, LANES), low)], axis=0
        )
        wdt_ref[index * part : (index + 1) * part, :] = dot_nt(turn, shard).astype(low)
    nm.finish()
    wa.finish()
    last = steps - 1
    bias, rate = head_ref[0:1, :], head_ref[1:2, :]
    for index in [last] + list(range(last)):
        at = slice(index * block, (index + 1) * block)
        first = dot_wide(normed_ref[at, :], wa_ref[...])
        pre_ref[8 + index * block : 8 + (index + 1) * block, :] = first.astype(low).astype(f32)
        if index == last:
            tail[...] = pre_ref[tokens : tokens + 8, :]
            pre_copy.start()
        raw_ref[at, :] = dot_wide(normed_ref[at, :], wdt_ref[...]) + bias
    seg_copy.wait()
    pos = lax.broadcasted_iota(jnp.int32, (tokens + 16, LANES), 0) + (data.me * tokens - 8 + LENGTH)
    key_ref[...] = key_ref[...] * sequences + (pos // LENGTH).astype(f32)
    ends[...] = jnp.zeros_like(ends)
    total_cum = jnp.zeros((1, LANES), f32)
    first_before = key_ref[7:8, :]
    before = first_before
    pre_copy.wait()
    for index in range(steps):
        start = index * block
        at = slice(start, start + block)
        key = key_ref[8 + start : 8 + start + block, :]
        total = jnp.broadcast_to(cw[kernel : kernel + 1, :], (block, wide))
        for offset in range(kernel):
            shift = slice(8 - kernel + 1 + offset + start, 8 - kernel + 1 + offset + start + block)
            tap = cw[offset : offset + 1, :] * pre_ref[shift, :]
            if offset < kernel - 1:
                same = jnp.where(key_ref[shift, :] == key, 1.0, 0.0)
                tap = tap * jnp.concatenate([same] * (wide // LANES), axis=1)
            total = total + tap
        act_ref[at, :] = (total * jax.nn.sigmoid(total)).astype(low)
        dt = softplus(raw_ref[at, :])
        cum = running_sum(dt * rate)
        cum_ref[at, :] = cum
        inflow, tail_w, passing = block_parts(cum, key, before)
        pushed = (
            act_ref[at, :inner].astype(f32) * spread_heads(tail_w * dt, head_size, inner)
        ).astype(low)
        states_ref[index] = ends[...]
        reach = jnp.where(before == first_before, jnp.exp(total_cum), 0.0)
        decays[index * 8 : index * 8 + 1, :] = reach
        ends[...] = ends[...] * rows_of_heads(passing, heads, head_size) + dot_tn(
            pushed, act_ref[at, inner : inner + state]
        )
        total_cum = total_cum + cum[block - 1 :, :]
        before = key[block - 1 :, :]
        if index == 0:
            ct.forward()
    reach = jnp.where(before == first_before, jnp.exp(total_cum), 0.0)
    turned = jnp.broadcast_to(reach, (LANES, LANES)).T[:8, :]
    hi, lo = split(turned, 2)
    sent[0:inner, :] = ends[...].astype(low)
    sent[inner : inner + 16, :] = jnp.concatenate([hi, lo], axis=0)
    line_start = (data.me // group) * group
    place = lax.rem(data.me, group)

    def line_copy(hop):
        return remote(
            sent, got.at[place], sl.at[hop], rl.at[hop], "dp",
            line_start + lax.rem(place + hop, group),
        )

    for hop in range(1, group):
        line_copy(hop).start()
    got[place] = sent[...]
    row_i = lax.broadcasted_iota(jnp.int32, (block, block), 0)
    col_i = lax.broadcasted_iota(jnp.int32, (block, block), 1)
    for index in range(steps):
        start = index * block
        at = slice(start, start + block)
        key = key_ref[8 + start : 8 + start + block, :]
        keyt = key.T
        same = (row_i >= col_i) & (
            jnp.concatenate([key] * (block // LANES), axis=1) == keyt[0:1, :]
        )
        cum = cum_ref[at, :]
        cumt = cum.T
        dtt = softplus(raw_ref[at, :]).T
        x = act_ref[at, :inner]
        scores = dot_nt(act_ref[at, inner + state :], act_ref[at, inner : inner + state])
        for head in range(heads):
            cols = slice(head * head_size, (head + 1) * head_size)
            mixing = (
                scores * head_decay(same, cum, cumt, head) * dtt[head : head + 1, :]
            ).astype(low)
            y[at, cols] = dot_wide(mixing, x[:, cols])
        if index == 0:
            wb.forward()
    ct.finish()
    wb.finish()
    for index in range(steps):
        at = slice(index * block, (index + 1) * block)
        gate[at, :] = dot_wide(normed_ref[at, :], wb_ref[:, :inner])
        dno[at, :] = dot_wide(cotl_ref[at, :], wb_ref[:, inner:])
    for hop in range(1, group):
        line_copy(hop).wait()
    entry = jnp.zeros((inner, state), f32)
    for index in range(group - 1):
        factor = got[index, inner : inner + 8, :].astype(f32) + got[index, inner + 8 :, :].astype(f32)
        factor = jnp.concatenate(
            [jnp.broadcast_to(factor[h : h + 1, :], (head_size, LANES)) for h in range(heads)], axis=0
        )
        longer = entry * factor + got[index, :inner, :].astype(f32)
        entry = jnp.where(index < place, longer, entry)
    skip = spread_heads(head_ref[0:8, :], head_size, inner, 3)[2:3, :]
    ggain = ggain_ref[units][None, :]
    before = first_before
    for index in range(steps):
        start = index * block
        at = slice(start, start + block)
        full = states_ref[index] + entry * rows_of_heads(
            decays[index * 8 : index * 8 + 1, :], heads, head_size
        )
        states_ref[index] = full
        key = key_ref[8 + start : 8 + start + block, :]
        inflow = jnp.where(key == before, jnp.exp(cum_ref[at, :]), 0.0)
        before = key[block - 1 :, :]
        mixed = (
            y[at, :]
            + dot_nt(act_ref[at, inner + state :], full.astype(low))
            * spread_heads(inflow, head_size, inner)
            + skip * act_ref[at, :inner].astype(f32)
        )
        y[at, :] = mixed
        gate_in = gate[at, :]
        gated = mixed * (gate_in * jax.nn.sigmoid(gate_in))
        squares = jnp.sum(gated * gated, axis=1, keepdims=True)
        dots = jnp.sum(gated * (ggain * dno[at, :]), axis=1, keepdims=True)
        lane = lax.broadcasted_iota(jnp.int32, (block, LANES), 1)
        both = jnp.where(lane == 0, squares, jnp.where(lane == 1, dots, 0.0))
        sums[:, at] = both.T[:8, :]

    def sums_copy(hop):
        return remote(
            sums, sums_all.at[hop], ss.at[hop], rs.at[hop], "tensor",
            lax.rem(model.me + hop, tensor),
        )

    for hop in range(1, tensor):
        sums_copy(hop).start()
    for hop in range(1, tensor):
        sums_copy(hop).wait_recv()
    before = first_before
    to_exit = jnp.zeros((1, LANES), f32)
    scot = jnp.zeros((inner, state), f32)
    g_gate = jnp.zeros((1, inner), f32)
    g_skip = jnp.zeros((1, inner), f32)
    total_cum = jnp.zeros((1, LANES), f32)
    for index in range(steps):
        start = index * block
        at = slice(start, start + block)
        total = sums[:, at]
        for hop in range(1, tensor):
            total = total + sums_all[hop, :, at]
        total = total / (inner * tensor)
        turned = jnp.concatenate([total, jnp.zeros((LANES - 8, block), f32)], axis=0).T
        rstd_gate = lax.rsqrt(turned[:, 0:1] + EPSILON)
        gate_dots = turned[:, 1:2]
        gate_in, mixed, d_out = gate[at, :], y[at, :], dno[at, :]
        sigm = jax.nn.sigmoid(gate_in)
        gate_act = gate_in * sigm
        gated = mixed * gate_act
        gated_normed = gated * rstd_gate
        nout_ref[at, :] = (gated_normed * ggain).astype(low)
        g_gate += jnp.sum(d_out * gated_normed, axis=0, keepdims=True)
        d_gated = rstd_gate * (ggain * d_out) - gated * (rstd_gate * rstd_gate * rstd_gate * gate_dots)
        d_mixed = d_gated * gate_act
        dmix_ref[at, :] = d_mixed
        dgate_ref[at, :] = (
            d_gated * mixed * sigm * (1.0 + gate_in * (1.0 - sigm))
        ).astype(low)
        g_skip += jnp.sum(d_mixed * act_ref[at, :inner].astype(f32), axis=0, keepdims=True)
        key = key_ref[8 + start : 8 + start + block, :]
        cum = cum_ref[at, :]
        reach = jnp.where(key == first_before, jnp.exp(cum + total_cum), 0.0)
        total_cum = total_cum + cum[block - 1 :, :]
        scot += dot_tn(
            (d_mixed * spread_heads(reach, head_size, inner)).astype(low),
            act_ref[at, inner + state :],
        )
    scot_ref[0:inner, :] = scot.astype(low)
    scot_ref[inner:, :] = sent[inner:, :]
    gsum_ref[...] = jnp.concatenate([g_gate, g_skip, jnp.zeros((6, inner), f32)], axis=0)
    for hop in range(1, tensor):
        sums_copy(hop).wait_send()
    for one in (wa, wb, wd, nm, ct):
        one.drain()


def backward_part(
    dp, tensor, group, heads, kernel, mean_of,
    normed_ref, cotl_ref, wa_ref, wb_ref, wdt_ref, pre_ref, key_ref, act_ref, raw_ref, cum_ref,
    states_ref, dmix_ref, dgate_ref, nout_ref, scot_ref, gsum_ref,
    x_ref, gain_ref, cot_ref, cw, head_ref,
    packed,
    dx, dbc, draw, dz, dpre, dbc_all, branch_part, gb_part, rows_part, ga_part, gs_part,
    halo_out, halo_in, halo_bc_out, halo_bc_in, cot, got, small, small_all, sums_own, bc_own, gbc_ref, sums_ref,
    b1, b2, b3, bs, br, r1, r2, r3, rs, rr, q1, q2, q3, qs, qr, g1, g2, g3, gs, gr,
    h1, h2, h3, hs_, hr_, k1, k2, k3, ks, kr,
    as_, ar_, hs, hr, ss, sr, ts, tr, us, ur, sl, rl,
):
    tokens = normed_ref.shape[0]
    wide = act_ref.shape[1]
    inner = dmix_ref.shape[1]
    bc = wide - inner
    state = bc // 2
    head_size = inner // heads
    rows, width = x_ref.shape
    part = wa_ref.shape[0] // dp
    data, model = Grid2("dp", dp), Grid2("tensor", tensor)
    block = min(GROUP, tokens)
    steps = tokens // block
    following = lax.rem(data.me + dp - 1, dp)
    f32 = jnp.float32
    own = pl.ds(pl.multiple_of(model.me * rows, rows), rows)
    quarter = bc // tensor
    bc_lane = lax.rem(model.me * quarter, LANES)
    dt_lane = lax.rem(bc_lane + quarter, LANES)

    line_start = (data.me // group) * group
    place = lax.rem(data.me, group)

    def line_copy(hop):
        return remote(
            scot_ref, got.at[place], sl.at[hop], rl.at[hop], "dp",
            line_start + lax.rem(place + hop, group),
        )

    for hop in range(1, group):
        line_copy(hop).start()
    scatter_br = Scatter(model, branch_part, q1, q2, q3, rows, qs, qr)
    scatter_gb = Scatter(data, gb_part, h1, h2, h3, part, hs_, hr_)
    scatter_bc = Scatter(model, dbc, b1, b2, b3, rows, bs, br)
    scatter_rows = Scatter(model, rows_part, r1, r2, r3, rows, rs, rr)
    scatter_ga = Scatter(data, ga_part, g1, g2, g3, part, gs, gr)
    scatter_gs = Scatter(data, gs_part, k1, k2, k3, part, ks, kr)
    gb_part[:, :inner] = dot_tn(normed_ref[...], dgate_ref[...]).astype(low)
    gb_part[:, inner:] = dot_tn(cotl_ref[...], nout_ref[...]).astype(low)
    scatter_gb.start()
    for index in range(steps):
        at = slice(index * block, (index + 1) * block)
        branch_part[at, :] = dot_nt(nout_ref[at, :], wb_ref[:, inner:]).astype(low)
    scatter_br.start()
    got[place] = scot_ref[...]
    small[...] = jnp.zeros_like(small)
    for hop in range(1, group):
        line_copy(hop).wait()
    leave = jnp.zeros((inner, state), f32)
    for index in range(group - 1, 0, -1):
        factor = got[index, inner : inner + 8, :].astype(f32) + got[index, inner + 8 :, :].astype(f32)
        factor = jnp.concatenate(
            [jnp.broadcast_to(factor[h : h + 1, :], (head_size, LANES)) for h in range(heads)], axis=0
        )
        longer = leave * factor + got[index, :inner, :].astype(f32)
        leave = jnp.where(index > place, longer, leave)
    cot[...] = leave
    rate = head_ref[1:2, :]
    skip = spread_heads(head_ref[0:8, :], head_size, inner, 3)[2:3, :]
    row_i = lax.broadcasted_iota(jnp.int32, (block, block), 0)
    col_i = lax.broadcasted_iota(jnp.int32, (block, block), 1)
    lane = lax.broadcasted_iota(jnp.int32, (block, LANES), 1)
    d_bias = jnp.zeros((1, LANES), f32)
    d_log = jnp.zeros((1, LANES), f32)
    for index in range(steps - 1, -1, -1):
        start = index * block
        at = slice(start, start + block)
        key = key_ref[8 + start : 8 + start + block, :]
        keyt = key.T
        equal = jnp.concatenate([key] * (block // LANES), axis=1) == keyt[0:1, :]
        same, strict = equal & (row_i >= col_i), row_i > col_i
        cum = cum_ref[at, :]
        cumt = cum.T
        raw = raw_ref[at, :]
        dt = softplus(raw)
        dtt = dt.T
        inflow, tail, passing = block_parts(cum, key, key_ref[7 + start : 8 + start, :])
        x, b, c = act_ref[at, :inner], act_ref[at, inner : inner + state], act_ref[at, inner + state :]
        x_wide = x.astype(f32)
        dy = dmix_ref[at, :]
        dy_low = dy.astype(low)
        full, grad = states_ref[index], cot[...]
        full_low, grad_low = full.astype(low), grad.astype(low)
        scores = dot_nt(c, b)
        from_state = dot_nt(c, full_low)
        from_grad = dot_nt(b, grad_low)
        tail_wide = spread_heads(tail, head_size, inner)
        dt_wide = spread_heads(dt, head_size, inner)
        d_in = (dy * spread_heads(inflow, head_size, inner)).astype(low)
        pushed = (x_wide * tail_wide * dt_wide).astype(low)
        d_scores = jnp.zeros((block, block), f32)
        dxd, col_sums = [], []
        change = jnp.zeros((block, LANES), f32)
        for head in range(heads):
            cols = slice(head * head_size, (head + 1) * head_size)
            decay = head_decay(same, cum, cumt, head)
            mixing = scores * decay
            both = dot_nt(dy_low[:, cols], x[:, cols]) * dtt[head : head + 1, :]
            d_scores = d_scores + both * decay
            joint = jnp.where(strict, both * mixing, 0.0)
            change = jnp.where(lane == head, jnp.sum(joint, axis=1, keepdims=True), change)
            col_sums.append(jnp.sum(joint, axis=0, keepdims=True))
            dxd.append(dot_tn(mixing.astype(low), dy_low[:, cols]))
        dxd = jnp.concatenate(dxd, axis=1) + from_grad * tail_wide
        dx[at, :] = dxd * dt_wide + dy * skip
        d_low = d_scores.astype(low)
        dbc[at, state:] = (dot_wide(d_low, b) + dot_wide(d_in, full_low)).astype(low)
        dbc[at, :state] = (dot_tn(d_low, c) + dot_wide(pushed, grad_low)).astype(low)
        through = sum_heads(dy * from_state, head_size) * inflow
        kept = sum_heads(x_wide * from_grad, head_size) * (tail * dt)
        columns = jnp.concatenate(
            col_sums + [jnp.zeros((LANES - heads, block), f32)], axis=0
        ).T
        product = full * grad
        whole = jnp.concatenate(
            [
                jnp.sum(product[h * head_size : (h + 1) * head_size, :], axis=0, keepdims=True)
                for h in range(heads)
            ]
            + [jnp.zeros((LANES - heads, state), f32)],
            axis=0,
        )
        whole = jnp.sum(whole.T, axis=0, keepdims=True)
        d_la = running_sum(change - columns + through - kept, True) + (
            jnp.sum(kept, axis=0, keepdims=True) + passing * whole
        )
        d_log = d_log + jnp.sum(d_la * (dt * rate), axis=0, keepdims=True)
        d_raw = (d_la * rate + sum_heads(dxd * x_wide, head_size)) * jax.nn.sigmoid(raw)
        d_raw = jnp.where(lane < heads, d_raw, 0.0)
        d_bias = d_bias + jnp.sum(d_raw, axis=0, keepdims=True)
        draw[at, :] = d_raw.astype(low)
        cot[...] = grad * rows_of_heads(passing, heads, head_size) + dot_tn(d_in, c)
        if index == steps - 2:
            scatter_br.middle()
            scatter_gb.middle()
    scatter_bc.start()

    def conv_back(cols, get):
        size = cols.stop - cols.start
        dz[0:8, cols] = jnp.zeros((8, size), f32)
        dz[8 + tokens :, cols] = jnp.zeros((8, size), f32)
        tap_sums = [jnp.zeros((1, size), f32) for _ in range(kernel + 1)]
        for index in range(steps):
            start = index * block
            key = key_ref[8 + start : 8 + start + block, :]
            total = jnp.broadcast_to(cw[kernel : kernel + 1, cols], (block, size))
            taps = []
            for offset in range(kernel):
                at = slice(8 - kernel + 1 + offset + start, 8 - kernel + 1 + offset + start + block)
                tap = pre_ref[at, cols]
                if offset < kernel - 1:
                    same = jnp.where(key_ref[at, :] == key, 1.0, 0.0)
                    tap = tap * jnp.concatenate([same] * (size // LANES), axis=1)
                taps.append(tap)
                total = total + cw[offset : offset + 1, cols] * tap
            sigm = jax.nn.sigmoid(total)
            change = get(index) * (sigm * (1.0 + total * (1.0 - sigm)))
            dz[8 + start : 8 + start + block, cols] = change
            for offset in range(kernel):
                tap_sums[offset] += jnp.sum(taps[offset] * change, axis=0, keepdims=True)
            tap_sums[kernel] += jnp.sum(change, axis=0, keepdims=True)
        for offset in range(kernel + 1):
            small[offset : offset + 1, cols] = tap_sums[offset]

    def back_rows(start, size, cols):
        span = cols.stop - cols.start
        key = key_ref[start : start + size, :]
        total = cw[kernel - 1 : kernel, cols] * dz[start : start + size, cols]
        for offset in range(kernel - 1):
            at = slice(start + kernel - 1 - offset, start + kernel - 1 - offset + size)
            same = jnp.where(key_ref[at, :] == key, 1.0, 0.0)
            total = total + cw[offset : offset + 1, cols] * (
                dz[at, cols] * jnp.concatenate([same] * (span // LANES), axis=1)
            )
        return total

    def halo(cols, out, arrived, slot):
        out[...] = back_rows(0, 8, cols)
        copy = remote(out, arrived, hs.at[slot], hr.at[slot], "dp", following)
        copy.start()
        return copy

    def finish_pre(cols, copy, arrived):
        for index in range(steps):
            start = index * block
            value = back_rows(8 + start, block, cols)
            if index == steps - 1:
                copy.wait()
                edge = value[block - 8 :, :] + arrived[...]
                value = jnp.concatenate([value[: block - 8], edge], axis=0)
            dpre[start : start + block, cols] = value.astype(low)

    cols = slice(0, inner)
    conv_back(cols, lambda index: dx[index * block : (index + 1) * block, :])
    copy = halo(cols, halo_out, halo_in, 0)
    scatter_bc.middle()
    finish_pre(cols, copy, halo_in)
    ga_part[...] = dot_tn(normed_ref[...], dpre[:, :inner]).astype(low)
    scatter_ga.start()
    dbc_all[own, :] = scatter_bc.finish().astype(low)
    gather_bc = Gather(model, dbc_all, rows, as_, ar_)
    gather_bc.start()
    for index in range(steps):
        at = slice(index * block, (index + 1) * block)
        part_sum = dot_nt(dgate_ref[at, :], wb_ref[:, :inner])
        part_sum = part_sum + dot_nt(dpre[at, :inner], wa_ref[:, :inner])
        part_sum = part_sum + dot_nt(draw[at, :], wdt_ref[...])
        rows_part[at, :] = part_sum.astype(low)
    scatter_rows.start()
    gather_bc.forward()
    gather_bc.finish()
    cols = slice(inner, wide)
    conv_back(cols, lambda index: dbc_all[index * block : (index + 1) * block, :].astype(f32))
    copy = halo(cols, halo_bc_out, halo_bc_in, 1)
    scatter_rows.middle()
    scatter_ga.middle()
    finish_pre(cols, copy, halo_bc_in)

    def pick_exact(value, one):
        return dot_wide(
            jnp.concatenate(split(value, 3), axis=1), jnp.concatenate([one] * 3, axis=0)
        )

    def picker(count, first, lane_at, many):
        down = lax.broadcasted_iota(jnp.int32, (count, LANES), 0)
        over = lax.broadcasted_iota(jnp.int32, (count, LANES), 1) - lane_at
        return ((down == over + first) & (over >= 0) & (over < many)).astype(f32).astype(low)

    side = (
        dot_wide(dpre[:, inner:], picker(bc, model.me * quarter, bc_lane, quarter))
        + dot_wide(draw[...], picker(LANES, 0, dt_lane, heads))
    ).astype(low)
    gs_part[...] = dot_tn(normed_ref[...], side).astype(low)
    scatter_gs.start()
    d_rows = scatter_rows.finish() + dot_nt(dpre[own, inner:], wa_ref[:, inner:wide])
    scatter_gs.middle()
    x = x_ref[...]
    rstd = lax.rsqrt(jnp.sum(x * x, axis=-1, keepdims=True) / mean_of + EPSILON)
    scaled = gain_ref[...][None, :] * d_rows
    small[kernel + 1 : kernel + 2, :width] = jnp.sum(d_rows * x * rstd, axis=0, keepdims=True)
    small[kernel + 2 : kernel + 3, :inner] = gsum_ref[0:1, :]
    d_heads = jnp.concatenate(
        [d_bias, d_log, sum_heads(gsum_ref[...], head_size, 3)[1:2, :], jnp.zeros((5, LANES), f32)],
        axis=0,
    )
    d_heads = pick_exact(d_heads, picker(LANES, 0, model.me * heads, heads))
    for index in range(3):
        small[kernel + 3 : kernel + 4, index * LANES : (index + 1) * LANES] = d_heads[
            index : index + 1, :
        ]

    def small_copy(hop):
        return remote(
            small, small_all.at[hop], ss.at[hop], sr.at[hop], "dp", lax.rem(data.me + hop, dp)
        )

    for hop in range(1, dp):
        small_copy(hop).start()
    packed[rows : 2 * rows, :width] = (
        cot_ref[...]
        + rstd * scaled
        - x * (rstd * rstd * rstd * (jnp.sum(scaled * x, axis=-1, keepdims=True) / mean_of))
    )
    packed[0:rows, :width] = x + scatter_br.finish()
    base = 2 * rows
    packed[base : base + part, : 2 * inner] = scatter_gb.finish()
    packed[base + part : base + 2 * part, :inner] = scatter_ga.finish()
    total = small[...]
    for hop in range(1, dp):
        small_copy(hop).wait_recv()
        total = total + small_all[hop]
    sums_own[...] = total

    def sums_copy(hop):
        return remote(
            sums_own, sums_ref.at[model.me], ts.at[hop], tr.at[hop], "tensor",
            lax.rem(model.me + hop, tensor),
        )

    for hop in range(1, tensor):
        sums_copy(hop).start()
    sums_ref[model.me] = total
    side_sum = scatter_gs.finish()
    packed[base + part : base + 2 * part, inner : inner + LANES] = pick_exact(
        side_sum, picker(LANES, dt_lane, 0, heads)
    )
    bc_own[...] = side_sum

    def bc_copy(hop):
        return remote(
            bc_own, gbc_ref.at[model.me], us.at[hop], ur.at[hop], "tensor",
            lax.rem(model.me + hop, tensor),
        )

    for hop in range(1, tensor):
        bc_copy(hop).start()
    gbc_ref[model.me] = side_sum
    for hop in range(1, tensor):
        sums_copy(hop).wait()
        bc_copy(hop).wait()
    for hop in range(1, dp):
        small_copy(hop).wait_send()
    for one in (scatter_bc, scatter_rows, scatter_ga, scatter_gs, scatter_br, scatter_gb, gather_bc):
        one.drain()
    for index in range(tensor):
        at = base + 2 * part + index * part
        packed[at : at + part, :LANES] = gbc_ref[index]
        at = base + (2 + tensor) * part + index * 8
        packed[at : at + 8, :] = sums_ref[index]


def block_kernel(dp, tensor, group, heads, kernel, mean_of, sequences, counts, *refs):
    sizes, parts, start = counts, [], 0
    for size in sizes:
        parts.append(refs[start : start + size])
        start += size
    ins, (packed,), kept, fscratch, bscratch = parts
    (
        x_ref, gain_ref, cot_ref, zx_ref, bcw_ref, dtt_ref, out_ref, seg_ref, cxw_ref, cxb_ref,
        cbw_ref, cbb_ref, bias_ref, log_ref, skip_ref, ggain_ref,
    ) = ins
    head_ref = fscratch[0]
    total = bias_ref.shape[0]
    rows = jnp.concatenate(
        [bias_ref[...][None, :], -jnp.exp(log_ref[...][None, :]), skip_ref[...][None, :],
         jnp.zeros((5, total), jnp.float32)],
        axis=0,
    )
    down = lax.broadcasted_iota(jnp.int32, (total, LANES), 0)
    over = lax.broadcasted_iota(jnp.int32, (total, LANES), 1)
    one = ((down == over + lax.axis_index("tensor") * heads) & (over < heads)).astype(
        jnp.float32
    ).astype(low)
    hi, mid, lo = split(rows, 3)
    head_ref[...] = dot_wide(hi, one) + dot_wide(mid, one) + dot_wide(lo, one)
    forward_part(
        dp, tensor, group, heads, mean_of, sequences,
        x_ref, gain_ref, cot_ref, zx_ref, bcw_ref, dtt_ref, out_ref, seg_ref, cxw_ref, cxb_ref,
        cbw_ref, cbb_ref, head_ref, ggain_ref, *kept, *fscratch[1:],
    )
    cw = fscratch[3]
    backward_part(
        dp, tensor, group, heads, kernel, mean_of, *kept, x_ref, gain_ref, cot_ref, cw, head_ref,
        packed, *bscratch,
    )


def finish_kernel(
    tensor, heads, kernel,
    packed,
    o_res, o_gin, o_norm, o_zx, o_bc, o_dt, o_cxw, o_cxb, o_cbw, o_cbb, o_dtb, o_log, o_skip,
    o_gate, o_out,
):
    part, inner = o_zx.shape[1:]
    rows, width = o_gin.shape
    base = 2 * rows
    bc = o_bc.shape[1]
    quarter = bc // tensor
    o_res[...] = packed[0:rows, :width]
    o_gin[...] = packed[rows : 2 * rows, :width]
    o_zx[0] = packed[base : base + part, :inner]
    o_zx[1] = packed[base + part : base + 2 * part, :inner]
    o_out[...] = packed[base : base + part, inner : 2 * inner]
    turned = jnp.concatenate(
        [
            packed[base + part : base + 2 * part, inner : inner + LANES],
            jnp.zeros((-part % LANES, LANES), jnp.float32),
        ],
        axis=0,
    ).T
    o_dt[...] = turned[: o_dt.shape[0], :part]
    base = base + 2 * part
    lane = lax.broadcasted_iota(jnp.int32, (part, LANES), 1)
    for start in range(0, bc, LANES):
        tile = jnp.zeros((part, LANES), jnp.float32)
        for one in range(tensor):
            if start <= one * quarter < start + LANES:
                at = one * quarter - start
                tile = jnp.where((lane >= at) & (lane < at + quarter), packed[base + one * part : base + (one + 1) * part, :LANES], tile)
        o_bc[:, start : start + LANES] = tile
    base = base + tensor * part
    sums = [packed[base + 8 * one : base + 8 * (one + 1), :] for one in range(tensor)]
    total = sums[0]
    for one in range(1, tensor):
        total = total + sums[one]
    o_norm[...] = total[kernel + 1, :width]
    o_cbw[...] = sums[0][0:kernel, inner : inner + bc]
    o_cbb[...] = sums[0][kernel, inner : inner + bc]
    for one in range(tensor):
        cols = slice(one * inner, (one + 1) * inner)
        o_cxw[:, cols] = sums[one][0:kernel, :inner]
        o_cxb[cols] = sums[one][kernel, :inner]
        o_gate[cols] = sums[one][kernel + 2, :inner]
    for index, out in enumerate((o_dtb, o_log, o_skip)):
        out[...] = total[kernel + 3, index * LANES : index * LANES + out.shape[0]]


def block_call(dp, tensor, group, heads, mean_of, sequences, *arrays):
    x, zx, bcw, cxw = arrays[0], arrays[3], arrays[4], arrays[8]
    rows, width = x.shape
    tokens, part, inner = rows * tensor, zx.shape[1], zx.shape[2]
    bc = bcw.shape[1]
    wide, state = inner + bc, bc // 2
    steps = tokens // min(GROUP, tokens)
    small = (8, -(-max(width, wide, 2 * inner, 3 * LANES) // LANES) * LANES)
    f32 = jnp.float32
    dma = pltpu.SemaphoreType.DMA
    kept = [
        pltpu.VMEM((tokens, width), low),
        pltpu.VMEM((tokens, width), low),
        pltpu.VMEM((dp * part, wide), low),
        pltpu.VMEM((dp * part, 2 * inner), low),
        pltpu.VMEM((dp * part, LANES), low),
        pltpu.VMEM((tokens + 8, wide), f32),
        pltpu.VMEM((tokens + 16, LANES), f32),
        pltpu.VMEM((tokens, wide), low),
        pltpu.VMEM((tokens, LANES), f32),
        pltpu.VMEM((tokens, LANES), f32),
        pltpu.VMEM((steps, inner, state), f32),
        pltpu.VMEM((tokens, inner), f32),
        pltpu.VMEM((tokens, inner), low),
        pltpu.VMEM((tokens, inner), low),
        pltpu.VMEM((inner + 16, state), low),
        pltpu.VMEM((8, inner), f32),
    ]
    forward_scratch = [
        pltpu.VMEM((8, LANES), f32),
        pltpu.VMEM((8, wide), f32),
        pltpu.VMEM((dp * 16, LANES), low),
        pltpu.VMEM((8, wide), f32),
        pltpu.VMEM((tokens, inner), f32),
        pltpu.VMEM((tokens, inner), f32),
        pltpu.VMEM((tokens, inner), f32),
        pltpu.VMEM((inner + 16, state), low),
        pltpu.VMEM((group, inner + 16, state), low),
        pltpu.VMEM((inner, state), f32),
        pltpu.VMEM((8 * steps, LANES), f32),
        pltpu.VMEM((8, tokens), f32),
        pltpu.VMEM((tensor, 8, tokens), f32),
        *[dma((2 * n,)) for n in (dp, dp, dp, dp, dp, dp, tensor, tensor, tensor, tensor)],
        dma((2,)), dma((2,)),
        dma((group,)), dma((group,)),
        dma((tensor,)), dma((tensor,)),
    ]
    backward_scratch = [
        pltpu.VMEM((tokens, inner), f32),
        pltpu.VMEM((tokens, bc), low),
        pltpu.VMEM((tokens, LANES), low),
        pltpu.VMEM((tokens + 16, wide), f32),
        pltpu.VMEM((tokens, wide), low),
        pltpu.VMEM((tokens, bc), low),
        pltpu.VMEM((tokens, width), low),
        pltpu.VMEM((dp * part, 2 * inner), low),
        pltpu.VMEM((tokens, width), low),
        pltpu.VMEM((dp * part, inner), low),
        pltpu.VMEM((dp * part, LANES), low),
        pltpu.VMEM((8, inner), f32),
        pltpu.VMEM((8, inner), f32),
        pltpu.VMEM((8, bc), f32),
        pltpu.VMEM((8, bc), f32),
        pltpu.VMEM((inner, state), f32),
        pltpu.VMEM((group, inner + 16, state), low),
        pltpu.VMEM(small, f32),
        pltpu.VMEM((dp,) + small, f32),
        pltpu.VMEM(small, f32),
        pltpu.VMEM((part, LANES), f32),
        pltpu.VMEM((tensor, part, LANES), f32),
        pltpu.VMEM((tensor,) + small, f32),
        *Scatter.scratch(tensor, rows, bc),
        *Scatter.scratch(tensor, rows, width),
        *Scatter.scratch(tensor, rows, width),
        *Scatter.scratch(dp, part, inner),
        *Scatter.scratch(dp, part, 2 * inner),
        *Scatter.scratch(dp, part, LANES),
        dma((2 * tensor,)), dma((2 * tensor,)),
        dma((2,)), dma((2,)),
        dma((dp,)), dma((dp,)),
        dma((tensor,)), dma((tensor,)),
        dma((tensor,)), dma((tensor,)),
        dma((group,)), dma((group,)),
    ]
    counts = (len(arrays), 1, len(kept), len(forward_scratch), len(backward_scratch))
    lines = 2 * rows + (2 + tensor) * part + 8 * tensor
    return pl.pallas_call(
        functools.partial(
            block_kernel, dp, tensor, group, heads, cxw.shape[0], mean_of, sequences, counts
        ),
        out_shape=jax.ShapeDtypeStruct((lines, small[1]), f32),
        in_specs=vmem(len(arrays)),
        out_specs=vmem(1)[0],
        scratch_shapes=kept + forward_scratch + backward_scratch,
        compiler_params=pltpu.CompilerParams(
            collective_id=0, has_side_effects=True, vmem_limit_bytes=63 * 2**20
        ),
        name="block",
    )(*arrays)


def finish_call(tensor, heads, kernel, rows, width, part, inner, heads_total, bc, packed):
    inner_total = inner * tensor
    outs = (
        (rows, width), (rows, width), (width,), (2, part, inner), (part, bc), (heads, part),
        (kernel, inner_total), (inner_total,), (kernel, bc), (bc,), (heads_total,),
        (heads_total,), (heads_total,), (inner_total,), (part, inner),
    )
    return pl.pallas_call(
        functools.partial(finish_kernel, tensor, heads, kernel),
        out_shape=tuple(jax.ShapeDtypeStruct(one, jnp.float32) for one in outs),
        in_specs=vmem(1),
        out_specs=tuple(vmem(len(outs))),
        compiler_params=pltpu.CompilerParams(vmem_limit_bytes=32 * 2**20),
        name="finish",
    )(packed)


def pad_to(array, size, axis):
    widths = [(0, 0)] * array.ndim
    widths[axis] = (0, size - array.shape[axis])
    return jnp.pad(array, widths)


def per_device(
    block_input,
    norm_gain,
    zx_weight,
    bc_weight,
    dt_weight,
    conv_x_weight,
    conv_x_bias,
    conv_bc_weight,
    conv_bc_bias,
    dt_bias,
    decay_log,
    skip_gain,
    gate_gain,
    out_weight,
    segments,
    cotangent,
):
    tensor_count = lax.axis_size("tensor")
    data_count = lax.axis_size("dp")
    token_count = segments.shape[0]
    row_count, width = block_input.shape
    part = zx_weight.shape[1]
    heads_here = dt_weight.shape[1]
    heads_total = dt_bias.shape[0]
    taps = conv_x_weight.shape[0]
    bc_size = bc_weight.shape[1]
    padded = -(-part // 16) * 16
    columns = data_count * padded

    def widen(array):
        if padded == part:
            return array
        lead = array.shape[:-1]
        return pad_to(array.reshape(lead + (data_count, part)), padded, -1).reshape(lead + (columns,))

    def narrow(array):
        if padded == part:
            return array
        lead = array.shape[:-1]
        return array.reshape(lead + (data_count, padded))[..., :part].reshape(lead + (width,))

    group = max(1, LENGTH // token_count)
    if data_count % group:
        group = data_count
    sequences = data_count * token_count // LENGTH + 1
    packed = block_call(
        data_count, tensor_count, group, heads_here, width, sequences,
        widen(block_input), widen(norm_gain), widen(cotangent), pad_to(zx_weight, padded, 1),
        pad_to(bc_weight, padded, 0), dt_weight.T, pad_to(out_weight.T, padded, 0), segments,
        conv_x_weight, conv_x_bias, conv_bc_weight, conv_bc_bias, dt_bias, decay_log, skip_gain,
        gate_gain,
    )
    outs = list(
        finish_call(
            tensor_count, heads_here, taps, row_count, columns, padded, zx_weight.shape[2],
            heads_total, bc_size, packed,
        )
    )
    for index in (0, 1, 2):
        outs[index] = narrow(outs[index])
    if padded != part:
        outs[3] = outs[3][:, :part]
        outs[4], outs[5], outs[14] = outs[4][:part], outs[5][:, :part], outs[14][:part]
    outs[5], outs[14] = outs[5].T, outs[14].T
    return tuple(outs)


def solution(mesh):
    in_specs = (
        P(("dp", "tensor"), None),
        P(),
        P(None, "dp", "tensor"),
        P("dp", None),
        P("dp", "tensor"),
        P(),
        P(),
        P(),
        P(),
        P(),
        P(),
        P(),
        P(),
        P("tensor", "dp"),
        P("dp"),
        P(("dp", "tensor"), None),
    )
    out_specs = (
        P(("dp", "tensor"), None),
        P(("dp", "tensor"), None),
        P(),
        P(None, "dp", "tensor"),
        P("dp", None),
        P("dp", "tensor"),
        P(),
        P(),
        P(),
        P(),
        P(),
        P(),
        P(),
        P(),
        P("tensor", "dp"),
    )
    return jax.shard_map(
        per_device, mesh=mesh, in_specs=in_specs, out_specs=out_specs, check_vma=False
    )
```

```python
import functools
import jax
import jax.numpy as jnp
from jax import lax
from jax.experimental import pallas as pl
from jax.experimental.pallas import tpu as pltpu
from jax.sharding import PartitionSpec as P

GROUP = 256
LENGTH = 4096
EPSILON = 1e-05
PAD = 8
LANES = 128
MESH = pl.DeviceIdType.MESH
low = jnp.bfloat16


def dot_wide(left, right):
    return jnp.dot(left, right, preferred_element_type=jnp.float32)


def dot_nt(left, right):
    return lax.dot_general(left, right, (((1,), (1,)), ((), ())), preferred_element_type=jnp.float32)


def dot_tn(left, right):
    return lax.dot_general(left, right, (((0,), (0,)), ((), ())), preferred_element_type=jnp.float32)


def head_decay(same, cum, cumt, head):
    spread = jnp.where(same, cum[:, head : head + 1] - cumt[head : head + 1, :], -1e30)
    return jnp.exp(spread)


def vmem(count):
    return [pl.BlockSpec(memory_space=pltpu.VMEM)] * count


class Grid2:
    def __init__(self, axis, count):
        self.axis, self.count = axis, count
        self.inner = 2 if count % 2 == 0 else 1
        self.outer = count // self.inner
        self.me = lax.axis_index(axis)
        self.mi = lax.rem(self.me, self.inner)
        self.mo = self.me // self.inner

    def at(self, hop, inner):
        return lax.rem(self.mo + hop + self.outer, self.outer) * self.inner + inner

    @property
    def partner(self):
        return self.mo * self.inner + (self.inner - 1 - self.mi)


def remote(src, dst, send, recv, axis, index):
    return pltpu.make_async_remote_copy(
        src_ref=src, dst_ref=dst, send_sem=send, recv_sem=recv,
        device_id={axis: index}, device_id_type=MESH,
    )


def greet(*axes):
    barrier = pltpu.get_barrier_semaphore()
    total = 0
    for axis, count in axes:
        me = lax.axis_index(axis)
        for hop in range(1, count):
            pl.semaphore_signal(
                barrier, inc=1, device_id={axis: lax.rem(me + hop, count)}, device_id_type=MESH
            )
            total += 1
    if total:
        pl.semaphore_wait(barrier, total)


class Gather:
    def __init__(self, grid, ref, rows, send, recv):
        self.grid, self.ref, self.rows, self.send, self.recv = grid, ref, rows, send, recv
        self.todo = list(range(1, grid.outer))

    def copy(self, outer, inner, slot, target_outer, target_inner):
        g = self.grid
        index = outer * g.inner + inner
        piece = self.ref.at[pl.ds(pl.multiple_of(index * self.rows, self.rows), self.rows), :]
        return remote(
            piece, piece, self.send.at[slot], self.recv.at[slot], g.axis,
            target_outer * g.inner + target_inner,
        )

    def along(self, way, step):
        g = self.grid
        slot = step if way > 0 else g.outer - 1 + step
        return self.copy(g.mo - way * (step - 1), g.mi, slot, g.mo + way, g.mi)

    def over(self, way, step, inner):
        g = self.grid
        slot = 2 * g.outer - 2 + step + (0 if way > 0 else g.outer - 1)
        return self.copy(g.mo - way * step, inner, slot, g.mo, g.inner - 1 - g.mi)

    def has(self, way, step):
        g = self.grid
        return g.mo - step >= 0 if way > 0 else g.mo + step < g.outer

    def leads(self, way):
        return self.has(-way, 1)

    def start(self):
        g = self.grid
        if g.outer > 1:
            for way in (1, -1):
                pl.when(self.leads(way))(lambda way=way: self.along(way, 1).start())
        if g.inner > 1:
            self.copy(g.mo, g.mi, 0, g.mo, g.inner - 1 - g.mi).start()

    def step(self):
        g = self.grid
        if not self.todo:
            return
        step = self.todo.pop(0)
        for way in (1, -1):

            @pl.when(self.has(way, step))
            def _(way=way):
                slot = step if way > 0 else g.outer - 1 + step
                self.copy(g.mo - way * step, g.mi, slot, g.mo, g.mi).wait_recv()
                if step + 1 < g.outer:
                    pl.when(self.leads(way))(lambda: self.along(way, step + 1).start())
                if g.inner > 1:
                    self.over(way, step, g.mi).start()

    def finish(self):
        g = self.grid
        while self.todo:
            self.step()
        if g.inner > 1:
            self.copy(g.mo, g.inner - 1 - g.mi, 0, g.mo, g.mi).wait_recv()
            for step in range(1, g.outer):
                for way in (1, -1):
                    pl.when(self.has(way, step))(
                        lambda way=way: self.over(way, step, g.inner - 1 - g.mi).wait_recv()
                    )

    def drain(self):
        g = self.grid
        if g.inner > 1:
            self.copy(g.mo, g.mi, 0, g.mo, g.inner - 1 - g.mi).wait_send()
        for step in range(1, g.outer):
            for way in (1, -1):
                there = self.has(way, step - 1) if step > 1 else True
                pl.when(jnp.logical_and(self.leads(way), there))(
                    lambda way=way: self.along(way, step).wait_send()
                )
                if g.inner > 1:
                    pl.when(self.has(way, step))(
                        lambda way=way: self.over(way, step, g.mi).wait_send()
                    )


class Scatter:
    def __init__(self, grid, src, first, second, landed, rows, send, recv):
        self.grid, self.src, self.rows, self.send, self.recv = grid, src, rows, send, recv
        self.first, self.second, self.landed = first, second, landed

    @staticmethod
    def scratch(count, rows, width):
        outer = count // (2 if count % 2 == 0 else 1)
        return [
            pltpu.VMEM((outer, rows, width), low),
            pltpu.VMEM((outer, rows, width), low),
            pltpu.VMEM((outer, rows, width), low),
            pltpu.SemaphoreType.DMA((2 * outer,)),
            pltpu.SemaphoreType.DMA((2 * outer,)),
        ]

    def block(self, index):
        return self.src.at[pl.ds(pl.multiple_of(index * self.rows, self.rows), self.rows), :]

    def over(self, hop):
        g = self.grid
        return remote(
            self.block(g.at(hop, g.inner - 1 - g.mi)), self.first.at[hop],
            self.send.at[hop], self.recv.at[hop], g.axis, g.partner,
        )

    def along(self, hop):
        g = self.grid
        slot = g.outer + hop
        return remote(
            self.second.at[hop], self.landed.at[hop],
            self.send.at[slot], self.recv.at[slot], g.axis, g.at(hop, g.mi),
        )

    def start(self):
        if self.grid.inner > 1:
            for hop in list(range(1, self.grid.outer)) + [0]:
                self.over(hop).start()

    def pair(self, hop):
        g = self.grid
        total = self.block(g.at(hop, g.mi))[...].astype(jnp.float32)
        if g.inner > 1:
            self.over(hop).wait_recv()
            total = total + self.first[hop].astype(jnp.float32)
        return total

    def middle(self):
        for hop in range(1, self.grid.outer):
            self.second[hop] = self.pair(hop).astype(low)
            self.along(hop).start()

    def finish(self):
        g = self.grid
        total = self.pair(0)
        for hop in range(1, g.outer):
            self.along(hop).wait_recv()
            total = total + self.landed[hop].astype(jnp.float32)
        return total

    def drain(self):
        g = self.grid
        for hop in range(g.outer):
            if g.inner > 1:
                self.over(hop).wait_send()
            if hop:
                self.along(hop).wait_send()


def split(value, pieces):
    out = []
    for _ in range(pieces):
        piece = value.astype(low)
        out.append(piece)
        value = value - piece.astype(jnp.float32)
    return out


def spread_heads(value, head_size, inner, pieces=2):
    one = (
        lax.broadcasted_iota(jnp.int32, (LANES, inner), 1) // head_size
        == lax.broadcasted_iota(jnp.int32, (LANES, inner), 0)
    ).astype(jnp.float32).astype(low)
    return dot_wide(
        jnp.concatenate(split(value, pieces), axis=1), jnp.concatenate([one] * pieces, axis=0)
    )


def sum_heads(value, head_size, pieces=2):
    inner = value.shape[1]
    one = (
        lax.broadcasted_iota(jnp.int32, (inner, LANES), 0) // head_size
        == lax.broadcasted_iota(jnp.int32, (inner, LANES), 1)
    ).astype(jnp.float32).astype(low)
    return dot_wide(
        jnp.concatenate(split(value, pieces), axis=1), jnp.concatenate([one] * pieces, axis=0)
    )


def running_sum(value, reverse=False):
    size = value.shape[0]
    row = lax.broadcasted_iota(jnp.int32, (size, size), 0)
    col = lax.broadcasted_iota(jnp.int32, (size, size), 1)
    keep = (row <= col) if reverse else (row >= col)
    keep = keep.astype(jnp.float32).astype(low)
    pieces = split(value, 3)
    total = dot_wide(keep, jnp.concatenate(pieces, axis=1))
    width = value.shape[1]
    return total[:, :width] + total[:, width : 2 * width] + total[:, 2 * width :]


def rows_of_heads(row, heads, head_size):
    turned = jnp.broadcast_to(row, (LANES, LANES)).T
    return jnp.concatenate(
        [jnp.broadcast_to(turned[h : h + 1, :], (head_size, LANES)) for h in range(heads)], axis=0
    )


def softplus(value):
    return jnp.maximum(value, 0.0) + jnp.log1p(jnp.exp(-jnp.abs(value)))


def block_parts(cum, key, before):
    size = cum.shape[0]
    last_key, last = key[size - 1 :, :], cum[size - 1 :, :]
    inflow = jnp.where(key == before, jnp.exp(cum), 0.0)
    tail = jnp.where(key == last_key, jnp.exp(last - cum), 0.0)
    passing = jnp.where(last_key == before, jnp.exp(last), 0.0)
    return inflow, tail, passing


def forward_part(
    dp, tensor, group, heads, mean_of, sequences,
    x_ref, gain_ref, cot_ref, zx_ref, bcw_ref, dtt_ref, out_ref, seg_ref, cxw_ref, cxb_ref, cbw_ref,
    cbb_ref, head_ref, ggain_ref,
    normed_ref, cotl_ref, wa_ref, wb_ref, wdt_ref, pre_ref, key_ref, act_ref, raw_ref, cum_ref,
    states_ref, dmix_ref, dgate_ref, nout_ref, scot_ref, gsum_ref,
    tail, dtall, cw, y, gate, dno, sent, got, ends, decays, sums, sums_all,
    sa, ra, sb, rb, sd, rd, sn, rn, sc, rc, sh, rh, sl, rl, ss, rs,
):
    rows, width = x_ref.shape
    tokens = normed_ref.shape[0]
    part, inner = zx_ref.shape[1], zx_ref.shape[2]
    bc = bcw_ref.shape[1]
    wide, state = inner + bc, bc // 2
    head_size = inner // heads
    kernel = cxw_ref.shape[0]
    block = min(GROUP, tokens)
    steps = tokens // block
    f32 = jnp.float32
    data, model = Grid2("dp", dp), Grid2("tensor", tensor)
    mine = pl.ds(pl.multiple_of(data.me * part, part), part)
    own = pl.ds(pl.multiple_of(model.me * rows, rows), rows)
    units = pl.ds(pl.multiple_of(model.me * inner, LANES), inner)

    wa_ref[mine, :inner] = zx_ref[1]
    wa_ref[mine, inner:] = bcw_ref[...]
    wb_ref[mine, :inner] = zx_ref[0]
    wb_ref[mine, inner:] = out_ref[...]
    flat = dtt_ref[...].astype(f32)
    flat = jnp.concatenate([flat, jnp.zeros((heads, LANES - flat.shape[1]), f32)], axis=1)
    flat = jnp.concatenate([flat, jnp.zeros((16 - heads, LANES), f32)], axis=0)
    dtall[pl.ds(pl.multiple_of(data.me * 16, 16), 16), :] = flat.astype(low)
    x = x_ref[...]
    rstd = lax.rsqrt(jnp.sum(x * x, axis=-1, keepdims=True) / mean_of + EPSILON)
    normed_ref[own, :] = (x * rstd * gain_ref[...][None, :]).astype(low)
    cotl_ref[own, :] = cot_ref[...].astype(low)
    for index in range(steps):
        at = slice(index * block, (index + 1) * block)
        line = seg_ref[at][None, :].astype(f32)
        key_ref[8 + index * block : 8 + (index + 1) * block, :] = jnp.broadcast_to(
            line, (LANES, block)
        ).T
    key_ref[8 + tokens :, :] = jnp.zeros((8, LANES), f32)
    greet(("dp", dp), ("tensor", tensor))
    wa = Gather(data, wa_ref, part, sa, ra)
    wb = Gather(data, wb_ref, part, sb, rb)
    wd = Gather(data, dtall, 16, sd, rd)
    nm = Gather(model, normed_ref, rows, sn, rn)
    ct = Gather(model, cotl_ref, rows, sc, rc)
    following = lax.rem(data.me + 1, dp)
    seg_copy = remote(
        key_ref.at[pl.ds(tokens, 8), :], key_ref.at[pl.ds(0, 8), :], sh.at[0], rh.at[0], "dp",
        following,
    )
    pre_copy = remote(
        tail, pre_ref.at[pl.ds(0, 8), :], sh.at[1], rh.at[1], "dp", following
    )
    wd.start()
    wa.start()
    nm.start()
    seg_copy.start()
    for step in range(1, data.outer):
        wd.step()
        wa.step()
        if step == min(2, data.outer - 1):
            nm.step()
            ct.start()
    wb.start()
    cw[0:kernel, :inner] = cxw_ref[:, units]
    cw[0:kernel, inner:] = cbw_ref[...]
    cw[kernel : kernel + 1, :inner] = cxb_ref[units][None, :]
    cw[kernel : kernel + 1, inner:] = cbb_ref[...][None, :]
    wd.finish()
    turn = (
        lax.broadcasted_iota(jnp.int32, (part, LANES), 0)
        == lax.broadcasted_iota(jnp.int32, (part, LANES), 1)
    ).astype(f32).astype(low)
    for index in range(dp):
        shard = jnp.concatenate(
            [dtall[index * 16 : (index + 1) * 16, :], jnp.zeros((LANES - 16, LANES), low)], axis=0
        )
        wdt_ref[index * part : (index + 1) * part, :] = dot_nt(turn, shard).astype(low)
    nm.finish()
    wa.finish()
    last = steps - 1
    bias, rate = head_ref[0:1, :], head_ref[1:2, :]
    for index in [last] + list(range(last)):
        at = slice(index * block, (index + 1) * block)
        first = dot_wide(normed_ref[at, :], wa_ref[...])
        pre_ref[8 + index * block : 8 + (index + 1) * block, :] = first.astype(low).astype(f32)
        if index == last:
            tail[...] = pre_ref[tokens : tokens + 8, :]
            pre_copy.start()
        raw_ref[at, :] = dot_wide(normed_ref[at, :], wdt_ref[...]) + bias
    wb.step()
    seg_copy.wait()
    pos = lax.broadcasted_iota(jnp.int32, (tokens + 16, LANES), 0) + (data.me * tokens - 8 + LENGTH)
    key_ref[...] = key_ref[...] * sequences + (pos // LENGTH).astype(f32)
    ends[...] = jnp.zeros_like(ends)
    total_cum = jnp.zeros((1, LANES), f32)
    first_before = key_ref[7:8, :]
    before = first_before
    pre_copy.wait()
    for index in range(steps):
        start = index * block
        at = slice(start, start + block)
        key = key_ref[8 + start : 8 + start + block, :]
        total = jnp.broadcast_to(cw[kernel : kernel + 1, :], (block, wide))
        for offset in range(kernel):
            shift = slice(8 - kernel + 1 + offset + start, 8 - kernel + 1 + offset + start + block)
            tap = cw[offset : offset + 1, :] * pre_ref[shift, :]
            if offset < kernel - 1:
                same = jnp.where(key_ref[shift, :] == key, 1.0, 0.0)
                tap = tap * jnp.concatenate([same] * (wide // LANES), axis=1)
            total = total + tap
        act_ref[at, :] = (total * jax.nn.sigmoid(total)).astype(low)
        dt = softplus(raw_ref[at, :])
        cum = running_sum(dt * rate)
        cum_ref[at, :] = cum
        inflow, tail_w, passing = block_parts(cum, key, before)
        pushed = (
            act_ref[at, :inner].astype(f32) * spread_heads(tail_w * dt, head_size, inner)
        ).astype(low)
        states_ref[index] = ends[...]
        reach = jnp.where(before == first_before, jnp.exp(total_cum), 0.0)
        decays[index * 8 : index * 8 + 1, :] = reach
        ends[...] = ends[...] * rows_of_heads(passing, heads, head_size) + dot_tn(
            pushed, act_ref[at, inner : inner + state]
        )
        total_cum = total_cum + cum[block - 1 :, :]
        before = key[block - 1 :, :]
        if index == 0:
            ct.step()
        if index % 2 == 1:
            wb.step()
    reach = jnp.where(before == first_before, jnp.exp(total_cum), 0.0)
    turned = jnp.broadcast_to(reach, (LANES, LANES)).T[:8, :]
    hi, lo = split(turned, 2)
    sent[0:inner, :] = ends[...].astype(low)
    sent[inner : inner + 16, :] = jnp.concatenate([hi, lo], axis=0)
    line_start = (data.me // group) * group
    place = lax.rem(data.me, group)

    def line_copy(hop):
        return remote(
            sent, got.at[place], sl.at[hop], rl.at[hop], "dp",
            line_start + lax.rem(place + hop, group),
        )

    for hop in range(1, group):
        line_copy(hop).start()
    got[place] = sent[...]
    row_i = lax.broadcasted_iota(jnp.int32, (block, block), 0)
    col_i = lax.broadcasted_iota(jnp.int32, (block, block), 1)
    for index in range(steps):
        start = index * block
        at = slice(start, start + block)
        key = key_ref[8 + start : 8 + start + block, :]
        keyt = key.T
        same = (row_i >= col_i) & (
            jnp.concatenate([key] * (block // LANES), axis=1) == keyt[0:1, :]
        )
        cum = cum_ref[at, :]
        cumt = cum.T
        dtt = softplus(raw_ref[at, :]).T
        x = act_ref[at, :inner]
        scores = dot_nt(act_ref[at, inner + state :], act_ref[at, inner : inner + state])
        for head in range(heads):
            cols = slice(head * head_size, (head + 1) * head_size)
            mixing = (
                scores * head_decay(same, cum, cumt, head) * dtt[head : head + 1, :]
            ).astype(low)
            y[at, cols] = dot_wide(mixing, x[:, cols])
        wb.step()
    ct.finish()
    wb.finish()
    for index in range(steps):
        at = slice(index * block, (index + 1) * block)
        gate[at, :] = dot_wide(normed_ref[at, :], wb_ref[:, :inner])
        dno[at, :] = dot_wide(cotl_ref[at, :], wb_ref[:, inner:])
    for hop in range(1, group):
        line_copy(hop).wait()
    entry = jnp.zeros((inner, state), f32)
    for index in range(group - 1):
        factor = got[index, inner : inner + 8, :].astype(f32) + got[index, inner + 8 :, :].astype(f32)
        factor = jnp.concatenate(
            [jnp.broadcast_to(factor[h : h + 1, :], (head_size, LANES)) for h in range(heads)], axis=0
        )
        longer = entry * factor + got[index, :inner, :].astype(f32)
        entry = jnp.where(index < place, longer, entry)
    skip = spread_heads(head_ref[0:8, :], head_size, inner, 3)[2:3, :]
    ggain = ggain_ref[units][None, :]
    before = first_before
    for index in range(steps):
        start = index * block
        at = slice(start, start + block)
        full = states_ref[index] + entry * rows_of_heads(
            decays[index * 8 : index * 8 + 1, :], heads, head_size
        )
        states_ref[index] = full
        key = key_ref[8 + start : 8 + start + block, :]
        inflow = jnp.where(key == before, jnp.exp(cum_ref[at, :]), 0.0)
        before = key[block - 1 :, :]
        mixed = (
            y[at, :]
            + dot_nt(act_ref[at, inner + state :], full.astype(low))
            * spread_heads(inflow, head_size, inner)
            + skip * act_ref[at, :inner].astype(f32)
        )
        y[at, :] = mixed
        gate_in = gate[at, :]
        gated = mixed * (gate_in * jax.nn.sigmoid(gate_in))
        squares = jnp.sum(gated * gated, axis=1, keepdims=True)
        dots = jnp.sum(gated * (ggain * dno[at, :]), axis=1, keepdims=True)
        lane = lax.broadcasted_iota(jnp.int32, (block, LANES), 1)
        both = jnp.where(lane == 0, squares, jnp.where(lane == 1, dots, 0.0))
        sums[:, at] = both.T[:8, :]

    def sums_copy(hop):
        return remote(
            sums, sums_all.at[hop], ss.at[hop], rs.at[hop], "tensor",
            lax.rem(model.me + hop, tensor),
        )

    for hop in range(1, tensor):
        sums_copy(hop).start()
    for hop in range(1, tensor):
        sums_copy(hop).wait_recv()
    before = first_before
    to_exit = jnp.zeros((1, LANES), f32)
    scot = jnp.zeros((inner, state), f32)
    g_gate = jnp.zeros((1, inner), f32)
    g_skip = jnp.zeros((1, inner), f32)
    total_cum = jnp.zeros((1, LANES), f32)
    for index in range(steps):
        start = index * block
        at = slice(start, start + block)
        total = sums[:, at]
        for hop in range(1, tensor):
            total = total + sums_all[hop, :, at]
        total = total / (inner * tensor)
        turned = jnp.concatenate([total, jnp.zeros((LANES - 8, block), f32)], axis=0).T
        rstd_gate = lax.rsqrt(turned[:, 0:1] + EPSILON)
        gate_dots = turned[:, 1:2]
        gate_in, mixed, d_out = gate[at, :], y[at, :], dno[at, :]
        sigm = jax.nn.sigmoid(gate_in)
        gate_act = gate_in * sigm
        gated = mixed * gate_act
        gated_normed = gated * rstd_gate
        nout_ref[at, :] = (gated_normed * ggain).astype(low)
        g_gate += jnp.sum(d_out * gated_normed, axis=0, keepdims=True)
        d_gated = rstd_gate * (ggain * d_out) - gated * (rstd_gate * rstd_gate * rstd_gate * gate_dots)
        d_mixed = d_gated * gate_act
        dmix_ref[at, :] = d_mixed
        dgate_ref[at, :] = (
            d_gated * mixed * sigm * (1.0 + gate_in * (1.0 - sigm))
        ).astype(low)
        g_skip += jnp.sum(d_mixed * act_ref[at, :inner].astype(f32), axis=0, keepdims=True)
        key = key_ref[8 + start : 8 + start + block, :]
        cum = cum_ref[at, :]
        reach = jnp.where(key == first_before, jnp.exp(cum + total_cum), 0.0)
        total_cum = total_cum + cum[block - 1 :, :]
        scot += dot_tn(
            (d_mixed * spread_heads(reach, head_size, inner)).astype(low),
            act_ref[at, inner + state :],
        )
    scot_ref[0:inner, :] = scot.astype(low)
    scot_ref[inner:, :] = sent[inner:, :]
    gsum_ref[...] = jnp.concatenate([g_gate, g_skip, jnp.zeros((6, inner), f32)], axis=0)
    for hop in range(1, tensor):
        sums_copy(hop).wait_send()
    for one in (wa, wb, wd, nm, ct):
        one.drain()


def backward_part(
    dp, tensor, group, heads, kernel, mean_of,
    normed_ref, cotl_ref, wa_ref, wb_ref, wdt_ref, pre_ref, key_ref, act_ref, raw_ref, cum_ref,
    states_ref, dmix_ref, dgate_ref, nout_ref, scot_ref, gsum_ref,
    x_ref, gain_ref, cot_ref, cw, head_ref,
    packed,
    dx, dbc, draw, dz, dpre, dbc_all, branch_part, gb_part, rows_part, ga_part, gs_part,
    halo_out, halo_in, halo_bc_out, halo_bc_in, cot, got, small, small_all, sums_own, bc_own, gbc_ref, sums_ref,
    b1, b2, b3, bs, br, r1, r2, r3, rs, rr, q1, q2, q3, qs, qr, g1, g2, g3, gs, gr,
    h1, h2, h3, hs_, hr_, k1, k2, k3, ks, kr,
    as_, ar_, hs, hr, ss, sr, ts, tr, us, ur, sl, rl,
):
    tokens = normed_ref.shape[0]
    wide = act_ref.shape[1]
    inner = dmix_ref.shape[1]
    bc = wide - inner
    state = bc // 2
    head_size = inner // heads
    rows, width = x_ref.shape
    part = wa_ref.shape[0] // dp
    data, model = Grid2("dp", dp), Grid2("tensor", tensor)
    block = min(GROUP, tokens)
    steps = tokens // block
    following = lax.rem(data.me + dp - 1, dp)
    f32 = jnp.float32
    own = pl.ds(pl.multiple_of(model.me * rows, rows), rows)
    quarter = bc // tensor
    bc_lane = lax.rem(model.me * quarter, LANES)
    dt_lane = lax.rem(bc_lane + quarter, LANES)

    line_start = (data.me // group) * group
    place = lax.rem(data.me, group)

    def line_copy(hop):
        return remote(
            scot_ref, got.at[place], sl.at[hop], rl.at[hop], "dp",
            line_start + lax.rem(place + hop, group),
        )

    for hop in range(1, group):
        line_copy(hop).start()
    scatter_br = Scatter(model, branch_part, q1, q2, q3, rows, qs, qr)
    scatter_gb = Scatter(data, gb_part, h1, h2, h3, part, hs_, hr_)
    scatter_bc = Scatter(model, dbc, b1, b2, b3, rows, bs, br)
    scatter_rows = Scatter(model, rows_part, r1, r2, r3, rows, rs, rr)
    scatter_ga = Scatter(data, ga_part, g1, g2, g3, part, gs, gr)
    scatter_gs = Scatter(data, gs_part, k1, k2, k3, part, ks, kr)
    gb_part[:, :inner] = dot_tn(normed_ref[...], dgate_ref[...]).astype(low)
    gb_part[:, inner:] = dot_tn(cotl_ref[...], nout_ref[...]).astype(low)
    scatter_gb.start()
    for index in range(steps):
        at = slice(index * block, (index + 1) * block)
        branch_part[at, :] = dot_nt(nout_ref[at, :], wb_ref[:, inner:]).astype(low)
    scatter_br.start()
    got[place] = scot_ref[...]
    small[...] = jnp.zeros_like(small)
    for hop in range(1, group):
        line_copy(hop).wait()
    leave = jnp.zeros((inner, state), f32)
    for index in range(group - 1, 0, -1):
        factor = got[index, inner : inner + 8, :].astype(f32) + got[index, inner + 8 :, :].astype(f32)
        factor = jnp.concatenate(
            [jnp.broadcast_to(factor[h : h + 1, :], (head_size, LANES)) for h in range(heads)], axis=0
        )
        longer = leave * factor + got[index, :inner, :].astype(f32)
        leave = jnp.where(index > place, longer, leave)
    cot[...] = leave
    rate = head_ref[1:2, :]
    skip = spread_heads(head_ref[0:8, :], head_size, inner, 3)[2:3, :]
    row_i = lax.broadcasted_iota(jnp.int32, (block, block), 0)
    col_i = lax.broadcasted_iota(jnp.int32, (block, block), 1)
    lane = lax.broadcasted_iota(jnp.int32, (block, LANES), 1)
    d_bias = jnp.zeros((1, LANES), f32)
    d_log = jnp.zeros((1, LANES), f32)
    for index in range(steps - 1, -1, -1):
        start = index * block
        at = slice(start, start + block)
        key = key_ref[8 + start : 8 + start + block, :]
        keyt = key.T
        equal = jnp.concatenate([key] * (block // LANES), axis=1) == keyt[0:1, :]
        same, strict = equal & (row_i >= col_i), row_i > col_i
        cum = cum_ref[at, :]
        cumt = cum.T
        raw = raw_ref[at, :]
        dt = softplus(raw)
        dtt = dt.T
        inflow, tail, passing = block_parts(cum, key, key_ref[7 + start : 8 + start, :])
        x, b, c = act_ref[at, :inner], act_ref[at, inner : inner + state], act_ref[at, inner + state :]
        x_wide = x.astype(f32)
        dy = dmix_ref[at, :]
        dy_low = dy.astype(low)
        full, grad = states_ref[index], cot[...]
        full_low, grad_low = full.astype(low), grad.astype(low)
        scores = dot_nt(c, b)
        from_state = dot_nt(c, full_low)
        from_grad = dot_nt(b, grad_low)
        tail_wide = spread_heads(tail, head_size, inner)
        dt_wide = spread_heads(dt, head_size, inner)
        d_in = (dy * spread_heads(inflow, head_size, inner)).astype(low)
        pushed = (x_wide * tail_wide * dt_wide).astype(low)
        d_scores = jnp.zeros((block, block), f32)
        dxd, col_sums = [], []
        change = jnp.zeros((block, LANES), f32)
        for head in range(heads):
            cols = slice(head * head_size, (head + 1) * head_size)
            decay = head_decay(same, cum, cumt, head)
            mixing = scores * decay
            both = dot_nt(dy_low[:, cols], x[:, cols]) * dtt[head : head + 1, :]
            d_scores = d_scores + both * decay
            joint = jnp.where(strict, both * mixing, 0.0)
            change = jnp.where(lane == head, jnp.sum(joint, axis=1, keepdims=True), change)
            col_sums.append(jnp.sum(joint, axis=0, keepdims=True))
            dxd.append(dot_tn(mixing.astype(low), dy_low[:, cols]))
        dxd = jnp.concatenate(dxd, axis=1) + from_grad * tail_wide
        dx[at, :] = dxd * dt_wide + dy * skip
        d_low = d_scores.astype(low)
        dbc[at, state:] = (dot_wide(d_low, b) + dot_wide(d_in, full_low)).astype(low)
        dbc[at, :state] = (dot_tn(d_low, c) + dot_wide(pushed, grad_low)).astype(low)
        through = sum_heads(dy * from_state, head_size) * inflow
        kept = sum_heads(x_wide * from_grad, head_size) * (tail * dt)
        columns = jnp.concatenate(
            col_sums + [jnp.zeros((LANES - heads, block), f32)], axis=0
        ).T
        product = full * grad
        whole = jnp.concatenate(
            [
                jnp.sum(product[h * head_size : (h + 1) * head_size, :], axis=0, keepdims=True)
                for h in range(heads)
            ]
            + [jnp.zeros((LANES - heads, state), f32)],
            axis=0,
        )
        whole = jnp.sum(whole.T, axis=0, keepdims=True)
        d_la = running_sum(change - columns + through - kept, True) + (
            jnp.sum(kept, axis=0, keepdims=True) + passing * whole
        )
        d_log = d_log + jnp.sum(d_la * (dt * rate), axis=0, keepdims=True)
        d_raw = (d_la * rate + sum_heads(dxd * x_wide, head_size)) * jax.nn.sigmoid(raw)
        d_raw = jnp.where(lane < heads, d_raw, 0.0)
        d_bias = d_bias + jnp.sum(d_raw, axis=0, keepdims=True)
        draw[at, :] = d_raw.astype(low)
        cot[...] = grad * rows_of_heads(passing, heads, head_size) + dot_tn(d_in, c)
        if index == steps - 2:
            scatter_br.middle()
            scatter_gb.middle()
    scatter_bc.start()

    def conv_back(cols, get):
        size = cols.stop - cols.start
        dz[0:8, cols] = jnp.zeros((8, size), f32)
        dz[8 + tokens :, cols] = jnp.zeros((8, size), f32)
        tap_sums = [jnp.zeros((1, size), f32) for _ in range(kernel + 1)]
        for index in range(steps):
            start = index * block
            key = key_ref[8 + start : 8 + start + block, :]
            total = jnp.broadcast_to(cw[kernel : kernel + 1, cols], (block, size))
            taps = []
            for offset in range(kernel):
                at = slice(8 - kernel + 1 + offset + start, 8 - kernel + 1 + offset + start + block)
                tap = pre_ref[at, cols]
                if offset < kernel - 1:
                    same = jnp.where(key_ref[at, :] == key, 1.0, 0.0)
                    tap = tap * jnp.concatenate([same] * (size // LANES), axis=1)
                taps.append(tap)
                total = total + cw[offset : offset + 1, cols] * tap
            sigm = jax.nn.sigmoid(total)
            change = get(index) * (sigm * (1.0 + total * (1.0 - sigm)))
            dz[8 + start : 8 + start + block, cols] = change
            for offset in range(kernel):
                tap_sums[offset] += jnp.sum(taps[offset] * change, axis=0, keepdims=True)
            tap_sums[kernel] += jnp.sum(change, axis=0, keepdims=True)
        for offset in range(kernel + 1):
            small[offset : offset + 1, cols] = tap_sums[offset]

    def back_rows(start, size, cols):
        span = cols.stop - cols.start
        key = key_ref[start : start + size, :]
        total = cw[kernel - 1 : kernel, cols] * dz[start : start + size, cols]
        for offset in range(kernel - 1):
            at = slice(start + kernel - 1 - offset, start + kernel - 1 - offset + size)
            same = jnp.where(key_ref[at, :] == key, 1.0, 0.0)
            total = total + cw[offset : offset + 1, cols] * (
                dz[at, cols] * jnp.concatenate([same] * (span // LANES), axis=1)
            )
        return total

    def halo(cols, out, arrived, slot):
        out[...] = back_rows(0, 8, cols)
        copy = remote(out, arrived, hs.at[slot], hr.at[slot], "dp", following)
        copy.start()
        return copy

    def finish_pre(cols, copy, arrived):
        for index in range(steps):
            start = index * block
            value = back_rows(8 + start, block, cols)
            if index == steps - 1:
                copy.wait()
                edge = value[block - 8 :, :] + arrived[...]
                value = jnp.concatenate([value[: block - 8], edge], axis=0)
            dpre[start : start + block, cols] = value.astype(low)

    cols = slice(0, inner)
    conv_back(cols, lambda index: dx[index * block : (index + 1) * block, :])
    copy = halo(cols, halo_out, halo_in, 0)
    scatter_bc.middle()
    finish_pre(cols, copy, halo_in)
    for index in range(steps):
        at = slice(index * block, (index + 1) * block)
        part_sum = dot_nt(dgate_ref[at, :], wb_ref[:, :inner])
        part_sum = part_sum + dot_nt(dpre[at, :inner], wa_ref[:, :inner])
        part_sum = part_sum + dot_nt(draw[at, :], wdt_ref[...])
        rows_part[at, :] = part_sum.astype(low)
    scatter_rows.start()
    dbc_all[own, :] = scatter_bc.finish().astype(low)
    gather_bc = Gather(model, dbc_all, rows, as_, ar_)
    gather_bc.start()
    ga_part[...] = dot_tn(normed_ref[...], dpre[:, :inner]).astype(low)
    scatter_ga.start()
    scatter_rows.middle()
    gather_bc.step()
    gather_bc.finish()
    cols = slice(inner, wide)
    conv_back(cols, lambda index: dbc_all[index * block : (index + 1) * block, :].astype(f32))
    copy = halo(cols, halo_bc_out, halo_bc_in, 1)
    scatter_ga.middle()
    finish_pre(cols, copy, halo_bc_in)

    def pick_exact(value, one):
        return dot_wide(
            jnp.concatenate(split(value, 3), axis=1), jnp.concatenate([one] * 3, axis=0)
        )

    def picker(count, first, lane_at, many):
        down = lax.broadcasted_iota(jnp.int32, (count, LANES), 0)
        over = lax.broadcasted_iota(jnp.int32, (count, LANES), 1) - lane_at
        return ((down == over + first) & (over >= 0) & (over < many)).astype(f32).astype(low)

    side = (
        dot_wide(dpre[:, inner:], picker(bc, model.me * quarter, bc_lane, quarter))
        + dot_wide(draw[...], picker(LANES, 0, dt_lane, heads))
    ).astype(low)
    gs_part[...] = dot_tn(normed_ref[...], side).astype(low)
    scatter_gs.start()
    d_rows = dot_nt(dpre[own, inner:], wa_ref[:, inner:wide])
    scatter_gs.middle()
    d_rows = d_rows + scatter_rows.finish()
    x = x_ref[...]
    rstd = lax.rsqrt(jnp.sum(x * x, axis=-1, keepdims=True) / mean_of + EPSILON)
    scaled = gain_ref[...][None, :] * d_rows
    small[kernel + 1 : kernel + 2, :width] = jnp.sum(d_rows * x * rstd, axis=0, keepdims=True)
    small[kernel + 2 : kernel + 3, :inner] = gsum_ref[0:1, :]
    d_heads = jnp.concatenate(
        [d_bias, d_log, sum_heads(gsum_ref[...], head_size, 3)[1:2, :], jnp.zeros((5, LANES), f32)],
        axis=0,
    )
    d_heads = pick_exact(d_heads, picker(LANES, 0, model.me * heads, heads))
    for index in range(3):
        small[kernel + 3 : kernel + 4, index * LANES : (index + 1) * LANES] = d_heads[
            index : index + 1, :
        ]

    def small_copy(hop):
        return remote(
            small, small_all.at[hop], ss.at[hop], sr.at[hop], "dp", lax.rem(data.me + hop, dp)
        )

    for hop in range(1, dp):
        small_copy(hop).start()
    packed[rows : 2 * rows, :width] = (
        cot_ref[...]
        + rstd * scaled
        - x * (rstd * rstd * rstd * (jnp.sum(scaled * x, axis=-1, keepdims=True) / mean_of))
    )
    packed[0:rows, :width] = x + scatter_br.finish()
    base = 2 * rows
    packed[base : base + part, : 2 * inner] = scatter_gb.finish()
    packed[base + part : base + 2 * part, :inner] = scatter_ga.finish()
    total = small[...]
    for hop in range(1, dp):
        small_copy(hop).wait_recv()
        total = total + small_all[hop]
    sums_own[...] = total

    def sums_copy(hop):
        return remote(
            sums_own, sums_ref.at[model.me], ts.at[hop], tr.at[hop], "tensor",
            lax.rem(model.me + hop, tensor),
        )

    for hop in range(1, tensor):
        sums_copy(hop).start()
    sums_ref[model.me] = total
    side_sum = scatter_gs.finish()
    packed[base + part : base + 2 * part, inner : inner + LANES] = pick_exact(
        side_sum, picker(LANES, dt_lane, 0, heads)
    )
    bc_own[...] = side_sum

    def bc_copy(hop):
        return remote(
            bc_own, gbc_ref.at[model.me], us.at[hop], ur.at[hop], "tensor",
            lax.rem(model.me + hop, tensor),
        )

    for hop in range(1, tensor):
        bc_copy(hop).start()
    gbc_ref[model.me] = side_sum
    for hop in range(1, tensor):
        sums_copy(hop).wait()
        bc_copy(hop).wait()
    for hop in range(1, dp):
        small_copy(hop).wait_send()
    for one in (scatter_bc, scatter_rows, scatter_ga, scatter_gs, scatter_br, scatter_gb, gather_bc):
        one.drain()
    for index in range(tensor):
        at = base + 2 * part + index * part
        packed[at : at + part, :LANES] = gbc_ref[index]
        at = base + (2 + tensor) * part + index * 8
        packed[at : at + 8, :] = sums_ref[index]


def block_kernel(dp, tensor, group, heads, kernel, mean_of, sequences, counts, *refs):
    sizes, parts, start = counts, [], 0
    for size in sizes:
        parts.append(refs[start : start + size])
        start += size
    ins, (packed,), kept, fscratch, bscratch = parts
    (
        x_ref, gain_ref, cot_ref, zx_ref, bcw_ref, dtt_ref, out_ref, seg_ref, cxw_ref, cxb_ref,
        cbw_ref, cbb_ref, bias_ref, log_ref, skip_ref, ggain_ref,
    ) = ins
    head_ref = fscratch[0]
    total = bias_ref.shape[0]
    rows = jnp.concatenate(
        [bias_ref[...][None, :], -jnp.exp(log_ref[...][None, :]), skip_ref[...][None, :],
         jnp.zeros((5, total), jnp.float32)],
        axis=0,
    )
    down = lax.broadcasted_iota(jnp.int32, (total, LANES), 0)
    over = lax.broadcasted_iota(jnp.int32, (total, LANES), 1)
    one = ((down == over + lax.axis_index("tensor") * heads) & (over < heads)).astype(
        jnp.float32
    ).astype(low)
    hi, mid, lo = split(rows, 3)
    head_ref[...] = dot_wide(hi, one) + dot_wide(mid, one) + dot_wide(lo, one)
    forward_part(
        dp, tensor, group, heads, mean_of, sequences,
        x_ref, gain_ref, cot_ref, zx_ref, bcw_ref, dtt_ref, out_ref, seg_ref, cxw_ref, cxb_ref,
        cbw_ref, cbb_ref, head_ref, ggain_ref, *kept, *fscratch[1:],
    )
    cw = fscratch[3]
    backward_part(
        dp, tensor, group, heads, kernel, mean_of, *kept, x_ref, gain_ref, cot_ref, cw, head_ref,
        packed, *bscratch,
    )


def finish_kernel(
    tensor, heads, kernel,
    packed,
    o_res, o_gin, o_norm, o_zx, o_bc, o_dt, o_cxw, o_cxb, o_cbw, o_cbb, o_dtb, o_log, o_skip,
    o_gate, o_out,
):
    part, inner = o_zx.shape[1:]
    rows, width = o_gin.shape
    base = 2 * rows
    bc = o_bc.shape[1]
    quarter = bc // tensor
    o_res[...] = packed[0:rows, :width]
    o_gin[...] = packed[rows : 2 * rows, :width]
    o_zx[0] = packed[base : base + part, :inner]
    o_zx[1] = packed[base + part : base + 2 * part, :inner]
    o_out[...] = packed[base : base + part, inner : 2 * inner]
    turned = jnp.concatenate(
        [
            packed[base + part : base + 2 * part, inner : inner + LANES],
            jnp.zeros((-part % LANES, LANES), jnp.float32),
        ],
        axis=0,
    ).T
    o_dt[...] = turned[: o_dt.shape[0], :part]
    base = base + 2 * part
    lane = lax.broadcasted_iota(jnp.int32, (part, LANES), 1)
    for start in range(0, bc, LANES):
        tile = jnp.zeros((part, LANES), jnp.float32)
        for one in range(tensor):
            if start <= one * quarter < start + LANES:
                at = one * quarter - start
                tile = jnp.where((lane >= at) & (lane < at + quarter), packed[base + one * part : base + (one + 1) * part, :LANES], tile)
        o_bc[:, start : start + LANES] = tile
    base = base + tensor * part
    sums = [packed[base + 8 * one : base + 8 * (one + 1), :] for one in range(tensor)]
    total = sums[0]
    for one in range(1, tensor):
        total = total + sums[one]
    o_norm[...] = total[kernel + 1, :width]
    o_cbw[...] = sums[0][0:kernel, inner : inner + bc]
    o_cbb[...] = sums[0][kernel, inner : inner + bc]
    for one in range(tensor):
        cols = slice(one * inner, (one + 1) * inner)
        o_cxw[:, cols] = sums[one][0:kernel, :inner]
        o_cxb[cols] = sums[one][kernel, :inner]
        o_gate[cols] = sums[one][kernel + 2, :inner]
    for index, out in enumerate((o_dtb, o_log, o_skip)):
        out[...] = total[kernel + 3, index * LANES : index * LANES + out.shape[0]]


def block_call(dp, tensor, group, heads, mean_of, sequences, *arrays):
    x, zx, bcw, cxw = arrays[0], arrays[3], arrays[4], arrays[8]
    rows, width = x.shape
    tokens, part, inner = rows * tensor, zx.shape[1], zx.shape[2]
    bc = bcw.shape[1]
    wide, state = inner + bc, bc // 2
    steps = tokens // min(GROUP, tokens)
    small = (8, -(-max(width, wide, 2 * inner, 3 * LANES) // LANES) * LANES)
    f32 = jnp.float32
    dma = pltpu.SemaphoreType.DMA
    kept = [
        pltpu.VMEM((tokens, width), low),
        pltpu.VMEM((tokens, width), low),
        pltpu.VMEM((dp * part, wide), low),
        pltpu.VMEM((dp * part, 2 * inner), low),
        pltpu.VMEM((dp * part, LANES), low),
        pltpu.VMEM((tokens + 8, wide), f32),
        pltpu.VMEM((tokens + 16, LANES), f32),
        pltpu.VMEM((tokens, wide), low),
        pltpu.VMEM((tokens, LANES), f32),
        pltpu.VMEM((tokens, LANES), f32),
        pltpu.VMEM((steps, inner, state), f32),
        pltpu.VMEM((tokens, inner), f32),
        pltpu.VMEM((tokens, inner), low),
        pltpu.VMEM((tokens, inner), low),
        pltpu.VMEM((inner + 16, state), low),
        pltpu.VMEM((8, inner), f32),
    ]
    forward_scratch = [
        pltpu.VMEM((8, LANES), f32),
        pltpu.VMEM((8, wide), f32),
        pltpu.VMEM((dp * 16, LANES), low),
        pltpu.VMEM((8, wide), f32),
        pltpu.VMEM((tokens, inner), f32),
        pltpu.VMEM((tokens, inner), f32),
        pltpu.VMEM((tokens, inner), f32),
        pltpu.VMEM((inner + 16, state), low),
        pltpu.VMEM((group, inner + 16, state), low),
        pltpu.VMEM((inner, state), f32),
        pltpu.VMEM((8 * steps, LANES), f32),
        pltpu.VMEM((8, tokens), f32),
        pltpu.VMEM((tensor, 8, tokens), f32),
        *[dma((2 * n,)) for n in (dp, dp, dp, dp, dp, dp, tensor, tensor, tensor, tensor)],
        dma((2,)), dma((2,)),
        dma((group,)), dma((group,)),
        dma((tensor,)), dma((tensor,)),
    ]
    backward_scratch = [
        pltpu.VMEM((tokens, inner), f32),
        pltpu.VMEM((tokens, bc), low),
        pltpu.VMEM((tokens, LANES), low),
        pltpu.VMEM((tokens + 16, wide), f32),
        pltpu.VMEM((tokens, wide), low),
        pltpu.VMEM((tokens, bc), low),
        pltpu.VMEM((tokens, width), low),
        pltpu.VMEM((dp * part, 2 * inner), low),
        pltpu.VMEM((tokens, width), low),
        pltpu.VMEM((dp * part, inner), low),
        pltpu.VMEM((dp * part, LANES), low),
        pltpu.VMEM((8, inner), f32),
        pltpu.VMEM((8, inner), f32),
        pltpu.VMEM((8, bc), f32),
        pltpu.VMEM((8, bc), f32),
        pltpu.VMEM((inner, state), f32),
        pltpu.VMEM((group, inner + 16, state), low),
        pltpu.VMEM(small, f32),
        pltpu.VMEM((dp,) + small, f32),
        pltpu.VMEM(small, f32),
        pltpu.VMEM((part, LANES), f32),
        pltpu.VMEM((tensor, part, LANES), f32),
        pltpu.VMEM((tensor,) + small, f32),
        *Scatter.scratch(tensor, rows, bc),
        *Scatter.scratch(tensor, rows, width),
        *Scatter.scratch(tensor, rows, width),
        *Scatter.scratch(dp, part, inner),
        *Scatter.scratch(dp, part, 2 * inner),
        *Scatter.scratch(dp, part, LANES),
        dma((2 * tensor,)), dma((2 * tensor,)),
        dma((2,)), dma((2,)),
        dma((dp,)), dma((dp,)),
        dma((tensor,)), dma((tensor,)),
        dma((tensor,)), dma((tensor,)),
        dma((group,)), dma((group,)),
    ]
    counts = (len(arrays), 1, len(kept), len(forward_scratch), len(backward_scratch))
    lines = 2 * rows + (2 + tensor) * part + 8 * tensor
    return pl.pallas_call(
        functools.partial(
            block_kernel, dp, tensor, group, heads, cxw.shape[0], mean_of, sequences, counts
        ),
        out_shape=jax.ShapeDtypeStruct((lines, small[1]), f32),
        in_specs=vmem(len(arrays)),
        out_specs=vmem(1)[0],
        scratch_shapes=kept + forward_scratch + backward_scratch,
        compiler_params=pltpu.CompilerParams(
            collective_id=0, has_side_effects=True, vmem_limit_bytes=63 * 2**20
        ),
        name="block",
    )(*arrays)


def finish_call(tensor, heads, kernel, rows, width, part, inner, heads_total, bc, packed):
    inner_total = inner * tensor
    outs = (
        (rows, width), (rows, width), (width,), (2, part, inner), (part, bc), (heads, part),
        (kernel, inner_total), (inner_total,), (kernel, bc), (bc,), (heads_total,),
        (heads_total,), (heads_total,), (inner_total,), (part, inner),
    )
    return pl.pallas_call(
        functools.partial(finish_kernel, tensor, heads, kernel),
        out_shape=tuple(jax.ShapeDtypeStruct(one, jnp.float32) for one in outs),
        in_specs=vmem(1),
        out_specs=tuple(vmem(len(outs))),
        compiler_params=pltpu.CompilerParams(vmem_limit_bytes=32 * 2**20),
        name="finish",
    )(packed)


def pad_to(array, size, axis):
    widths = [(0, 0)] * array.ndim
    widths[axis] = (0, size - array.shape[axis])
    return jnp.pad(array, widths)


def per_device(
    block_input,
    norm_gain,
    zx_weight,
    bc_weight,
    dt_weight,
    conv_x_weight,
    conv_x_bias,
    conv_bc_weight,
    conv_bc_bias,
    dt_bias,
    decay_log,
    skip_gain,
    gate_gain,
    out_weight,
    segments,
    cotangent,
):
    tensor_count = lax.axis_size("tensor")
    data_count = lax.axis_size("dp")
    token_count = segments.shape[0]
    row_count, width = block_input.shape
    part = zx_weight.shape[1]
    heads_here = dt_weight.shape[1]
    heads_total = dt_bias.shape[0]
    taps = conv_x_weight.shape[0]
    bc_size = bc_weight.shape[1]
    padded = -(-part // 16) * 16
    columns = data_count * padded

    def widen(array):
        if padded == part:
            return array
        lead = array.shape[:-1]
        return pad_to(array.reshape(lead + (data_count, part)), padded, -1).reshape(lead + (columns,))

    def narrow(array):
        if padded == part:
            return array
        lead = array.shape[:-1]
        return array.reshape(lead + (data_count, padded))[..., :part].reshape(lead + (width,))

    group = max(1, LENGTH // token_count)
    if data_count % group:
        group = data_count
    sequences = data_count * token_count // LENGTH + 1
    packed = block_call(
        data_count, tensor_count, group, heads_here, width, sequences,
        widen(block_input), widen(norm_gain), widen(cotangent), pad_to(zx_weight, padded, 1),
        pad_to(bc_weight, padded, 0), dt_weight.T, pad_to(out_weight.T, padded, 0), segments,
        conv_x_weight, conv_x_bias, conv_bc_weight, conv_bc_bias, dt_bias, decay_log, skip_gain,
        gate_gain,
    )
    outs = list(
        finish_call(
            tensor_count, heads_here, taps, row_count, columns, padded, zx_weight.shape[2],
            heads_total, bc_size, packed,
        )
    )
    for index in (0, 1, 2):
        outs[index] = narrow(outs[index])
    if padded != part:
        outs[3] = outs[3][:, :part]
        outs[4], outs[5], outs[14] = outs[4][:part], outs[5][:, :part], outs[14][:part]
    outs[5], outs[14] = outs[5].T, outs[14].T
    return tuple(outs)


def solution(mesh):
    in_specs = (
        P(("dp", "tensor"), None),
        P(),
        P(None, "dp", "tensor"),
        P("dp", None),
        P("dp", "tensor"),
        P(),
        P(),
        P(),
        P(),
        P(),
        P(),
        P(),
        P(),
        P("tensor", "dp"),
        P("dp"),
        P(("dp", "tensor"), None),
    )
    out_specs = (
        P(("dp", "tensor"), None),
        P(("dp", "tensor"), None),
        P(),
        P(None, "dp", "tensor"),
        P("dp", None),
        P("dp", "tensor"),
        P(),
        P(),
        P(),
        P(),
        P(),
        P(),
        P(),
        P(),
        P("tensor", "dp"),
    )
    return jax.shard_map(
        per_device, mesh=mesh, in_specs=in_specs, out_specs=out_specs, check_vma=False
    )
```

```python
import functools
import jax
import jax.numpy as jnp
from jax import lax
from jax.experimental import pallas as pl
from jax.experimental.pallas import tpu as pltpu
from jax.sharding import PartitionSpec as P

GROUP = 256
LENGTH = 4096
EPSILON = 1e-05
PAD = 8
LANES = 128
MESH = pl.DeviceIdType.MESH
low = jnp.bfloat16


def dot_wide(left, right):
    return jnp.dot(left, right, preferred_element_type=jnp.float32)


def dot_nt(left, right):
    return lax.dot_general(left, right, (((1,), (1,)), ((), ())), preferred_element_type=jnp.float32)


def dot_tn(left, right):
    return lax.dot_general(left, right, (((0,), (0,)), ((), ())), preferred_element_type=jnp.float32)


def halves(size):
    half = size // 2 if size % (2 * LANES) == 0 else size
    return [(start, start + half) for start in range(0, size, half)]


def head_decay(same, cum, cumt, head):
    spread = jnp.where(same, cum[:, head : head + 1] - cumt[head : head + 1, :], -1e30)
    return jnp.exp(spread)


def vmem(count):
    return [pl.BlockSpec(memory_space=pltpu.VMEM)] * count


class Grid2:
    def __init__(self, axis, count):
        self.axis, self.count = axis, count
        self.inner = 2 if count % 2 == 0 else 1
        self.outer = count // self.inner
        self.me = lax.axis_index(axis)
        self.mi = lax.rem(self.me, self.inner)
        self.mo = self.me // self.inner

    def at(self, hop, inner):
        return lax.rem(self.mo + hop + self.outer, self.outer) * self.inner + inner

    @property
    def partner(self):
        return self.mo * self.inner + (self.inner - 1 - self.mi)


def remote(src, dst, send, recv, axis, index):
    return pltpu.make_async_remote_copy(
        src_ref=src, dst_ref=dst, send_sem=send, recv_sem=recv,
        device_id={axis: index}, device_id_type=MESH,
    )


def greet(*axes):
    barrier = pltpu.get_barrier_semaphore()
    total = 0
    for axis, count in axes:
        me = lax.axis_index(axis)
        for hop in range(1, count):
            pl.semaphore_signal(
                barrier, inc=1, device_id={axis: lax.rem(me + hop, count)}, device_id_type=MESH
            )
            total += 1
    return total


class Gather:
    def __init__(self, grid, ref, rows, send, recv):
        self.grid, self.ref, self.rows, self.send, self.recv = grid, ref, rows, send, recv
        self.todo = list(range(1, grid.outer))

    def copy(self, outer, inner, slot, target_outer, target_inner):
        g = self.grid
        index = outer * g.inner + inner
        piece = self.ref.at[pl.ds(pl.multiple_of(index * self.rows, self.rows), self.rows), :]
        return remote(
            piece, piece, self.send.at[slot], self.recv.at[slot], g.axis,
            target_outer * g.inner + target_inner,
        )

    def along(self, way, step):
        g = self.grid
        slot = step if way > 0 else g.outer - 1 + step
        return self.copy(g.mo - way * (step - 1), g.mi, slot, g.mo + way, g.mi)

    def over(self, way, step, inner):
        g = self.grid
        slot = 2 * g.outer - 2 + step + (0 if way > 0 else g.outer - 1)
        return self.copy(g.mo - way * step, inner, slot, g.mo, g.inner - 1 - g.mi)

    def has(self, way, step):
        g = self.grid
        return g.mo - step >= 0 if way > 0 else g.mo + step < g.outer

    def leads(self, way):
        return self.has(-way, 1)

    def start(self):
        self.start_along()
        self.start_over()

    def start_along(self):
        if self.grid.outer > 1:
            for way in (1, -1):
                pl.when(self.leads(way))(lambda way=way: self.along(way, 1).start())

    def start_over(self):
        g = self.grid
        if g.inner > 1:
            self.copy(g.mo, g.mi, 0, g.mo, g.inner - 1 - g.mi).start()

    def step(self):
        g = self.grid
        if not self.todo:
            return
        step = self.todo.pop(0)
        for way in (1, -1):

            @pl.when(self.has(way, step))
            def _(way=way):
                slot = step if way > 0 else g.outer - 1 + step
                self.copy(g.mo - way * step, g.mi, slot, g.mo, g.mi).wait_recv()
                if step + 1 < g.outer:
                    pl.when(self.leads(way))(lambda: self.along(way, step + 1).start())
                if g.inner > 1:
                    self.over(way, step, g.mi).start()

    def finish(self):
        g = self.grid
        while self.todo:
            self.step()
        if g.inner > 1:
            self.copy(g.mo, g.inner - 1 - g.mi, 0, g.mo, g.mi).wait_recv()
            for step in range(1, g.outer):
                for way in (1, -1):
                    pl.when(self.has(way, step))(
                        lambda way=way: self.over(way, step, g.inner - 1 - g.mi).wait_recv()
                    )

    def drain(self):
        g = self.grid
        if g.inner > 1:
            self.copy(g.mo, g.mi, 0, g.mo, g.inner - 1 - g.mi).wait_send()
        for step in range(1, g.outer):
            for way in (1, -1):
                there = self.has(way, step - 1) if step > 1 else True
                pl.when(jnp.logical_and(self.leads(way), there))(
                    lambda way=way: self.along(way, step).wait_send()
                )
                if g.inner > 1:
                    pl.when(self.has(way, step))(
                        lambda way=way: self.over(way, step, g.mi).wait_send()
                    )


class Scatter:
    def __init__(self, grid, src, first, second, landed, rows, send, recv):
        self.grid, self.src, self.rows, self.send, self.recv = grid, src, rows, send, recv
        self.first, self.second, self.landed = first, second, landed

    @staticmethod
    def scratch(count, rows, width):
        outer = count // (2 if count % 2 == 0 else 1)
        return [
            pltpu.VMEM((outer, rows, width), low),
            pltpu.VMEM((outer, rows, width), low),
            pltpu.VMEM((outer, rows, width), low),
            pltpu.SemaphoreType.DMA((2 * outer,)),
            pltpu.SemaphoreType.DMA((2 * outer,)),
        ]

    def block(self, index):
        return self.src.at[pl.ds(pl.multiple_of(index * self.rows, self.rows), self.rows), :]

    def over(self, hop):
        g = self.grid
        return remote(
            self.block(g.at(hop, g.inner - 1 - g.mi)), self.first.at[hop],
            self.send.at[hop], self.recv.at[hop], g.axis, g.partner,
        )

    def along(self, hop):
        g = self.grid
        slot = g.outer + hop
        return remote(
            self.second.at[hop], self.landed.at[hop],
            self.send.at[slot], self.recv.at[slot], g.axis, g.at(hop, g.mi),
        )

    def start(self):
        if self.grid.inner > 1:
            for hop in list(range(1, self.grid.outer)) + [0]:
                self.over(hop).start()

    def pair(self, hop):
        g = self.grid
        total = self.block(g.at(hop, g.mi))[...].astype(jnp.float32)
        if g.inner > 1:
            self.over(hop).wait_recv()
            total = total + self.first[hop].astype(jnp.float32)
        return total

    def middle(self):
        for hop in range(1, self.grid.outer):
            self.second[hop] = self.pair(hop).astype(low)
            self.along(hop).start()

    def finish(self):
        g = self.grid
        total = self.pair(0)
        for hop in range(1, g.outer):
            self.along(hop).wait_recv()
            total = total + self.landed[hop].astype(jnp.float32)
        return total

    def drain(self):
        g = self.grid
        for hop in range(g.outer):
            if g.inner > 1:
                self.over(hop).wait_send()
            if hop:
                self.along(hop).wait_send()


def split(value, pieces):
    out = []
    for _ in range(pieces):
        piece = value.astype(low)
        out.append(piece)
        value = value - piece.astype(jnp.float32)
    return out


def spread_heads(value, head_size, inner, pieces=2):
    one = (
        lax.broadcasted_iota(jnp.int32, (LANES, inner), 1) // head_size
        == lax.broadcasted_iota(jnp.int32, (LANES, inner), 0)
    ).astype(jnp.float32).astype(low)
    return dot_wide(
        jnp.concatenate(split(value, pieces), axis=1), jnp.concatenate([one] * pieces, axis=0)
    )


def sum_heads(value, head_size, pieces=2):
    inner = value.shape[1]
    one = (
        lax.broadcasted_iota(jnp.int32, (inner, LANES), 0) // head_size
        == lax.broadcasted_iota(jnp.int32, (inner, LANES), 1)
    ).astype(jnp.float32).astype(low)
    return dot_wide(
        jnp.concatenate(split(value, pieces), axis=1), jnp.concatenate([one] * pieces, axis=0)
    )


def running_sum(value, reverse=False):
    size = value.shape[0]
    row = lax.broadcasted_iota(jnp.int32, (size, size), 0)
    col = lax.broadcasted_iota(jnp.int32, (size, size), 1)
    keep = (row <= col) if reverse else (row >= col)
    keep = keep.astype(jnp.float32).astype(low)
    pieces = split(value, 3)
    total = dot_wide(keep, jnp.concatenate(pieces, axis=1))
    width = value.shape[1]
    return total[:, :width] + total[:, width : 2 * width] + total[:, 2 * width :]


def rows_of_heads(row, heads, head_size):
    turned = jnp.broadcast_to(row, (LANES, LANES)).T
    return jnp.concatenate(
        [jnp.broadcast_to(turned[h : h + 1, :], (head_size, LANES)) for h in range(heads)], axis=0
    )


def softplus(value):
    return jnp.maximum(value, 0.0) + jnp.log1p(jnp.exp(-jnp.abs(value)))


def block_parts(cum, key, before):
    size = cum.shape[0]
    last_key, last = key[size - 1 :, :], cum[size - 1 :, :]
    inflow = jnp.where(key == before, jnp.exp(cum), 0.0)
    tail = jnp.where(key == last_key, jnp.exp(last - cum), 0.0)
    passing = jnp.where(last_key == before, jnp.exp(last), 0.0)
    return inflow, tail, passing


def forward_part(
    dp, tensor, group, heads, mean_of, sequences,
    x_ref, gain_ref, cot_ref, zx_ref, bcw_ref, dtt_ref, out_ref, seg_ref, cxw_ref, cxb_ref, cbw_ref,
    cbb_ref, head_ref, ggain_ref,
    normed_ref, cotl_ref, wa_ref, wb_ref, wdt_ref, pre_ref, key_ref, act_ref, raw_ref, cum_ref,
    states_ref, dmix_ref, dgate_ref, nout_ref, scot_ref, gsum_ref,
    tail, dtall, cw, y, gate, dno, sent, got, ends, decays, sums, sums_all,
    sa, ra, sb, rb, sd, rd, sn, rn, sc, rc, sh, rh, sl, rl, ss, rs,
):
    rows, width = x_ref.shape
    tokens = normed_ref.shape[0]
    part, inner = zx_ref.shape[1], zx_ref.shape[2]
    bc = bcw_ref.shape[1]
    wide, state = inner + bc, bc // 2
    head_size = inner // heads
    kernel = cxw_ref.shape[0]
    block = min(GROUP, tokens)
    steps = tokens // block
    f32 = jnp.float32
    data, model = Grid2("dp", dp), Grid2("tensor", tensor)
    mine = pl.ds(pl.multiple_of(data.me * part, part), part)
    own = pl.ds(pl.multiple_of(model.me * rows, rows), rows)
    greeted = greet(("dp", dp), ("tensor", tensor))
    units = pl.ds(pl.multiple_of(model.me * inner, LANES), inner)

    wa_ref[mine, :inner] = zx_ref[1]
    wa_ref[mine, inner:] = bcw_ref[...]
    wb_ref[mine, :inner] = zx_ref[0]
    wb_ref[mine, inner:] = out_ref[...]
    flat = dtt_ref[...].astype(f32)
    flat = jnp.concatenate([flat, jnp.zeros((heads, LANES - flat.shape[1]), f32)], axis=1)
    flat = jnp.concatenate([flat, jnp.zeros((16 - heads, LANES), f32)], axis=0)
    dtall[pl.ds(pl.multiple_of(data.me * 16, 16), 16), :] = flat.astype(low)
    wa = Gather(data, wa_ref, part, sa, ra)
    wb = Gather(data, wb_ref, part, sb, rb)
    wd = Gather(data, dtall, 16, sd, rd)
    nm = Gather(model, normed_ref, rows, sn, rn)
    ct = Gather(model, cotl_ref, rows, sc, rc)
    following = lax.rem(data.me + 1, dp)
    seg_copy = remote(
        key_ref.at[pl.ds(tokens, 8), :], key_ref.at[pl.ds(0, 8), :], sh.at[0], rh.at[0], "dp",
        following,
    )
    pre_copy = remote(
        tail, pre_ref.at[pl.ds(0, 8), :], sh.at[1], rh.at[1], "dp", following
    )
    if greeted:
        pl.semaphore_wait(pltpu.get_barrier_semaphore(), greeted)
    wd.start()
    wa.start()
    x = x_ref[...]
    rstd = lax.rsqrt(jnp.sum(x * x, axis=-1, keepdims=True) / mean_of + EPSILON)
    normed_ref[own, :] = (x * rstd * gain_ref[...][None, :]).astype(low)
    nm.start()
    wb.start_over()
    cotl_ref[own, :] = cot_ref[...].astype(low)
    for index in range(steps):
        at = slice(index * block, (index + 1) * block)
        line = seg_ref[at][None, :].astype(f32)
        key_ref[8 + index * block : 8 + (index + 1) * block, :] = jnp.broadcast_to(
            line, (LANES, block)
        ).T
    key_ref[8 + tokens :, :] = jnp.zeros((8, LANES), f32)
    seg_copy.start()
    for step in range(1, data.outer):
        wd.step()
        wa.step()
        if step == min(2, data.outer - 1):
            wb.start_along()
            nm.step()
            ct.start()
    if data.outer == 1:
        nm.step()
        ct.start()
    cw[0:kernel, :inner] = cxw_ref[:, units]
    cw[0:kernel, inner:] = cbw_ref[...]
    cw[kernel : kernel + 1, :inner] = cxb_ref[units][None, :]
    cw[kernel : kernel + 1, inner:] = cbb_ref[...][None, :]
    wd.finish()
    turn = (
        lax.broadcasted_iota(jnp.int32, (part, LANES), 0)
        == lax.broadcasted_iota(jnp.int32, (part, LANES), 1)
    ).astype(f32).astype(low)
    for index in range(dp):
        shard = jnp.concatenate(
            [dtall[index * 16 : (index + 1) * 16, :], jnp.zeros((LANES - 16, LANES), low)], axis=0
        )
        wdt_ref[index * part : (index + 1) * part, :] = dot_nt(turn, shard).astype(low)
    nm.finish()
    wa.finish()
    last = steps - 1
    bias, rate = head_ref[0:1, :], head_ref[1:2, :]
    for index in [last] + list(range(last)):
        at = slice(index * block, (index + 1) * block)
        first = dot_wide(normed_ref[at, :], wa_ref[...])
        pre_ref[8 + index * block : 8 + (index + 1) * block, :] = first.astype(low).astype(f32)
        if index == last:
            tail[...] = pre_ref[tokens : tokens + 8, :]
            pre_copy.start()
        raw_ref[at, :] = dot_wide(normed_ref[at, :], wdt_ref[...]) + bias
    wb.step()
    seg_copy.wait()
    pos = lax.broadcasted_iota(jnp.int32, (tokens + 16, LANES), 0) + (data.me * tokens - 8 + LENGTH)
    key_ref[...] = key_ref[...] * sequences + (pos // LENGTH).astype(f32)
    ends[...] = jnp.zeros_like(ends)
    total_cum = jnp.zeros((1, LANES), f32)
    first_before = key_ref[7:8, :]
    before = first_before
    pre_copy.wait()
    for index in range(steps):
        start = index * block
        at = slice(start, start + block)
        key = key_ref[8 + start : 8 + start + block, :]
        total = jnp.broadcast_to(cw[kernel : kernel + 1, :], (block, wide))
        for offset in range(kernel):
            shift = slice(8 - kernel + 1 + offset + start, 8 - kernel + 1 + offset + start + block)
            tap = cw[offset : offset + 1, :] * pre_ref[shift, :]
            if offset < kernel - 1:
                same = jnp.where(key_ref[shift, :] == key, 1.0, 0.0)
                tap = tap * jnp.concatenate([same] * (wide // LANES), axis=1)
            total = total + tap
        act_ref[at, :] = (total * jax.nn.sigmoid(total)).astype(low)
        dt = softplus(raw_ref[at, :])
        cum = running_sum(dt * rate)
        cum_ref[at, :] = cum
        inflow, tail_w, passing = block_parts(cum, key, before)
        pushed = (
            act_ref[at, :inner].astype(f32) * spread_heads(tail_w * dt, head_size, inner)
        ).astype(low)
        states_ref[index] = ends[...]
        reach = jnp.where(before == first_before, jnp.exp(total_cum), 0.0)
        decays[index * 8 : index * 8 + 1, :] = reach
        ends[...] = ends[...] * rows_of_heads(passing, heads, head_size) + dot_tn(
            pushed, act_ref[at, inner : inner + state]
        )
        total_cum = total_cum + cum[block - 1 :, :]
        before = key[block - 1 :, :]
        if index == 0:
            ct.step()
        if index % 2 == 1:
            wb.step()
    reach = jnp.where(before == first_before, jnp.exp(total_cum), 0.0)
    turned = jnp.broadcast_to(reach, (LANES, LANES)).T[:8, :]
    hi, lo = split(turned, 2)
    sent[0:inner, :] = ends[...].astype(low)
    sent[inner : inner + 16, :] = jnp.concatenate([hi, lo], axis=0)
    line_start = (data.me // group) * group
    place = lax.rem(data.me, group)

    def line_copy(hop):
        return remote(
            sent, got.at[place], sl.at[hop], rl.at[hop], "dp",
            line_start + lax.rem(place + hop, group),
        )

    for hop in range(1, group):
        line_copy(hop).start()
    got[place] = sent[...]
    row_i = lax.broadcasted_iota(jnp.int32, (block, block), 0)
    col_i = lax.broadcasted_iota(jnp.int32, (block, block), 1)
    for index in range(steps):
        start = index * block
        at = slice(start, start + block)
        key = key_ref[8 + start : 8 + start + block, :]
        keyt = key.T
        same = (row_i >= col_i) & (
            jnp.concatenate([key] * (block // LANES), axis=1) == keyt[0:1, :]
        )
        cum = cum_ref[at, :]
        cumt = cum.T
        dtt = softplus(raw_ref[at, :]).T
        x = act_ref[at, :inner]
        scores = dot_nt(act_ref[at, inner + state :], act_ref[at, inner : inner + state])
        for head in range(heads):
            cols = slice(head * head_size, (head + 1) * head_size)
            for top, stop in halves(block):
                mixing = (
                    scores[top:stop, :stop]
                    * head_decay(same[top:stop, :stop], cum[top:stop, :], cumt[:, :stop], head)
                    * dtt[head : head + 1, :stop]
                ).astype(low)
                y[start + top : start + stop, cols] = dot_wide(mixing, x[:stop, cols])
        wb.step()
    ct.finish()
    wb.finish()
    for index in range(steps):
        at = slice(index * block, (index + 1) * block)
        gate[at, :] = dot_wide(normed_ref[at, :], wb_ref[:, :inner])
        dno[at, :] = dot_wide(cotl_ref[at, :], wb_ref[:, inner:])
    for hop in range(1, group):
        line_copy(hop).wait()
    entry = jnp.zeros((inner, state), f32)
    for index in range(group - 1):
        factor = got[index, inner : inner + 8, :].astype(f32) + got[index, inner + 8 :, :].astype(f32)
        factor = jnp.concatenate(
            [jnp.broadcast_to(factor[h : h + 1, :], (head_size, LANES)) for h in range(heads)], axis=0
        )
        longer = entry * factor + got[index, :inner, :].astype(f32)
        entry = jnp.where(index < place, longer, entry)
    skip = spread_heads(head_ref[0:8, :], head_size, inner, 3)[2:3, :]
    ggain = ggain_ref[units][None, :]
    before = first_before
    for index in range(steps):
        start = index * block
        at = slice(start, start + block)
        full = states_ref[index] + entry * rows_of_heads(
            decays[index * 8 : index * 8 + 1, :], heads, head_size
        )
        states_ref[index] = full
        key = key_ref[8 + start : 8 + start + block, :]
        inflow = jnp.where(key == before, jnp.exp(cum_ref[at, :]), 0.0)
        before = key[block - 1 :, :]
        mixed = (
            y[at, :]
            + dot_nt(act_ref[at, inner + state :], full.astype(low))
            * spread_heads(inflow, head_size, inner)
            + skip * act_ref[at, :inner].astype(f32)
        )
        y[at, :] = mixed
        gate_in = gate[at, :]
        gated = mixed * (gate_in * jax.nn.sigmoid(gate_in))
        squares = jnp.sum(gated * gated, axis=1, keepdims=True)
        dots = jnp.sum(gated * (ggain * dno[at, :]), axis=1, keepdims=True)
        lane = lax.broadcasted_iota(jnp.int32, (block, LANES), 1)
        both = jnp.where(lane == 0, squares, jnp.where(lane == 1, dots, 0.0))
        sums[:, at] = both.T[:8, :]

    def sums_copy(hop):
        return remote(
            sums, sums_all.at[hop], ss.at[hop], rs.at[hop], "tensor",
            lax.rem(model.me + hop, tensor),
        )

    for hop in range(1, tensor):
        sums_copy(hop).start()
    for hop in range(1, tensor):
        sums_copy(hop).wait_recv()
    before = first_before
    to_exit = jnp.zeros((1, LANES), f32)
    scot = jnp.zeros((inner, state), f32)
    g_gate = jnp.zeros((1, inner), f32)
    g_skip = jnp.zeros((1, inner), f32)
    total_cum = jnp.zeros((1, LANES), f32)
    for index in range(steps):
        start = index * block
        at = slice(start, start + block)
        total = sums[:, at]
        for hop in range(1, tensor):
            total = total + sums_all[hop, :, at]
        total = total / (inner * tensor)
        turned = jnp.concatenate([total, jnp.zeros((LANES - 8, block), f32)], axis=0).T
        rstd_gate = lax.rsqrt(turned[:, 0:1] + EPSILON)
        gate_dots = turned[:, 1:2]
        gate_in, mixed, d_out = gate[at, :], y[at, :], dno[at, :]
        sigm = jax.nn.sigmoid(gate_in)
        gate_act = gate_in * sigm
        gated = mixed * gate_act
        gated_normed = gated * rstd_gate
        nout_ref[at, :] = (gated_normed * ggain).astype(low)
        g_gate += jnp.sum(d_out * gated_normed, axis=0, keepdims=True)
        d_gated = rstd_gate * (ggain * d_out) - gated * (rstd_gate * rstd_gate * rstd_gate * gate_dots)
        d_mixed = d_gated * gate_act
        dmix_ref[at, :] = d_mixed
        dgate_ref[at, :] = (
            d_gated * mixed * sigm * (1.0 + gate_in * (1.0 - sigm))
        ).astype(low)
        g_skip += jnp.sum(d_mixed * act_ref[at, :inner].astype(f32), axis=0, keepdims=True)
        key = key_ref[8 + start : 8 + start + block, :]
        cum = cum_ref[at, :]
        reach = jnp.where(key == first_before, jnp.exp(cum + total_cum), 0.0)
        total_cum = total_cum + cum[block - 1 :, :]
        scot += dot_tn(
            (d_mixed * spread_heads(reach, head_size, inner)).astype(low),
            act_ref[at, inner + state :],
        )
    scot_ref[0:inner, :] = scot.astype(low)
    scot_ref[inner:, :] = sent[inner:, :]
    gsum_ref[...] = jnp.concatenate([g_gate, g_skip, jnp.zeros((6, inner), f32)], axis=0)
    for hop in range(1, tensor):
        sums_copy(hop).wait_send()
    for one in (wa, wb, wd, nm, ct):
        one.drain()


def backward_part(
    dp, tensor, group, heads, kernel, mean_of,
    normed_ref, cotl_ref, wa_ref, wb_ref, wdt_ref, pre_ref, key_ref, act_ref, raw_ref, cum_ref,
    states_ref, dmix_ref, dgate_ref, nout_ref, scot_ref, gsum_ref,
    x_ref, gain_ref, cot_ref, cw, head_ref,
    packed,
    dx, dbc, draw, dz, dpre, dbc_all, branch_part, gb_part, rows_part, ga_part, gs_part,
    halo_out, halo_in, halo_bc_out, halo_bc_in, cot, got, small, small_all, sums_own, bc_own, gbc_ref, sums_ref,
    b1, b2, b3, bs, br, r1, r2, r3, rs, rr, q1, q2, q3, qs, qr, g1, g2, g3, gs, gr,
    h1, h2, h3, hs_, hr_, k1, k2, k3, ks, kr,
    as_, ar_, hs, hr, ss, sr, ts, tr, us, ur, sl, rl,
):
    tokens = normed_ref.shape[0]
    wide = act_ref.shape[1]
    inner = dmix_ref.shape[1]
    bc = wide - inner
    state = bc // 2
    head_size = inner // heads
    rows, width = x_ref.shape
    part = wa_ref.shape[0] // dp
    data, model = Grid2("dp", dp), Grid2("tensor", tensor)
    block = min(GROUP, tokens)
    steps = tokens // block
    following = lax.rem(data.me + dp - 1, dp)
    f32 = jnp.float32
    own = pl.ds(pl.multiple_of(model.me * rows, rows), rows)
    quarter = bc // tensor
    bc_lane = lax.rem(model.me * quarter, LANES)
    dt_lane = lax.rem(bc_lane + quarter, LANES)

    line_start = (data.me // group) * group
    place = lax.rem(data.me, group)

    def line_copy(hop):
        return remote(
            scot_ref, got.at[place], sl.at[hop], rl.at[hop], "dp",
            line_start + lax.rem(place + hop, group),
        )

    for hop in range(1, group):
        line_copy(hop).start()
    scatter_br = Scatter(model, branch_part, q1, q2, q3, rows, qs, qr)
    scatter_gb = Scatter(data, gb_part, h1, h2, h3, part, hs_, hr_)
    scatter_bc = Scatter(model, dbc, b1, b2, b3, rows, bs, br)
    scatter_rows = Scatter(model, rows_part, r1, r2, r3, rows, rs, rr)
    scatter_ga = Scatter(data, ga_part, g1, g2, g3, part, gs, gr)
    scatter_gs = Scatter(data, gs_part, k1, k2, k3, part, ks, kr)
    gb_part[:, :inner] = dot_tn(normed_ref[...], dgate_ref[...]).astype(low)
    gb_part[:, inner:] = dot_tn(cotl_ref[...], nout_ref[...]).astype(low)
    scatter_gb.start()
    for index in range(steps):
        at = slice(index * block, (index + 1) * block)
        branch_part[at, :] = dot_nt(nout_ref[at, :], wb_ref[:, inner:]).astype(low)
    scatter_br.start()
    got[place] = scot_ref[...]
    small[...] = jnp.zeros_like(small)
    for hop in range(1, group):
        line_copy(hop).wait()
    leave = jnp.zeros((inner, state), f32)
    for index in range(group - 1, 0, -1):
        factor = got[index, inner : inner + 8, :].astype(f32) + got[index, inner + 8 :, :].astype(f32)
        factor = jnp.concatenate(
            [jnp.broadcast_to(factor[h : h + 1, :], (head_size, LANES)) for h in range(heads)], axis=0
        )
        longer = leave * factor + got[index, :inner, :].astype(f32)
        leave = jnp.where(index > place, longer, leave)
    cot[...] = leave
    rate = head_ref[1:2, :]
    skip = spread_heads(head_ref[0:8, :], head_size, inner, 3)[2:3, :]
    row_i = lax.broadcasted_iota(jnp.int32, (block, block), 0)
    col_i = lax.broadcasted_iota(jnp.int32, (block, block), 1)
    lane = lax.broadcasted_iota(jnp.int32, (block, LANES), 1)
    d_bias = jnp.zeros((1, LANES), f32)
    d_log = jnp.zeros((1, LANES), f32)
    for index in range(steps - 1, -1, -1):
        start = index * block
        at = slice(start, start + block)
        key = key_ref[8 + start : 8 + start + block, :]
        keyt = key.T
        equal = jnp.concatenate([key] * (block // LANES), axis=1) == keyt[0:1, :]
        same, strict = equal & (row_i >= col_i), row_i > col_i
        cum = cum_ref[at, :]
        cumt = cum.T
        raw = raw_ref[at, :]
        dt = softplus(raw)
        dtt = dt.T
        inflow, tail, passing = block_parts(cum, key, key_ref[7 + start : 8 + start, :])
        x, b, c = act_ref[at, :inner], act_ref[at, inner : inner + state], act_ref[at, inner + state :]
        x_wide = x.astype(f32)
        dy = dmix_ref[at, :]
        dy_low = dy.astype(low)
        full, grad = states_ref[index], cot[...]
        full_low, grad_low = full.astype(low), grad.astype(low)
        scores = dot_nt(c, b)
        from_state = dot_nt(c, full_low)
        from_grad = dot_nt(b, grad_low)
        tail_wide = spread_heads(tail, head_size, inner)
        dt_wide = spread_heads(dt, head_size, inner)
        d_in = (dy * spread_heads(inflow, head_size, inner)).astype(low)
        pushed = (x_wide * tail_wide * dt_wide).astype(low)
        d_scores = [jnp.zeros((stop - top, stop), f32) for top, stop in halves(block)]
        dxd, col_sums = [], []
        change = [jnp.zeros((stop - top, LANES), f32) for top, stop in halves(block)]
        for head in range(heads):
            cols = slice(head * head_size, (head + 1) * head_size)
            d_head = jnp.zeros((block, head_size), f32)
            col_sum = jnp.zeros((1, block), f32)
            for index_half, (top, stop) in enumerate(halves(block)):
                decay = head_decay(same[top:stop, :stop], cum[top:stop, :], cumt[:, :stop], head)
                dy_head = dy_low[top:stop, cols]
                flow = (
                    dot_nt(dy_head, x[:stop, cols]) * dtt[head : head + 1, :stop] * decay
                )
                d_scores[index_half] = d_scores[index_half] + flow
                joint = jnp.where(
                    strict[top:stop, :stop], flow * scores[top:stop, :stop], 0.0
                )
                change[index_half] = jnp.where(
                    lane[top:stop, :] == head,
                    jnp.sum(joint, axis=1, keepdims=True),
                    change[index_half],
                )
                mixing = (scores[top:stop, :stop] * decay).astype(low)
                col_piece = jnp.sum(joint, axis=0, keepdims=True)
                d_piece = dot_tn(mixing, dy_head)
                if stop < block:
                    col_piece = jnp.concatenate(
                        [col_piece, jnp.zeros((1, block - stop), f32)], axis=1
                    )
                    d_piece = jnp.concatenate(
                        [d_piece, jnp.zeros((block - stop, head_size), f32)], axis=0
                    )
                col_sum = col_sum + col_piece
                d_head = d_head + d_piece
            col_sums.append(col_sum)
            dxd.append(d_head)
        change = jnp.concatenate(change, axis=0)
        d_scores = jnp.concatenate(
            [
                jnp.concatenate([one, jnp.zeros((one.shape[0], block - one.shape[1]), f32)], axis=1)
                if one.shape[1] < block
                else one
                for one in d_scores
            ],
            axis=0,
        )
        dxd = jnp.concatenate(dxd, axis=1) + from_grad * tail_wide
        dx[at, :] = dxd * dt_wide + dy * skip
        d_low = d_scores.astype(low)
        dbc[at, state:] = (dot_wide(d_low, b) + dot_wide(d_in, full_low)).astype(low)
        dbc[at, :state] = (dot_tn(d_low, c) + dot_wide(pushed, grad_low)).astype(low)
        through = sum_heads(dy * from_state, head_size) * inflow
        kept = sum_heads(x_wide * from_grad, head_size) * (tail * dt)
        columns = jnp.concatenate(
            col_sums + [jnp.zeros((LANES - heads, block), f32)], axis=0
        ).T
        product = full * grad
        whole = jnp.concatenate(
            [
                jnp.sum(product[h * head_size : (h + 1) * head_size, :], axis=0, keepdims=True)
                for h in range(heads)
            ]
            + [jnp.zeros((LANES - heads, state), f32)],
            axis=0,
        )
        whole = jnp.sum(whole.T, axis=0, keepdims=True)
        d_la = running_sum(change - columns + through - kept, True) + (
            jnp.sum(kept, axis=0, keepdims=True) + passing * whole
        )
        d_log = d_log + jnp.sum(d_la * (dt * rate), axis=0, keepdims=True)
        d_raw = (d_la * rate + sum_heads(dxd * x_wide, head_size)) * jax.nn.sigmoid(raw)
        d_raw = jnp.where(lane < heads, d_raw, 0.0)
        d_bias = d_bias + jnp.sum(d_raw, axis=0, keepdims=True)
        draw[at, :] = d_raw.astype(low)
        cot[...] = grad * rows_of_heads(passing, heads, head_size) + dot_tn(d_in, c)
        if index == max(steps - 2, 0):
            scatter_br.middle()
        if index == max(steps - 3, 0):
            scatter_gb.middle()
    scatter_bc.start()

    def conv_back(cols, get):
        size = cols.stop - cols.start
        dz[0:8, cols] = jnp.zeros((8, size), f32)
        dz[8 + tokens :, cols] = jnp.zeros((8, size), f32)
        tap_sums = [jnp.zeros((1, size), f32) for _ in range(kernel + 1)]
        for index in range(steps):
            start = index * block
            key = key_ref[8 + start : 8 + start + block, :]
            total = jnp.broadcast_to(cw[kernel : kernel + 1, cols], (block, size))
            taps = []
            for offset in range(kernel):
                at = slice(8 - kernel + 1 + offset + start, 8 - kernel + 1 + offset + start + block)
                tap = pre_ref[at, cols]
                if offset < kernel - 1:
                    same = jnp.where(key_ref[at, :] == key, 1.0, 0.0)
                    tap = tap * jnp.concatenate([same] * (size // LANES), axis=1)
                taps.append(tap)
                total = total + cw[offset : offset + 1, cols] * tap
            sigm = jax.nn.sigmoid(total)
            change = get(index) * (sigm * (1.0 + total * (1.0 - sigm)))
            dz[8 + start : 8 + start + block, cols] = change
            for offset in range(kernel):
                tap_sums[offset] += jnp.sum(taps[offset] * change, axis=0, keepdims=True)
            tap_sums[kernel] += jnp.sum(change, axis=0, keepdims=True)
        for offset in range(kernel + 1):
            small[offset : offset + 1, cols] = tap_sums[offset]

    def back_rows(start, size, cols):
        span = cols.stop - cols.start
        key = key_ref[start : start + size, :]
        total = cw[kernel - 1 : kernel, cols] * dz[start : start + size, cols]
        for offset in range(kernel - 1):
            at = slice(start + kernel - 1 - offset, start + kernel - 1 - offset + size)
            same = jnp.where(key_ref[at, :] == key, 1.0, 0.0)
            total = total + cw[offset : offset + 1, cols] * (
                dz[at, cols] * jnp.concatenate([same] * (span // LANES), axis=1)
            )
        return total

    def halo(cols, out, arrived, slot):
        out[...] = back_rows(0, 8, cols)
        copy = remote(out, arrived, hs.at[slot], hr.at[slot], "dp", following)
        copy.start()
        return copy

    def finish_pre(cols, copy, arrived):
        for index in range(steps):
            start = index * block
            value = back_rows(8 + start, block, cols)
            if index == steps - 1:
                copy.wait()
                edge = value[block - 8 :, :] + arrived[...]
                value = jnp.concatenate([value[: block - 8], edge], axis=0)
            dpre[start : start + block, cols] = value.astype(low)

    cols = slice(0, inner)
    conv_back(cols, lambda index: dx[index * block : (index + 1) * block, :])
    copy = halo(cols, halo_out, halo_in, 0)
    scatter_bc.middle()
    finish_pre(cols, copy, halo_in)
    for index in range(steps):
        at = slice(index * block, (index + 1) * block)
        part_sum = dot_nt(dgate_ref[at, :], wb_ref[:, :inner])
        part_sum = part_sum + dot_nt(dpre[at, :inner], wa_ref[:, :inner])
        part_sum = part_sum + dot_nt(draw[at, :], wdt_ref[...])
        rows_part[at, :] = part_sum.astype(low)
    scatter_rows.start()
    dbc_all[own, :] = scatter_bc.finish().astype(low)
    gather_bc = Gather(model, dbc_all, rows, as_, ar_)
    gather_bc.start()
    ga_part[...] = dot_tn(normed_ref[...], dpre[:, :inner]).astype(low)
    scatter_ga.start()
    scatter_rows.middle()
    gather_bc.step()
    gather_bc.finish()
    cols = slice(inner, wide)
    conv_back(cols, lambda index: dbc_all[index * block : (index + 1) * block, :].astype(f32))
    copy = halo(cols, halo_bc_out, halo_bc_in, 1)
    scatter_ga.middle()
    finish_pre(cols, copy, halo_bc_in)

    def pick_exact(value, one):
        return dot_wide(
            jnp.concatenate(split(value, 3), axis=1), jnp.concatenate([one] * 3, axis=0)
        )

    def picker(count, first, lane_at, many):
        down = lax.broadcasted_iota(jnp.int32, (count, LANES), 0)
        over = lax.broadcasted_iota(jnp.int32, (count, LANES), 1) - lane_at
        return ((down == over + first) & (over >= 0) & (over < many)).astype(f32).astype(low)

    side = (
        dot_wide(dpre[:, inner:], picker(bc, model.me * quarter, bc_lane, quarter))
        + dot_wide(draw[...], picker(LANES, 0, dt_lane, heads))
    ).astype(low)
    gs_part[...] = dot_tn(normed_ref[...], side).astype(low)
    scatter_gs.start()
    d_rows = dot_nt(dpre[own, inner:], wa_ref[:, inner:wide])
    scatter_gs.middle()
    d_rows = d_rows + scatter_rows.finish()
    x = x_ref[...]
    rstd = lax.rsqrt(jnp.sum(x * x, axis=-1, keepdims=True) / mean_of + EPSILON)
    scaled = gain_ref[...][None, :] * d_rows
    small[kernel + 1 : kernel + 2, :width] = jnp.sum(d_rows * x * rstd, axis=0, keepdims=True)
    small[kernel + 2 : kernel + 3, :inner] = gsum_ref[0:1, :]
    d_heads = jnp.concatenate(
        [d_bias, d_log, sum_heads(gsum_ref[...], head_size, 3)[1:2, :], jnp.zeros((5, LANES), f32)],
        axis=0,
    )
    d_heads = pick_exact(d_heads, picker(LANES, 0, model.me * heads, heads))
    for index in range(3):
        small[kernel + 3 : kernel + 4, index * LANES : (index + 1) * LANES] = d_heads[
            index : index + 1, :
        ]

    def small_copy(hop):
        return remote(
            small, small_all.at[hop], ss.at[hop], sr.at[hop], "dp", lax.rem(data.me + hop, dp)
        )

    for hop in range(1, dp):
        small_copy(hop).start()
    packed[rows : 2 * rows, :width] = (
        cot_ref[...]
        + rstd * scaled
        - x * (rstd * rstd * rstd * (jnp.sum(scaled * x, axis=-1, keepdims=True) / mean_of))
    )
    packed[0:rows, :width] = x + scatter_br.finish()
    base = 2 * rows
    packed[base : base + part, : 2 * inner] = scatter_gb.finish()
    packed[base + part : base + 2 * part, :inner] = scatter_ga.finish()
    total = small[...]
    for hop in range(1, dp):
        small_copy(hop).wait_recv()
        total = total + small_all[hop]
    sums_own[...] = total

    def sums_copy(hop):
        return remote(
            sums_own, sums_ref.at[model.me], ts.at[hop], tr.at[hop], "tensor",
            lax.rem(model.me + hop, tensor),
        )

    for hop in range(1, tensor):
        sums_copy(hop).start()
    sums_ref[model.me] = total
    side_sum = scatter_gs.finish()
    packed[base + part : base + 2 * part, inner : inner + LANES] = pick_exact(
        side_sum, picker(LANES, dt_lane, 0, heads)
    )
    bc_own[...] = side_sum

    def bc_copy(hop):
        return remote(
            bc_own, gbc_ref.at[model.me], us.at[hop], ur.at[hop], "tensor",
            lax.rem(model.me + hop, tensor),
        )

    for hop in range(1, tensor):
        bc_copy(hop).start()
    gbc_ref[model.me] = side_sum
    for hop in range(1, tensor):
        sums_copy(hop).wait()
        bc_copy(hop).wait()
    for hop in range(1, dp):
        small_copy(hop).wait_send()
    for one in (scatter_bc, scatter_rows, scatter_ga, scatter_gs, scatter_br, scatter_gb, gather_bc):
        one.drain()
    for index in range(tensor):
        at = base + 2 * part + index * part
        packed[at : at + part, :LANES] = gbc_ref[index]
        at = base + (2 + tensor) * part + index * 8
        packed[at : at + 8, :] = sums_ref[index]


def block_kernel(dp, tensor, group, heads, kernel, mean_of, sequences, counts, *refs):
    sizes, parts, start = counts, [], 0
    for size in sizes:
        parts.append(refs[start : start + size])
        start += size
    ins, (packed,), kept, fscratch, bscratch = parts
    (
        x_ref, gain_ref, cot_ref, zx_ref, bcw_ref, dtt_ref, out_ref, seg_ref, cxw_ref, cxb_ref,
        cbw_ref, cbb_ref, bias_ref, log_ref, skip_ref, ggain_ref,
    ) = ins
    head_ref = fscratch[0]
    total = bias_ref.shape[0]
    rows = jnp.concatenate(
        [bias_ref[...][None, :], -jnp.exp(log_ref[...][None, :]), skip_ref[...][None, :],
         jnp.zeros((5, total), jnp.float32)],
        axis=0,
    )
    down = lax.broadcasted_iota(jnp.int32, (total, LANES), 0)
    over = lax.broadcasted_iota(jnp.int32, (total, LANES), 1)
    one = ((down == over + lax.axis_index("tensor") * heads) & (over < heads)).astype(
        jnp.float32
    ).astype(low)
    hi, mid, lo = split(rows, 3)
    head_ref[...] = dot_wide(hi, one) + dot_wide(mid, one) + dot_wide(lo, one)
    forward_part(
        dp, tensor, group, heads, mean_of, sequences,
        x_ref, gain_ref, cot_ref, zx_ref, bcw_ref, dtt_ref, out_ref, seg_ref, cxw_ref, cxb_ref,
        cbw_ref, cbb_ref, head_ref, ggain_ref, *kept, *fscratch[1:],
    )
    cw = fscratch[3]
    backward_part(
        dp, tensor, group, heads, kernel, mean_of, *kept, x_ref, gain_ref, cot_ref, cw, head_ref,
        packed, *bscratch,
    )


def finish_kernel(
    tensor, heads, kernel,
    packed,
    o_res, o_gin, o_norm, o_zx, o_bc, o_dt, o_cxw, o_cxb, o_cbw, o_cbb, o_dtb, o_log, o_skip,
    o_gate, o_out,
):
    part, inner = o_zx.shape[1:]
    rows, width = o_gin.shape
    base = 2 * rows
    bc = o_bc.shape[1]
    quarter = bc // tensor
    o_res[...] = packed[0:rows, :width]
    o_gin[...] = packed[rows : 2 * rows, :width]
    o_zx[0] = packed[base : base + part, :inner]
    o_zx[1] = packed[base + part : base + 2 * part, :inner]
    o_out[...] = packed[base : base + part, inner : 2 * inner]
    turned = jnp.concatenate(
        [
            packed[base + part : base + 2 * part, inner : inner + LANES],
            jnp.zeros((-part % LANES, LANES), jnp.float32),
        ],
        axis=0,
    ).T
    o_dt[...] = turned[: o_dt.shape[0], :part]
    base = base + 2 * part
    lane = lax.broadcasted_iota(jnp.int32, (part, LANES), 1)
    for start in range(0, bc, LANES):
        tile = jnp.zeros((part, LANES), jnp.float32)
        for one in range(tensor):
            if start <= one * quarter < start + LANES:
                at = one * quarter - start
                tile = jnp.where((lane >= at) & (lane < at + quarter), packed[base + one * part : base + (one + 1) * part, :LANES], tile)
        o_bc[:, start : start + LANES] = tile
    base = base + tensor * part
    sums = [packed[base + 8 * one : base + 8 * (one + 1), :] for one in range(tensor)]
    total = sums[0]
    for one in range(1, tensor):
        total = total + sums[one]
    o_norm[...] = total[kernel + 1, :width]
    o_cbw[...] = sums[0][0:kernel, inner : inner + bc]
    o_cbb[...] = sums[0][kernel, inner : inner + bc]
    for one in range(tensor):
        cols = slice(one * inner, (one + 1) * inner)
        o_cxw[:, cols] = sums[one][0:kernel, :inner]
        o_cxb[cols] = sums[one][kernel, :inner]
        o_gate[cols] = sums[one][kernel + 2, :inner]
    for index, out in enumerate((o_dtb, o_log, o_skip)):
        out[...] = total[kernel + 3, index * LANES : index * LANES + out.shape[0]]


def block_call(dp, tensor, group, heads, mean_of, sequences, *arrays):
    x, zx, bcw, cxw = arrays[0], arrays[3], arrays[4], arrays[8]
    rows, width = x.shape
    tokens, part, inner = rows * tensor, zx.shape[1], zx.shape[2]
    bc = bcw.shape[1]
    wide, state = inner + bc, bc // 2
    steps = tokens // min(GROUP, tokens)
    small = (8, -(-max(width, wide, 2 * inner, 3 * LANES) // LANES) * LANES)
    f32 = jnp.float32
    dma = pltpu.SemaphoreType.DMA
    kept = [
        pltpu.VMEM((tokens, width), low),
        pltpu.VMEM((tokens, width), low),
        pltpu.VMEM((dp * part, wide), low),
        pltpu.VMEM((dp * part, 2 * inner), low),
        pltpu.VMEM((dp * part, LANES), low),
        pltpu.VMEM((tokens + 8, wide), f32),
        pltpu.VMEM((tokens + 16, LANES), f32),
        pltpu.VMEM((tokens, wide), low),
        pltpu.VMEM((tokens, LANES), f32),
        pltpu.VMEM((tokens, LANES), f32),
        pltpu.VMEM((steps, inner, state), f32),
        pltpu.VMEM((tokens, inner), f32),
        pltpu.VMEM((tokens, inner), low),
        pltpu.VMEM((tokens, inner), low),
        pltpu.VMEM((inner + 16, state), low),
        pltpu.VMEM((8, inner), f32),
    ]
    forward_scratch = [
        pltpu.VMEM((8, LANES), f32),
        pltpu.VMEM((8, wide), f32),
        pltpu.VMEM((dp * 16, LANES), low),
        pltpu.VMEM((8, wide), f32),
        pltpu.VMEM((tokens, inner), f32),
        pltpu.VMEM((tokens, inner), f32),
        pltpu.VMEM((tokens, inner), f32),
        pltpu.VMEM((inner + 16, state), low),
        pltpu.VMEM((group, inner + 16, state), low),
        pltpu.VMEM((inner, state), f32),
        pltpu.VMEM((8 * steps, LANES), f32),
        pltpu.VMEM((8, tokens), f32),
        pltpu.VMEM((tensor, 8, tokens), f32),
        *[dma((2 * n,)) for n in (dp, dp, dp, dp, dp, dp, tensor, tensor, tensor, tensor)],
        dma((2,)), dma((2,)),
        dma((group,)), dma((group,)),
        dma((tensor,)), dma((tensor,)),
    ]
    backward_scratch = [
        pltpu.VMEM((tokens, inner), f32),
        pltpu.VMEM((tokens, bc), low),
        pltpu.VMEM((tokens, LANES), low),
        pltpu.VMEM((tokens + 16, wide), f32),
        pltpu.VMEM((tokens, wide), low),
        pltpu.VMEM((tokens, bc), low),
        pltpu.VMEM((tokens, width), low),
        pltpu.VMEM((dp * part, 2 * inner), low),
        pltpu.VMEM((tokens, width), low),
        pltpu.VMEM((dp * part, inner), low),
        pltpu.VMEM((dp * part, LANES), low),
        pltpu.VMEM((8, inner), f32),
        pltpu.VMEM((8, inner), f32),
        pltpu.VMEM((8, bc), f32),
        pltpu.VMEM((8, bc), f32),
        pltpu.VMEM((inner, state), f32),
        pltpu.VMEM((group, inner + 16, state), low),
        pltpu.VMEM(small, f32),
        pltpu.VMEM((dp,) + small, f32),
        pltpu.VMEM(small, f32),
        pltpu.VMEM((part, LANES), f32),
        pltpu.VMEM((tensor, part, LANES), f32),
        pltpu.VMEM((tensor,) + small, f32),
        *Scatter.scratch(tensor, rows, bc),
        *Scatter.scratch(tensor, rows, width),
        *Scatter.scratch(tensor, rows, width),
        *Scatter.scratch(dp, part, inner),
        *Scatter.scratch(dp, part, 2 * inner),
        *Scatter.scratch(dp, part, LANES),
        dma((2 * tensor,)), dma((2 * tensor,)),
        dma((2,)), dma((2,)),
        dma((dp,)), dma((dp,)),
        dma((tensor,)), dma((tensor,)),
        dma((tensor,)), dma((tensor,)),
        dma((group,)), dma((group,)),
    ]
    counts = (len(arrays), 1, len(kept), len(forward_scratch), len(backward_scratch))
    lines = 2 * rows + (2 + tensor) * part + 8 * tensor
    return pl.pallas_call(
        functools.partial(
            block_kernel, dp, tensor, group, heads, cxw.shape[0], mean_of, sequences, counts
        ),
        out_shape=jax.ShapeDtypeStruct((lines, small[1]), f32),
        in_specs=vmem(len(arrays)),
        out_specs=vmem(1)[0],
        scratch_shapes=kept + forward_scratch + backward_scratch,
        compiler_params=pltpu.CompilerParams(
            collective_id=0, has_side_effects=True, vmem_limit_bytes=63 * 2**20
        ),
        name="block",
    )(*arrays)


def finish_call(tensor, heads, kernel, rows, width, part, inner, heads_total, bc, packed):
    inner_total = inner * tensor
    outs = (
        (rows, width), (rows, width), (width,), (2, part, inner), (part, bc), (heads, part),
        (kernel, inner_total), (inner_total,), (kernel, bc), (bc,), (heads_total,),
        (heads_total,), (heads_total,), (inner_total,), (part, inner),
    )
    return pl.pallas_call(
        functools.partial(finish_kernel, tensor, heads, kernel),
        out_shape=tuple(jax.ShapeDtypeStruct(one, jnp.float32) for one in outs),
        in_specs=vmem(1),
        out_specs=tuple(vmem(len(outs))),
        compiler_params=pltpu.CompilerParams(vmem_limit_bytes=32 * 2**20),
        name="finish",
    )(packed)


def pad_to(array, size, axis):
    widths = [(0, 0)] * array.ndim
    widths[axis] = (0, size - array.shape[axis])
    return jnp.pad(array, widths)


def per_device(
    block_input,
    norm_gain,
    zx_weight,
    bc_weight,
    dt_weight,
    conv_x_weight,
    conv_x_bias,
    conv_bc_weight,
    conv_bc_bias,
    dt_bias,
    decay_log,
    skip_gain,
    gate_gain,
    out_weight,
    segments,
    cotangent,
):
    tensor_count = lax.axis_size("tensor")
    data_count = lax.axis_size("dp")
    token_count = segments.shape[0]
    row_count, width = block_input.shape
    part = zx_weight.shape[1]
    heads_here = dt_weight.shape[1]
    heads_total = dt_bias.shape[0]
    taps = conv_x_weight.shape[0]
    bc_size = bc_weight.shape[1]
    padded = -(-part // 16) * 16
    columns = data_count * padded

    def widen(array):
        if padded == part:
            return array
        lead = array.shape[:-1]
        return pad_to(array.reshape(lead + (data_count, part)), padded, -1).reshape(lead + (columns,))

    def narrow(array):
        if padded == part:
            return array
        lead = array.shape[:-1]
        return array.reshape(lead + (data_count, padded))[..., :part].reshape(lead + (width,))

    group = max(1, LENGTH // token_count)
    if data_count % group:
        group = data_count
    sequences = data_count * token_count // LENGTH + 1
    packed = block_call(
        data_count, tensor_count, group, heads_here, width, sequences,
        widen(block_input), widen(norm_gain), widen(cotangent), pad_to(zx_weight, padded, 1),
        pad_to(bc_weight, padded, 0), dt_weight.T, pad_to(out_weight.T, padded, 0), segments,
        conv_x_weight, conv_x_bias, conv_bc_weight, conv_bc_bias, dt_bias, decay_log, skip_gain,
        gate_gain,
    )
    outs = list(
        finish_call(
            tensor_count, heads_here, taps, row_count, columns, padded, zx_weight.shape[2],
            heads_total, bc_size, packed,
        )
    )
    for index in (0, 1, 2):
        outs[index] = narrow(outs[index])
    if padded != part:
        outs[3] = outs[3][:, :part]
        outs[4], outs[5], outs[14] = outs[4][:part], outs[5][:, :part], outs[14][:part]
    outs[5], outs[14] = outs[5].T, outs[14].T
    return tuple(outs)


def solution(mesh):
    in_specs = (
        P(("dp", "tensor"), None),
        P(),
        P(None, "dp", "tensor"),
        P("dp", None),
        P("dp", "tensor"),
        P(),
        P(),
        P(),
        P(),
        P(),
        P(),
        P(),
        P(),
        P("tensor", "dp"),
        P("dp"),
        P(("dp", "tensor"), None),
    )
    out_specs = (
        P(("dp", "tensor"), None),
        P(("dp", "tensor"), None),
        P(),
        P(None, "dp", "tensor"),
        P("dp", None),
        P("dp", "tensor"),
        P(),
        P(),
        P(),
        P(),
        P(),
        P(),
        P(),
        P(),
        P("tensor", "dp"),
    )
    return jax.shard_map(
        per_device, mesh=mesh, in_specs=in_specs, out_specs=out_specs, check_vma=False
    )
```
